32 devices in a mesh: section: 2 (over y), dp: 16 (over z, x, core).
Axes of the slice: x: 2, y: 2, z: 4, core: 2. Of those that a mesh axis runs over, the one named last changes fastest.
Arguments:
- tokens: bfloat16 [2, 4096, 768], P(None, 'dp'), may hold values from -6 to 6
- lengths: int32 [2, 16], replicated, may hold values from 200 to 256
- w_qkv: float32 [2, 768, 2304], P('section', 'dp'), may hold values from -0.21875 to 0.21875
- w_out: float32 [2, 768, 768], P('section', 'dp'), may hold values from -0.625 to 0.625
- w_gate_up: float32 [2, 768, 6144], P('section', 'dp'), may hold values from -0.21875 to 0.21875
- w_down: float32 [2, 3072, 768], P('section', 'dp'), may hold values from -0.109375 to 0.109375
- norm_gain: float32 [2, 2, 768], P('section', None, 'dp'), may hold values from 0.25 to 1.75
- norm_bias: float32 [2, 2, 768], P('section', None, 'dp'), may hold values from -3 to 3
- cotangent: bfloat16 [2, 4096, 768], P(None, 'dp'), may hold values from -6 to 6
Outputs:
- layer_outputs: bfloat16 [2, 2, 4096, 768], P('section', None, 'dp')
- input_grads: float32 [2, 2, 4096, 768], P('section', None, 'dp')
- grad_w_qkv: float32 [2, 768, 2304], P('section', 'dp')
- grad_w_out: float32 [2, 768, 768], P('section', 'dp')
- grad_w_gate_up: float32 [2, 768, 6144], P('section', 'dp')
- grad_w_down: float32 [2, 3072, 768], P('section', 'dp')
- grad_norm_gain: float32 [2, 2, 768], P('section', None, 'dp')
- grad_norm_bias: float32 [2, 2, 768], P('section', None, 'dp')
The draws below stay inside these ranges and needn't reach their ends.
Inputs may be any that keep to these rules, and one draw needn't show every extreme that they name: `lengths`: positions of a window from its length on are padding.
All inputs are finite; a program needn't handle non-finite values.
Results may differ from the reference program's by a relative error of at most 0.024.
The reference program's roundings to bfloat16 on the way count: a program that leaves them out, or rounds other values in their place, can miss the bound.
Values may be sent and summed in bfloat16 or wider, within the bound.
No kernel may reach another device: no remote copies, remote signals or barrier semaphores. Data moves between devices by JAX's collectives and lax.ppermute only.
A program may use at most 256 MiB of HBM per device.

```python
from functools import partial
import jax
import jax.numpy as jnp
from jax import lax

D = 768
HEADS = 12
HEAD = 64
FF = 3072
SEQ = 256
MB = 2
WINDOWS = 16
ROWS = 4096


def with_ends(drawn, stream_key, least, largest):
    index_at = [jax.random.randint(jax.random.fold_in(stream_key, axis), (), 0, length) for axis, length in enumerate(drawn.shape)]
    main_axis = drawn.shape.index(max(drawn.shape))
    next_to = index_at[:main_axis] + [(index_at[main_axis] + 1) % drawn.shape[main_axis]] + index_at[main_axis + 1:]
    return drawn.at[tuple(index_at)].set(least).at[tuple(next_to)].set(largest)


def raised(entries, stream_key, source, target, parts, factor):
    owner, partner = [(jnp.arange(entries.shape[position]) // (entries.shape[position] // parts)).reshape([-1 if axis == position else 1 for axis in range(entries.ndim)]) for position in (source, target)]
    chosen = jax.random.permutation(stream_key, parts)[partner]
    strong = (owner == chosen) | (owner == (partner + parts // 2) % parts)
    return jnp.where(strong, factor * entries, entries)


def steps_of(stream_key, shape, cuts, low, largest):
    factor_of = 1.0
    for position, blocks in cuts:
        steps = jax.random.uniform(jax.random.fold_in(jax.random.fold_in(stream_key, 6), position), (blocks,), jnp.float32, low / len(cuts), largest / len(cuts))
        factor_of = factor_of * jnp.repeat(jnp.exp(steps), shape[position] // blocks).reshape((-1,) + (1,) * (len(shape) - 1 - position))
    return factor_of


def noise(rng, extent, spread, most, cuts=(), held_as=jnp.bfloat16):
    factor_of = steps_of(rng, extent, cuts, -0.22, 0.18) if cuts else 1.0
    result = jax.random.normal(rng, extent, jnp.float32) * spread * factor_of
    return jnp.minimum(jnp.maximum(result, -most), most).astype(held_as)


def bell_draw_with(key, extent, spread, limit, cuts, heavy, held_as=jnp.bfloat16):
    entries = spread * jax.random.normal(key, extent, jnp.float32)
    if cuts:
        entries = entries * steps_of(key, extent, cuts, -0.22, 0.18)
    return jnp.clip(raised(entries, jax.random.fold_in(key, 3), *heavy), -limit, limit).astype(held_as)


def setup_inputs(seed: int = 0) -> dict:
    seeds = jax.random.split(jax.random.key(seed), 10)
    return {
        "tokens": bell_draw_with(seeds[0], (MB, ROWS, D), 1.0, 6.0, ((1, 16),), (1, 2, 16, 2.0)),
        "lengths": with_ends(jax.random.randint(seeds[1], (MB, WINDOWS), SEQ * 25 // 32, SEQ + 1), jax.random.fold_in(seeds[1], 1), SEQ * 25 // 32, SEQ).astype(jnp.int32),
        "w_qkv": noise(seeds[2], (2, D, 3 * D), D ** -0.5, 0.21875, ((0, 2), (1, 16)), jnp.float32),
        "w_out": noise(seeds[3], (2, D, D), (D // 8) ** -0.5, 0.625, ((0, 2), (1, 16)), jnp.float32),
        "w_gate_up": noise(seeds[4], (2, D, 2 * FF), D ** -0.5, 0.21875, ((0, 2), (1, 16)), jnp.float32),
        "w_down": noise(seeds[5], (2, FF, D), FF ** -0.5, 0.109375, ((0, 2), (1, 16)), jnp.float32),
        "norm_gain": jnp.clip(1.0 + 0.15 * jax.random.normal(seeds[6], (2, 2, D), jnp.float32), 0.25, 1.75),
        "norm_bias": noise(seeds[7], (2, 2, D), 0.3, 3.0, ((0, 2), (2, 16)), jnp.float32),
        "cotangent": noise(seeds[8], (MB, ROWS, D), 1.0, 6.0, ((1, 16),)),
    }


@jax.custom_vjp
def low(v):
    return lax.optimization_barrier(v.astype(jnp.bfloat16)).astype(jnp.float32)

@jax.custom_vjp
def low_back(v):
    return v

def low_keep(v):
    return (low(v), None)

def low_pass(kept, grad):
    return (grad,)

def back_keep(v):
    return (v, None)

def back_low(kept, grad):
    return (low(grad),)
low.defvjp(low_keep, low_pass)
low_back.defvjp(back_keep, back_low)
HIGHEST = lax.Precision.HIGHEST
EPSILON = 1e-05
NEGATIVE = -1e+30

def norm_rows(values, gain_row, bias_row):
    center = values - lax.optimization_barrier(jnp.mean(values, axis=-1, keepdims=True))
    variance = lax.optimization_barrier(jnp.mean(center * center, axis=-1, keepdims=True))
    return center * lax.rsqrt(variance + EPSILON) * gain_row + bias_row

def encoder_layer(inputs, lengths, w_qkv, w_out, w_gate_up, w_down, norm_gains, norm_biases):
    windows_here = inputs.shape[0]
    projected = low(low_back(jnp.einsum('wsd,de->wse', inputs, low(w_qkv), precision=HIGHEST)))
    queries = projected[..., :D].reshape(windows_here, SEQ, HEADS, HEAD)
    keys_all = projected[..., D:2 * D].reshape(windows_here, SEQ, HEADS, HEAD)
    values_all = projected[..., 2 * D:].reshape(windows_here, SEQ, HEADS, HEAD)
    slopes = jnp.exp2(-8.0 * (jnp.arange(HEADS).astype(jnp.float32) + 1.0) / HEADS)
    places = jnp.arange(SEQ).astype(jnp.int32)
    distance = jnp.abs(places[:, None] - places[None, :]).astype(jnp.float32)
    raw_scores = HEAD ** (-0.5) * jnp.einsum('wqhd,wkhd->whqk', queries, keys_all, precision=HIGHEST)
    raw_scores = raw_scores - slopes[None, :, None, None] * distance[None, None]
    key_valid = places[None, :] < lengths[:, None].astype(jnp.int32)
    scores = jnp.where(key_valid[:, None, None, :], low_back(raw_scores), NEGATIVE)
    row_peak = lax.optimization_barrier(jnp.max(scores, axis=-1, keepdims=True))
    row_exp = jnp.exp(scores - row_peak)
    attn_probs = row_exp / lax.optimization_barrier(jnp.sum(row_exp, axis=-1, keepdims=True))
    context = jnp.einsum('whqk,wkhd->wqhd', low(attn_probs), values_all, precision=HIGHEST)
    context = low(low_back(context.reshape(windows_here, SEQ, D)))
    attended = low_back(jnp.einsum('wsd,de->wse', context, low(w_out), precision=HIGHEST))
    first_norm = norm_rows(inputs + attended, low(norm_gains[0]), low(norm_biases[0]))
    gate_up = low_back(jnp.einsum('wsd,de->wse', low(first_norm), low(w_gate_up), precision=HIGHEST))
    gated_rows = low(jax.nn.gelu(gate_up[..., :FF], approximate=False) * gate_up[..., FF:])
    down_rows = low_back(jnp.einsum('wsf,fd->wsd', gated_rows, low(w_down), precision=HIGHEST))
    return norm_rows(first_norm + down_rows, low(norm_gains[1]), low(norm_biases[1]))

def both_layers(inputs, weights, probe_zero, lengths):
    w_qkv, w_out, w_gate_up, w_down, norm_gain, norm_bias = weights
    first_out = encoder_layer(inputs, lengths, w_qkv[0], w_out[0], w_gate_up[0], w_down[0], norm_gain[0], norm_bias[0])
    sent_rows = low(first_out)
    second_out = encoder_layer(low_back(sent_rows) + probe_zero, lengths, w_qkv[1], w_out[1], w_gate_up[1], w_down[1], norm_gain[1], norm_bias[1])
    return (second_out, sent_rows)

def reference(tokens, lengths, w_qkv, w_out, w_gate_up, w_down, norm_gain, norm_bias, cotangent):
    groups = MB * WINDOWS // 8
    token_groups = tokens.astype(jnp.float32).reshape(groups, 8, SEQ, D)
    cot_groups = cotangent.astype(jnp.float32).reshape(groups, 8, SEQ, D)
    length_groups = lengths.reshape(groups, 8)
    weights = (w_qkv, w_out, w_gate_up, w_down, norm_gain, norm_bias)

    def group_step(summed, batch_items):
        inputs, upstream, group_lengths = batch_items
        probe_zero = jnp.zeros_like(inputs)
        second_out, backward_fn, sent_rows = jax.vjp(partial(both_layers, lengths=group_lengths), inputs, weights, probe_zero, has_aux=True)
        input_grad, weight_grads, probe_grad = backward_fn(upstream)
        summed = jax.tree.map(jnp.add, summed, weight_grads)
        return (summed, (sent_rows, second_out, input_grad, probe_grad))
    initial = jax.tree.map(jnp.zeros_like, weights)
    summed, (sent_rows, second_out, input_grad, probe_grad) = lax.scan(group_step, initial, (token_groups, cot_groups, length_groups))
    full_shape = (MB, ROWS, D)
    layer_outputs = jnp.stack([sent_rows.reshape(full_shape), second_out.reshape(full_shape)]).astype(jnp.bfloat16)
    input_grads = jnp.stack([input_grad.reshape(full_shape), probe_grad.reshape(full_shape)])
    return (layer_outputs, input_grads, summed[0], summed[1], summed[2], summed[3], summed[4], summed[5])
```

```python
import functools

import jax
import jax.numpy as jnp
from jax import lax
from jax.experimental import pallas as pl
from jax.experimental.pallas import tpu as pltpu
from jax.sharding import PartitionSpec as P

D = 768
HEADS = 12
HEAD = 64
FF = 3072
SEQ = 256
MICRO = 2
EPSILON = 1e-05
FAR = 1e30
INV_SQRT_2PI = 0.3989422804014327
ROOT_HALF = 2.0 ** (-0.5)

COL_OUT = 3 * D
COL_GU = 4 * D
COL_DOWN = COL_GU + 2 * FF
COL_NORM = COL_DOWN + FF
WIDE = COL_NORM + 128

CHUNK = 1024
CHUNKS = FF // CHUNK
BF = jnp.bfloat16
F32 = jnp.float32
NN = (((1,), (0,)), ((), ()))
NT = (((1,), (1,)), ((), ()))
TN = (((0,), (0,)), ((), ()))
SLOPES = [2.0 ** (-8.0 * (h + 1) / HEADS) for h in range(HEADS)]

ANY = pl.BlockSpec(memory_space=pl.ANY)
SMEM = pl.BlockSpec(memory_space=pltpu.SMEM)


def matmul(left, right, dims=NN):
    return lax.dot_general(left, right, dims, preferred_element_type=F32)


def begin(source, target, semaphore):
    copy = pltpu.make_async_copy(source, target, semaphore)
    copy.start()
    return copy


def row_mean(values):
    return jnp.mean(values, axis=-1, keepdims=True)


def norm_forward(values, gain, bias):
    center = values - row_mean(values)
    inverse = lax.rsqrt(row_mean(center * center) + EPSILON)
    normed = center * inverse
    return normed * gain + bias, normed, inverse


def norm_backward(upstream, normed, inverse, gain):
    scaled = upstream * gain
    return inverse * (scaled - row_mean(scaled) - normed * row_mean(scaled * normed))


def forward_window(
    ids, lengths, given, wide, down, norms,
    x_out, qkv_out, probs_out, context_out, n1_out, h1_out, n2_out, inv_out, layer_out, hop_out,
    w_qkv, w_out, w_gu, w_down, x, qkv, probs, context, n1, h1, n2, inv, result, norm,
    w_sem, o_sem, i_sem, *, micro,
):
    window = ids[1]
    copies = {}
    copies["x"] = begin(given, x, i_sem.at[0])
    for k in range(3):
        cols = pl.ds(D * k, D)
        copies["qkv", k] = begin(wide.at[:, cols], w_qkv.at[:, cols], w_sem.at[k])
    copies["norm"] = begin(norms, norm, i_sem.at[1])

    def fetch_chunk(j):
        gate = wide.at[:, pl.ds(COL_GU + j * CHUNK, CHUNK)]
        rise = wide.at[:, pl.ds(COL_GU + FF + j * CHUNK, CHUNK)]
        copies["gate", j] = begin(gate, w_gu.at[j], w_sem.at[4 + j])
        copies["up", j] = begin(rise, w_gu.at[CHUNKS + j], w_sem.at[4 + CHUNKS + j])
        rows = down.at[pl.ds(j * CHUNK, CHUNK)]
        copies["down", j] = begin(rows, w_down.at[j], w_sem.at[4 + 2 * CHUNKS + j])

    flushed = []

    def flush(source, target):
        flushed.append(begin(source, target, o_sem.at[len(flushed)]))

    row_place = lax.broadcasted_iota(jnp.int32, (SEQ, SEQ), 0)
    key_place = lax.broadcasted_iota(jnp.int32, (SEQ, SEQ), 1)
    distance = jnp.abs(row_place - key_place).astype(F32)
    distance = jnp.where(key_place < lengths[micro, window], distance, FAR)
    lane = lax.broadcasted_iota(jnp.int32, (SEQ, 128), 1)
    first = lane < HEAD
    copies["x"].wait()
    rows_in = x[...]
    flush(x, x_out.at[micro])
    for k in range(3):
        copies["qkv", k].wait()
        if k == 1:
            copies["out"] = begin(wide.at[:, pl.ds(COL_OUT, D)], w_out, w_sem.at[3])
            fetch_chunk(0)
        if k == 2:
            for j in range(1, CHUNKS):
                fetch_chunk(j)
        cols = pl.ds(D * k, D)
        qkv[:, cols] = matmul(rows_in, w_qkv[:, cols]).astype(BF)
    flush(qkv, qkv_out.at[micro])
    for pair in range(HEADS // 2):
        query = qkv[:, pl.ds(128 * pair, 128)] * jnp.asarray(HEAD ** (-0.5), BF)
        key = qkv[:, pl.ds(D + 128 * pair, 128)]
        value = qkv[:, pl.ds(2 * D + 128 * pair, 128)]
        total = None
        for side in range(2):
            head = 2 * pair + side
            keep = first if side == 0 else ~first
            own_query = jnp.where(keep, query, jnp.zeros_like(query))
            own_value = jnp.where(keep, value, jnp.zeros_like(value))
            scores = matmul(own_query, key, NT) - distance * SLOPES[head]
            peak = jnp.max(scores, axis=-1, keepdims=True)
            grown = jnp.exp(scores - peak)
            share = 1.0 / jnp.sum(grown, axis=-1, keepdims=True)
            low_probs = (grown * share).astype(BF)
            probs[head] = low_probs
            mixed = matmul(low_probs, own_value)
            total = mixed if total is None else total + mixed
        context[:, pl.ds(128 * pair, 128)] = total.astype(BF)
    flush(probs, probs_out.at[micro])
    flush(context, context_out.at[micro])
    copies["out"].wait()
    copies["norm"].wait()
    summed = rows_in.astype(F32) + matmul(context[...], w_out[...])
    hidden, normed, inverse_one = norm_forward(summed, norm[0:1, :], norm[2:3, :])
    n1[...] = normed
    flush(n1, n1_out.at[micro])
    low_hidden = hidden.astype(BF)
    h1[...] = low_hidden
    flush(h1, h1_out.at[micro])
    for j in range(CHUNKS):
        copies["gate", j].wait()
        copies["up", j].wait()
        gate = matmul(low_hidden, w_gu[j])
        rise = matmul(low_hidden, w_gu[CHUNKS + j])
        gated = (gate * (0.5 * (1.0 + lax.erf(gate * ROOT_HALF))) * rise).astype(BF)
        copies["down", j].wait()
        hidden = hidden + matmul(gated, w_down[j])
    final, normed, inverse_two = norm_forward(hidden, norm[1:2, :], norm[3:4, :])
    result[...] = final.astype(BF)
    flush(result, hop_out)
    flush(result, layer_out.at[micro])
    n2[...] = normed
    flush(n2, n2_out.at[micro])
    inv[...] = jnp.where(first, inverse_one, inverse_two)
    flush(inv, inv_out.at[micro])
    for copy in flushed:
        copy.wait()


def backward_window(
    ids, given, wide, down, norms, qkv_in, probs_in, n1_in, h1_in, n2_in, inv_in,
    gated_out, down_out, gu_out, attn_out, qkv_out, grad_out, norm_out, hop_out,
    w_qkv, w_out, w_gu, w_down, upstream, qkv, probs, n1, h1, n2, inv, norm,
    gated, down_grad, gu_grad, attn_grad, context_grad, qkv_grad, grad, norm_grad, result,
    w_sem, o_sem, i_sem, *, micro,
):
    arriving = begin(given, upstream, i_sem.at[0])
    normed_two = begin(n2_in.at[micro], n2, i_sem.at[1])
    inverses = begin(inv_in.at[micro], inv, i_sem.at[2])
    gains = begin(norms, norm, i_sem.at[3])
    hidden = begin(h1_in.at[micro], h1, i_sem.at[4])
    copies = {}

    def fetch_chunk(j):
        gate = wide.at[:, pl.ds(COL_GU + j * CHUNK, CHUNK)]
        rise = wide.at[:, pl.ds(COL_GU + FF + j * CHUNK, CHUNK)]
        copies["gate", j] = begin(gate, w_gu.at[j], w_sem.at[j])
        copies["up", j] = begin(rise, w_gu.at[CHUNKS + j], w_sem.at[CHUNKS + j])
        rows = down.at[pl.ds(j * CHUNK, CHUNK)]
        copies["down", j] = begin(rows, w_down.at[j], w_sem.at[2 * CHUNKS + j])

    fetch_chunk(0)
    flushed = []

    def flush(source, target):
        flushed.append(begin(source, target, o_sem.at[len(flushed)]))

    arriving.wait()
    normed_two.wait()
    inverses.wait()
    gains.wait()
    up = upstream[...].astype(F32)
    normed = n2[...]
    grad_two = norm_backward(up, normed, inv[:, HEAD : HEAD + 1], norm[1:2, :])
    norm_grad[1:2, :] = jnp.sum(up * normed, axis=0, keepdims=True)
    norm_grad[3:4, :] = jnp.sum(up, axis=0, keepdims=True)
    low_grad = grad_two.astype(BF)
    down_grad[...] = low_grad
    flush(down_grad, down_out.at[micro])
    hidden.wait()
    low_hidden = h1[...]
    total = grad_two
    for j in range(CHUNKS):
        copies["gate", j].wait()
        copies["up", j].wait()
        if j + 1 < CHUNKS:
            fetch_chunk(j + 1)
        else:
            copies["probs"] = begin(probs_in.at[micro], probs, i_sem.at[5])
            copies["qkv"] = begin(qkv_in.at[micro], qkv, i_sem.at[6])
            copies["n1"] = begin(n1_in.at[micro], n1, i_sem.at[7])
            copies["out"] = begin(wide.at[:, pl.ds(COL_OUT, D)], w_out, w_sem.at[3 * CHUNKS])
            for k in range(3):
                cols = pl.ds(D * k, D)
                copies["w_qkv", k] = begin(
                    wide.at[:, cols], w_qkv.at[:, cols], w_sem.at[3 * CHUNKS + 1 + k]
                )
        gate = matmul(low_hidden, w_gu[j])
        rise = matmul(low_hidden, w_gu[CHUNKS + j])
        copies["down", j].wait()
        gated_grad = matmul(low_grad, w_down[j], NT)
        cdf = 0.5 * (1.0 + lax.erf(gate * ROOT_HALF))
        density = jnp.exp(-0.5 * gate * gate) * INV_SQRT_2PI
        bent = gate * cdf
        cols = pl.ds(j * CHUNK, CHUNK)
        late_cols = pl.ds(FF + j * CHUNK, CHUNK)
        gated[:, cols] = (bent * rise).astype(BF)
        flush(gated.at[:, cols], gated_out.at[micro, :, cols])
        gate_grad = (gated_grad * rise * (cdf + gate * density)).astype(BF)
        rise_grad = (gated_grad * bent).astype(BF)
        gu_grad[:, cols] = gate_grad
        gu_grad[:, late_cols] = rise_grad
        flush(gu_grad.at[:, cols], gu_out.at[micro, :, cols])
        flush(gu_grad.at[:, late_cols], gu_out.at[micro, :, late_cols])
        total = total + matmul(gate_grad, w_gu[j], NT) + matmul(rise_grad, w_gu[CHUNKS + j], NT)
    copies["n1"].wait()
    normed = n1[...]
    grad_one = norm_backward(total, normed, inv[:, 0:1], norm[0:1, :])
    norm_grad[0:1, :] = jnp.sum(total * normed, axis=0, keepdims=True)
    norm_grad[2:3, :] = jnp.sum(total, axis=0, keepdims=True)
    flush(norm_grad, norm_out.at[micro])
    low_attn = grad_one.astype(BF)
    attn_grad[...] = low_attn
    flush(attn_grad, attn_out.at[micro])
    copies["out"].wait()
    context_grad[...] = matmul(low_attn, w_out[...], NT).astype(BF)
    copies["probs"].wait()
    copies["qkv"].wait()
    first = lax.broadcasted_iota(jnp.int32, (SEQ, 128), 1) < HEAD
    root = jnp.asarray(HEAD ** (-0.5), BF)
    for pair in range(HEADS // 2):
        query = qkv[:, pl.ds(128 * pair, 128)] * root
        key = qkv[:, pl.ds(D + 128 * pair, 128)]
        value = qkv[:, pl.ds(2 * D + 128 * pair, 128)]
        upper = context_grad[:, pl.ds(128 * pair, 128)]
        query_across = query.T
        upper_across = upper.T
        query_sum, key_parts, value_parts = None, [], []
        for side in range(2):
            keep = first if side == 0 else ~first
            own_upper = jnp.where(keep, upper, jnp.zeros_like(upper))
            own_key = jnp.where(keep, key * root, jnp.zeros_like(key))
            low_probs = probs[2 * pair + side]
            wide_probs = low_probs.astype(F32)
            weighted = wide_probs * matmul(own_upper, value, NT)
            inner = jnp.sum(weighted, axis=-1, keepdims=True)
            score_grad = (weighted - wide_probs * inner).astype(BF)
            part = matmul(score_grad, own_key)
            query_sum = part if query_sum is None else query_sum + part
            rows = slice(HEAD * side, HEAD * (side + 1))
            key_parts.append(matmul(query_across[rows], score_grad))
            value_parts.append(matmul(upper_across[rows], low_probs))
        qkv_grad[:, pl.ds(128 * pair, 128)] = query_sum.astype(BF)
        key_grad = jnp.concatenate(key_parts, axis=0).T
        qkv_grad[:, pl.ds(D + 128 * pair, 128)] = key_grad.astype(BF)
        value_grad = jnp.concatenate(value_parts, axis=0).T
        qkv_grad[:, pl.ds(2 * D + 128 * pair, 128)] = value_grad.astype(BF)
    flush(qkv_grad, qkv_out.at[micro])
    input_grad = grad_one
    for k in range(3):
        copies["w_qkv", k].wait()
        cols = pl.ds(D * k, D)
        input_grad = input_grad + matmul(qkv_grad[:, cols], w_qkv[:, cols], NT)
    result[...] = input_grad.astype(BF)
    flush(result, hop_out)
    grad[...] = input_grad
    flush(grad, grad_out.at[micro])
    for copy in flushed:
        copy.wait()


FORWARD_KEPT = (
    (SEQ, D, BF),
    (SEQ, 3 * D, BF),
    (HEADS, SEQ, SEQ, BF),
    (SEQ, D, BF),
    (SEQ, D, F32),
    (SEQ, D, BF),
    (SEQ, D, F32),
    (SEQ, 128, F32),
    (SEQ, D, BF),
)
BACKWARD_KEPT = (
    (SEQ, FF, BF),
    (SEQ, D, BF),
    (SEQ, 2 * FF, BF),
    (SEQ, D, BF),
    (SEQ, 3 * D, BF),
    (SEQ, D, F32),
    (8, D, F32),
)
WEIGHT_SCRATCH = (
    pltpu.VMEM((D, 3 * D), BF),
    pltpu.VMEM((D, D), BF),
    pltpu.VMEM((2 * CHUNKS, D, CHUNK), BF),
    pltpu.VMEM((CHUNKS, CHUNK, D), BF),
)
DMA = pltpu.SemaphoreType.DMA


def guarded(body, inputs, kept, owner, carried):
    def kernel(*refs):
        @pl.when(refs[0][0] == owner)
        def _():
            skip = kept if carried else 0
            body(*refs[:inputs], *refs[inputs + skip :])

    return kernel


def call_window(body, name, owner, inputs, kept_shapes, before, scratch, flops, small):
    carried = before is not None
    count = len(kept_shapes)
    operands = tuple(inputs) + (tuple(before) if carried else ())
    shapes = [jax.ShapeDtypeStruct((MICRO,) + s[:-1], s[-1]) for s in kept_shapes]
    shapes.append(jax.ShapeDtypeStruct((SEQ, D), BF))
    specs = [SMEM] * small + [ANY] * (len(operands) - small)
    aliases = {len(inputs) + i: i for i in range(count)} if carried else {}
    return pl.pallas_call(
        guarded(body, len(inputs), count, owner, carried),
        out_shape=shapes,
        in_specs=specs,
        out_specs=[ANY] * (count + 1),
        input_output_aliases=aliases,
        scratch_shapes=list(WEIGHT_SCRATCH) + scratch,
        compiler_params=pltpu.CompilerParams(vmem_limit_bytes=58 << 20),
        cost_estimate=pl.CostEstimate(
            flops=flops, bytes_accessed=30_000_000, transcendentals=1_600_000
        ),
        name=name,
    )(*operands)


def forward_call(owner, micro, ids, lengths, given, wide, down, norms, before):
    scratch = [
        pltpu.VMEM((SEQ, D), BF),
        pltpu.VMEM((SEQ, 3 * D), BF),
        pltpu.VMEM((HEADS, SEQ, SEQ), BF),
        pltpu.VMEM((SEQ, D), BF),
        pltpu.VMEM((SEQ, D), F32),
        pltpu.VMEM((SEQ, D), BF),
        pltpu.VMEM((SEQ, D), F32),
        pltpu.VMEM((SEQ, 128), F32),
        pltpu.VMEM((SEQ, D), BF),
        pltpu.VMEM((8, D), F32),
        DMA((4 + 3 * CHUNKS,)),
        DMA((10,)),
        DMA((2,)),
    ]
    return call_window(
        functools.partial(forward_window, micro=micro),
        "layer_forward",
        owner,
        (ids, lengths, given, wide, down, norms),
        FORWARD_KEPT,
        before,
        scratch,
        5_000_000_000,
        2,
    )


def backward_call(owner, micro, ids, given, wide, down, norms, stash, before):
    scratch = [
        pltpu.VMEM((SEQ, D), BF),
        pltpu.VMEM((SEQ, 3 * D), BF),
        pltpu.VMEM((HEADS, SEQ, SEQ), BF),
        pltpu.VMEM((SEQ, D), F32),
        pltpu.VMEM((SEQ, D), BF),
        pltpu.VMEM((SEQ, D), F32),
        pltpu.VMEM((SEQ, 128), F32),
        pltpu.VMEM((8, D), F32),
        pltpu.VMEM((SEQ, FF), BF),
        pltpu.VMEM((SEQ, D), BF),
        pltpu.VMEM((SEQ, 2 * FF), BF),
        pltpu.VMEM((SEQ, D), BF),
        pltpu.VMEM((SEQ, D), BF),
        pltpu.VMEM((SEQ, 3 * D), BF),
        pltpu.VMEM((SEQ, D), F32),
        pltpu.VMEM((8, D), F32),
        pltpu.VMEM((SEQ, D), BF),
        DMA((4 + 3 * CHUNKS,)),
        DMA((6 + 3 * CHUNKS,)),
        DMA((8,)),
    ]
    return call_window(
        functools.partial(backward_window, micro=micro),
        "layer_backward",
        owner,
        (ids, given, wide, down, norms) + tuple(stash),
        BACKWARD_KEPT,
        before,
        scratch,
        8_000_000_000,
        1,
    )


def pack(w_qkv, w_out, w_gate_up, w_down, norm_gain, norm_bias):
    rows = w_qkv.shape[0]
    split_down = w_down.reshape(4, rows, D).transpose(1, 0, 2).reshape(rows, FF)
    norms = jnp.concatenate([norm_gain, norm_bias], axis=0).T
    norms = jnp.pad(norms, ((0, 0), (0, 128 - 4)))
    return jnp.concatenate([w_qkv, w_out, w_gate_up, split_down, norms], axis=1)


def shards(tokens, lengths, w_qkv, w_out, w_gate_up, w_down, norm_gain, norm_bias, cotangent):
    rows = w_qkv.shape[1]
    devices = D // rows
    section = lax.axis_index("section")
    ids = jnp.stack([section, lax.axis_index("dp")]).astype(jnp.int32)
    packed = pack(
        *(w[0].astype(BF) for w in (w_qkv, w_out, w_gate_up, w_down, norm_gain, norm_bias))
    )
    wide = lax.all_gather(packed, "dp", axis=0, tiled=True)
    down = wide[:, COL_DOWN:COL_NORM].reshape(devices, rows, 4, D)
    down = down.transpose(0, 2, 1, 3).reshape(FF, D)
    norms = wide[:, COL_NORM : COL_NORM + 8].astype(F32).T

    def hop(rows_sent, pair):
        return lax.ppermute(rows_sent, "section", [pair])

    common = (ids, lengths)
    weights = (wide, down, norms)
    *kept, sent = forward_call(0, 0, *common, tokens[0], *weights, None)
    arrived_first = hop(sent, (0, 1))
    *kept, sent = forward_call(0, 1, *common, tokens[1], *weights, kept)
    arrived_second = hop(sent, (0, 1))
    *kept, sent = forward_call(1, 0, *common, arrived_first, *weights, kept)
    *kept, sent = forward_call(1, 1, *common, arrived_second, *weights, kept)
    inputs, qkv, probs, context, n1, h1, n2, inv, layer_out = kept
    stash = (qkv, probs, n1, h1, n2, inv)

    *grads, sent = backward_call(1, 0, ids, cotangent[0], *weights, stash, None)
    arrived_first = hop(sent, (1, 0))
    *grads, sent = backward_call(1, 1, ids, cotangent[1], *weights, stash, grads)
    arrived_second = hop(sent, (1, 0))
    *grads, sent = backward_call(0, 0, ids, arrived_first, *weights, stash, grads)
    *grads, sent = backward_call(0, 1, ids, arrived_second, *weights, stash, grads)
    gated, down_grad, gu_grad, attn_grad, qkv_grad, input_grads, norm_grads = grads

    def flat(values):
        return values.reshape(MICRO * SEQ, values.shape[-1])

    def weight_grad(left, right):
        return matmul(flat(left), flat(right), TN)

    grad_qkv = weight_grad(inputs, qkv_grad).astype(BF)
    grad_out = weight_grad(context, attn_grad).astype(BF)
    grad_gu = weight_grad(h1, gu_grad).astype(BF)
    grad_down = weight_grad(gated, down_grad).astype(BF)
    grad_down = grad_down.reshape(devices, 4, rows, D).transpose(0, 2, 1, 3).reshape(D, FF)
    norm_sum = jnp.sum(norm_grads, axis=0)[:4].T.astype(BF)
    norm_sum = jnp.pad(norm_sum, ((0, 0), (0, 128 - 4)))
    summed = jnp.concatenate([grad_qkv, grad_out, grad_gu, grad_down, norm_sum], axis=1)
    share = lax.psum_scatter(summed, "dp", scatter_dimension=0, tiled=True).astype(F32)
    share_down = share[:, COL_DOWN:COL_NORM].reshape(rows, 4, D).transpose(1, 0, 2)
    share_norm = share[:, COL_NORM : COL_NORM + 4].T
    return (
        layer_out[None],
        input_grads[None],
        share[:, :COL_OUT][None],
        share[:, COL_OUT:COL_GU][None],
        share[:, COL_GU:COL_DOWN][None],
        share_down.reshape(4 * rows, D)[None],
        share_norm[:2][None],
        share_norm[2:][None],
    )


def solution(mesh):
    return jax.shard_map(
        shards,
        mesh=mesh,
        in_specs=(
            P(None, "dp", None),
            P(),
            P("section", "dp", None),
            P("section", "dp", None),
            P("section", "dp", None),
            P("section", "dp", None),
            P("section", None, "dp"),
            P("section", None, "dp"),
            P(None, "dp", None),
        ),
        out_specs=(
            P("section", None, "dp", None),
            P("section", None, "dp", None),
            P("section", "dp", None),
            P("section", "dp", None),
            P("section", "dp", None),
            P("section", "dp", None),
            P("section", None, "dp"),
            P("section", None, "dp"),
        ),
        check_vma=False,
    )
```

```python
import functools

import jax
import jax.numpy as jnp
from jax import lax
from jax.experimental import pallas as pl
from jax.experimental.pallas import tpu as pltpu
from jax.sharding import PartitionSpec as P

D = 768
HEADS = 12
HEAD = 64
FF = 3072
SEQ = 256
MICRO = 2
TOKENS = 2 * MICRO * SEQ
EPSILON = 1e-05
FAR = 1e30
INV_SQRT_2PI = 0.3989422804014327
ROOT_HALF = 2.0 ** (-0.5)

COL_OUT = 3 * D
COL_GU = 4 * D
COL_DOWN = COL_GU + 2 * FF
COL_NORM = COL_DOWN + FF
WIDE = COL_NORM + 128

CHUNK = 768
CHUNKS = FF // CHUNK
ROWS = 48
BF = jnp.bfloat16
F32 = jnp.float32
NN = (((1,), (0,)), ((), ()))
NT = (((1,), (1,)), ((), ()))
TN = (((0,), (0,)), ((), ()))
SLOPES = [2.0 ** (-8.0 * (h + 1) / HEADS) for h in range(HEADS)]

VMEM_LIMIT = 64 << 20
ANY = pl.BlockSpec(memory_space=pl.ANY)
SMEM = pl.BlockSpec(memory_space=pltpu.SMEM)


def matmul(left, right, dims=NN):
    return lax.dot_general(left, right, dims, preferred_element_type=F32)


def begin(source, target, semaphore):
    copy = pltpu.make_async_copy(source, target, semaphore)
    copy.start()
    return copy


def own_window(given, micro):
    return given if len(given.shape) == 2 else given.at[micro]


def row_mean(values):
    return jnp.mean(values, axis=-1, keepdims=True)


def norm_forward(values, gain, bias):
    center = values - row_mean(values)
    inverse = lax.rsqrt(row_mean(center * center) + EPSILON)
    normed = center * inverse
    return normed * gain + bias, normed, inverse


def norm_backward(upstream, normed, inverse, gain):
    scaled = upstream * gain
    return inverse * (scaled - row_mean(scaled) - normed * row_mean(scaled * normed))


def forward_window(
    ids, lengths, given, wide, down, norms,
    left_out, qkv_out, probs_out, n1_out, h1_out, n2_out, inv_out, layer_out, hop_out,
    w_qkv, w_out, w_gu, w_down, x, qkv, probs, context, n1, h1, n2, inv, result, norm, left,
    w_sem, o_sem, i_sem, *, micro, direct,
):
    window = ids[1]
    copies = {}
    copies["x"] = begin(own_window(given, micro), x, i_sem.at[0])
    for k in range(3):
        cols = pl.ds(D * k, D)
        copies["qkv", k] = begin(wide.at[:, cols], w_qkv.at[:, cols], w_sem.at[k])
    copies["norm"] = begin(norms, norm, i_sem.at[1])

    def fetch_down(j, base):
        owners = down.at[pl.ds(4 * j, 4)]
        for q in range(4):
            source = owners.at[:, :, pl.ds(COL_DOWN + D * q, D)] if direct else owners.at[:, q]
            copies["down", j, q] = begin(
                source, w_down.at[j, :, q], w_sem.at[base + 4 * j + q]
            )

    def fetch_chunk(j):
        gate = wide.at[:, pl.ds(COL_GU + j * CHUNK, CHUNK)]
        rise = wide.at[:, pl.ds(COL_GU + FF + j * CHUNK, CHUNK)]
        copies["gate", j] = begin(gate, w_gu.at[j], w_sem.at[4 + j])
        copies["up", j] = begin(rise, w_gu.at[CHUNKS + j], w_sem.at[4 + CHUNKS + j])
        fetch_down(j, 4 + 2 * CHUNKS)

    flushed = []

    def flush(source, target):
        flushed.append(begin(source, target, o_sem.at[len(flushed)]))

    row_place = lax.broadcasted_iota(jnp.int32, (SEQ, SEQ), 0)
    key_place = lax.broadcasted_iota(jnp.int32, (SEQ, SEQ), 1)
    distance = jnp.abs(row_place - key_place).astype(F32)
    distance = jnp.where(key_place < lengths[micro, window], distance, FAR)
    lane = lax.broadcasted_iota(jnp.int32, (SEQ, 128), 1)
    first = lane < HEAD
    copies["x"].wait()
    rows_in = x[...]


    def flush_turned(part, values):
        rows = pl.ds(D * part, D)
        left[rows] = values.T
        flush(left.at[rows], left_out.at[rows])

    flush_turned(0, rows_in)
    for k in range(3):
        copies["qkv", k].wait()
        if k == 1:
            copies["out"] = begin(wide.at[:, pl.ds(COL_OUT, D)], w_out, w_sem.at[3])
            fetch_chunk(0)
        if k == 2:
            for j in range(1, CHUNKS):
                fetch_chunk(j)
        cols = pl.ds(D * k, D)
        qkv[:, cols] = matmul(rows_in, w_qkv[:, cols]).astype(BF)
    flush(qkv, qkv_out)
    for pair in range(HEADS // 2):
        query = qkv[:, pl.ds(128 * pair, 128)] * jnp.asarray(HEAD ** (-0.5), BF)
        key = qkv[:, pl.ds(D + 128 * pair, 128)]
        value = qkv[:, pl.ds(2 * D + 128 * pair, 128)]
        total = None
        for side in range(2):
            head = 2 * pair + side
            keep = first if side == 0 else ~first
            own_query = jnp.where(keep, query, jnp.zeros_like(query))
            own_value = jnp.where(keep, value, jnp.zeros_like(value))
            scores = matmul(own_query, key, NT) - distance * SLOPES[head]
            peak = jnp.max(scores, axis=-1, keepdims=True)
            grown = jnp.exp(scores - peak)
            share = 1.0 / jnp.sum(grown, axis=-1, keepdims=True)
            low_probs = (grown * share).astype(BF)
            probs[head] = low_probs
            mixed = matmul(low_probs, own_value)
            total = mixed if total is None else total + mixed
        context[:, pl.ds(128 * pair, 128)] = total.astype(BF)
    flush(probs, probs_out)
    flush_turned(1, context[...])
    copies["out"].wait()
    copies["norm"].wait()
    summed = rows_in.astype(F32) + matmul(context[...], w_out[...])
    hidden, normed, inverse_one = norm_forward(summed, norm[0:1, :], norm[2:3, :])
    n1[...] = normed
    flush(n1, n1_out)
    low_hidden = hidden.astype(BF)
    h1[...] = low_hidden
    flush(h1, h1_out)
    flush_turned(2, low_hidden)
    for j in range(CHUNKS):
        copies["gate", j].wait()
        copies["up", j].wait()
        gate = matmul(low_hidden, w_gu[j])
        rise = matmul(low_hidden, w_gu[CHUNKS + j])
        gated = (gate * (0.5 * (1.0 + lax.erf(gate * ROOT_HALF))) * rise).astype(BF)
        for q in range(4):
            copies["down", j, q].wait()
        hidden = hidden + matmul(gated, w_down[j].reshape(CHUNK, D))
    final, normed, inverse_two = norm_forward(hidden, norm[1:2, :], norm[3:4, :])
    result[...] = final.astype(BF)
    flush(result, hop_out)
    flush(result, layer_out)
    n2[...] = normed
    flush(n2, n2_out)
    inv[...] = jnp.where(first, inverse_one, inverse_two)
    flush(inv, inv_out)
    for copy in flushed:
        copy.wait()


def backward_hidden(
    ids, given, wide, down, norms, n1_in, h1_in, n2_in, inv_in, hidden_out, gate_out, up_out,
    w_gu, w_down, upstream, n1, h1, n2, inv, norm, gated, down_grad, gu_grad, norm_grad,
    low_norm, w_sem, o_sem, i_sem, *, micro, direct, ahead,
):
    arriving = begin(own_window(given, micro), upstream, i_sem.at[0])
    normed_two = begin(n2_in.at[micro], n2, i_sem.at[1])
    inverses = begin(inv_in.at[micro], inv, i_sem.at[2])
    gains = begin(norms, norm, i_sem.at[3])
    hidden = begin(h1_in.at[micro], h1, i_sem.at[4])
    copies = {}

    def fetch_down(j, base):
        owners = down.at[pl.ds(4 * j, 4)]
        for q in range(4):
            source = owners.at[:, :, pl.ds(COL_DOWN + D * q, D)] if direct else owners.at[:, q]
            copies["down", j, q] = begin(
                source, w_down.at[j, :, q], w_sem.at[base + 4 * j + q]
            )

    def fetch_chunk(j):
        gate = wide.at[:, pl.ds(COL_GU + j * CHUNK, CHUNK)]
        rise = wide.at[:, pl.ds(COL_GU + FF + j * CHUNK, CHUNK)]
        copies["gate", j] = begin(gate, w_gu.at[j], w_sem.at[j])
        copies["up", j] = begin(rise, w_gu.at[CHUNKS + j], w_sem.at[CHUNKS + j])
        fetch_down(j, 2 * CHUNKS)

    fetch_chunk(0)
    flushed = []

    def flush(source, target):
        flushed.append(begin(source, target, o_sem.at[len(flushed)]))

    arriving.wait()
    normed_two.wait()
    inverses.wait()
    gains.wait()
    up = upstream[...].astype(F32)
    normed = n2[...]
    grad_two = norm_backward(up, normed, inv[:, HEAD : HEAD + 1], norm[1:2, :])
    norm_grad[...] = jnp.zeros_like(norm_grad)
    norm_grad[1:2, :] = jnp.sum(up * normed, axis=0, keepdims=True)
    norm_grad[3:4, :] = jnp.sum(up, axis=0, keepdims=True)
    low_grad = grad_two.astype(BF)
    down_grad[...] = low_grad.T
    flush(down_grad, hidden_out.at[pl.ds(FF, D)])
    hidden.wait()
    low_hidden = h1[...]
    total = grad_two
    for j in range(CHUNKS):
        copies["gate", j].wait()
        copies["up", j].wait()
        if j + 1 < CHUNKS:
            fetch_chunk(j + 1)
        else:
            first_norm = begin(n1_in.at[micro], n1, i_sem.at[5])
            ahead()
        gate = matmul(low_hidden, w_gu[j])
        rise = matmul(low_hidden, w_gu[CHUNKS + j])
        for q in range(4):
            copies["down", j, q].wait()
        gated_grad = matmul(low_grad, w_down[j].reshape(CHUNK, D), NT)
        cdf = 0.5 * (1.0 + lax.erf(gate * ROOT_HALF))
        density = jnp.exp(-0.5 * gate * gate) * INV_SQRT_2PI
        bent = gate * cdf
        cols = pl.ds(j * CHUNK, CHUNK)
        late_cols = pl.ds(FF + j * CHUNK, CHUNK)
        gated[cols] = (bent * rise).astype(BF).T
        flush(gated.at[cols], hidden_out.at[cols])
        gate_grad = (gated_grad * rise * (cdf + gate * density)).astype(BF)
        rise_grad = (gated_grad * bent).astype(BF)
        gu_grad[:, cols] = gate_grad
        gu_grad[:, late_cols] = rise_grad
        flush(gu_grad.at[:, cols], gate_out.at[:, cols])
        flush(gu_grad.at[:, late_cols], up_out.at[:, cols])
        total = total + matmul(gate_grad, w_gu[j], NT) + matmul(rise_grad, w_gu[CHUNKS + j], NT)
    first_norm.wait()
    normed = n1[...]
    grad_one = norm_backward(total, normed, inv[:, 0:1], norm[0:1, :])
    norm_grad[0:1, :] = jnp.sum(total * normed, axis=0, keepdims=True)
    norm_grad[2:3, :] = jnp.sum(total, axis=0, keepdims=True)
    low_norm[...] = norm_grad[...].astype(BF)
    for k in range(3):
        source = low_norm.at[:, pl.ds(SEQ * k, SEQ)]
        flush(source, hidden_out.at[pl.ds(FF + D + 16 * k, 16)])
    return grad_one, flushed


def fetch_attention(wide, qkv_in, probs_in, w_qkv, w_out, qkv, probs, w_sem, i_sem, micro):
    copies = [
        begin(wide.at[:, pl.ds(COL_OUT, D)], w_out, w_sem.at[0]),
        begin(probs_in.at[micro], probs, i_sem.at[0]),
        begin(qkv_in.at[micro], qkv, i_sem.at[1]),
    ]
    for k in range(3):
        cols = pl.ds(D * k, D)
        copies.append(begin(wide.at[:, cols], w_qkv.at[:, cols], w_sem.at[1 + k]))
    return copies


def backward_attention(
    grad_one, copies, qk_out, vc_out, grad_out, hop_out,
    w_qkv, w_out, qkv, probs, attn_grad, context_grad, qkv_grad, grad, result,
    o_sem, *, micro,
):
    flushed = []

    def flush(source, target):
        flushed.append(begin(source, target, o_sem.at[len(flushed)]))

    low_attn = grad_one.astype(BF)
    attn_grad[...] = low_attn
    flush(attn_grad, vc_out.at[:, pl.ds(D, D)])
    copies[0].wait()
    context_grad[...] = matmul(low_attn, w_out[...], NT).astype(BF)
    copies[1].wait()
    copies[2].wait()
    first = lax.broadcasted_iota(jnp.int32, (SEQ, 128), 1) < HEAD
    root = jnp.asarray(HEAD ** (-0.5), BF)
    for pair in range(HEADS // 2):
        query = qkv[:, pl.ds(128 * pair, 128)] * root
        key = qkv[:, pl.ds(D + 128 * pair, 128)]
        value = qkv[:, pl.ds(2 * D + 128 * pair, 128)]
        upper = context_grad[:, pl.ds(128 * pair, 128)]
        query_across = query.T
        upper_across = upper.T
        query_sum, key_parts, value_parts = None, [], []
        for side in range(2):
            keep = first if side == 0 else ~first
            own_upper = jnp.where(keep, upper, jnp.zeros_like(upper))
            own_key = jnp.where(keep, key * root, jnp.zeros_like(key))
            low_probs = probs[2 * pair + side]
            wide_probs = low_probs.astype(F32)
            weighted = wide_probs * matmul(own_upper, value, NT)
            inner = jnp.sum(weighted, axis=-1, keepdims=True)
            score_grad = (weighted - wide_probs * inner).astype(BF)
            part = matmul(score_grad, own_key)
            query_sum = part if query_sum is None else query_sum + part
            rows = slice(HEAD * side, HEAD * (side + 1))
            key_parts.append(matmul(query_across[rows], score_grad))
            value_parts.append(matmul(upper_across[rows], low_probs))
        qkv_grad[:, pl.ds(128 * pair, 128)] = query_sum.astype(BF)
        key_grad = jnp.concatenate(key_parts, axis=0).T
        qkv_grad[:, pl.ds(D + 128 * pair, 128)] = key_grad.astype(BF)
        value_grad = jnp.concatenate(value_parts, axis=0).T
        qkv_grad[:, pl.ds(2 * D + 128 * pair, 128)] = value_grad.astype(BF)
    flush(qkv_grad.at[:, pl.ds(0, 2 * D)], qk_out)
    flush(qkv_grad.at[:, pl.ds(2 * D, D)], vc_out.at[:, pl.ds(0, D)])
    input_grad = grad_one
    for k in range(3):
        copies[3 + k].wait()
        cols = pl.ds(D * k, D)
        input_grad = input_grad + matmul(qkv_grad[:, cols], w_qkv[:, cols], NT)
    result[...] = input_grad.astype(BF)
    flush(result, hop_out)
    grad[...] = input_grad
    flush(grad, grad_out)
    return flushed


def backward_window(
    ids, given, wide, down, norms, qkv_in, probs_in, n1_in, h1_in, n2_in, inv_in,
    hidden_out, gate_out, up_out, qk_out, vc_out, grad_out, hop_out,
    w_gu, w_down, upstream, n1, h1, n2, inv, norm, gated, down_grad, gu_grad, norm_grad, low_norm,
    w_qkv, w_out, qkv, probs, attn_grad, context_grad, qkv_grad, grad, result,
    w_sem, o_sem, i_sem, *, micro, direct,
):
    copies = []

    def ahead():
        copies.extend(
            fetch_attention(
                wide, qkv_in, probs_in, w_qkv, w_out, qkv, probs,
                w_sem.at[pl.ds(6 * CHUNKS, 4)], i_sem.at[pl.ds(6, 2)], micro,
            )
        )

    grad_one, flushed = backward_hidden(
        ids, given, wide, down, norms, n1_in, h1_in, n2_in, inv_in, hidden_out, gate_out, up_out,
        w_gu, w_down, upstream, n1, h1, n2, inv, norm, gated, down_grad, gu_grad, norm_grad,
        low_norm, w_sem, o_sem, i_sem, micro=micro, direct=direct, ahead=ahead,
    )
    flushed += backward_attention(
        grad_one, copies, qk_out, vc_out, grad_out, hop_out,
        w_qkv, w_out, qkv, probs, attn_grad, context_grad, qkv_grad, grad, result,
        o_sem.at[pl.ds(HIDDEN_STORES, 5)], micro=micro,
    )
    for copy in flushed:
        copy.wait()


def backward_first_half(
    ids, given, wide, down, norms, n1_in, h1_in, n2_in, inv_in,
    hidden_out, gate_out, up_out, half_out,
    w_gu, w_down, upstream, n1, h1, n2, inv, norm, gated, down_grad, gu_grad, norm_grad, low_norm,
    half, w_sem, o_sem, i_sem, *, micro, direct,
):
    grad_one, flushed = backward_hidden(
        ids, given, wide, down, norms, n1_in, h1_in, n2_in, inv_in, hidden_out, gate_out, up_out,
        w_gu, w_down, upstream, n1, h1, n2, inv, norm, gated, down_grad, gu_grad, norm_grad,
        low_norm, w_sem, o_sem, i_sem, micro=micro, direct=direct, ahead=lambda: None,
    )
    half[...] = grad_one
    flushed.append(begin(half, half_out, o_sem.at[HIDDEN_STORES]))
    for copy in flushed:
        copy.wait()


def backward_second_half(
    ids, given, wide, qkv_in, probs_in,
    qk_out, vc_out, grad_out, hop_out,
    half, w_qkv, w_out, qkv, probs, attn_grad, context_grad, qkv_grad, grad, result,
    w_sem, o_sem, i_sem, *, micro,
):
    arriving = begin(given, half, i_sem.at[2])
    copies = fetch_attention(
        wide, qkv_in, probs_in, w_qkv, w_out, qkv, probs, w_sem, i_sem, micro
    )
    arriving.wait()
    flushed = backward_attention(
        half[...], copies, qk_out, vc_out, grad_out, hop_out,
        w_qkv, w_out, qkv, probs, attn_grad, context_grad, qkv_grad, grad, result,
        o_sem, micro=micro,
    )
    for copy in flushed:
        copy.wait()


FORWARD_KEPT = (
    (True, 3 * D, SEQ, BF),
    (True, SEQ, 3 * D, BF),
    (True, HEADS, SEQ, SEQ, BF),
    (True, SEQ, D, F32),
    (True, SEQ, D, BF),
    (True, SEQ, D, F32),
    (True, SEQ, 128, F32),
    (True, SEQ, D, BF),
)
HIDDEN_KEPT = ((False, FF + D + 48, SEQ, BF), (False, SEQ, FF, BF), (False, SEQ, FF, BF))
ATTENTION_KEPT = ((False, SEQ, 2 * D, BF), (False, SEQ, 2 * D, BF), (True, SEQ, D, F32))
HIDDEN_STORES = 3 * CHUNKS + 4
HIDDEN_WEIGHTS = (
    pltpu.VMEM((2 * CHUNKS, D, CHUNK), BF),
    pltpu.VMEM((CHUNKS, 4, 4, ROWS, D), BF),
)
ATTENTION_WEIGHTS = (pltpu.VMEM((D, 3 * D), BF), pltpu.VMEM((D, D), BF))
HIDDEN_SCRATCH = HIDDEN_WEIGHTS + (
    pltpu.VMEM((SEQ, D), BF),
    pltpu.VMEM((SEQ, D), F32),
    pltpu.VMEM((SEQ, D), BF),
    pltpu.VMEM((SEQ, D), F32),
    pltpu.VMEM((SEQ, 128), F32),
    pltpu.VMEM((8, D), F32),
    pltpu.VMEM((FF, SEQ), BF),
    pltpu.VMEM((D, SEQ), BF),
    pltpu.VMEM((SEQ, 2 * FF), BF),
    pltpu.VMEM((16, D), F32),
    pltpu.VMEM((16, D), BF),
)
ATTENTION_SCRATCH = ATTENTION_WEIGHTS + (
    pltpu.VMEM((SEQ, 3 * D), BF),
    pltpu.VMEM((HEADS, SEQ, SEQ), BF),
    pltpu.VMEM((SEQ, D), BF),
    pltpu.VMEM((SEQ, D), BF),
    pltpu.VMEM((SEQ, 3 * D), BF),
    pltpu.VMEM((SEQ, D), F32),
    pltpu.VMEM((SEQ, D), BF),
)
DMA = pltpu.SemaphoreType.DMA


def call_window(
    body, name, owner, micro, inputs, kept_shapes, sent, before, scratch, flops, small, gates=()
):
    count = len(kept_shapes)
    operands = tuple(inputs)
    aliases = {}
    for position, array in enumerate(before):
        if array is not None:
            aliases[len(operands)] = position
            operands += (array,)
    operands += tuple(gates)
    shapes = [
        jax.ShapeDtypeStruct((MICRO,) * shared + tuple(shape), dtype)
        for shared, *shape, dtype in kept_shapes
    ]
    shapes.append(jax.ShapeDtypeStruct((SEQ, D), sent))

    def kernel(*refs):
        @pl.when(refs[0][0] == owner)
        def _():
            outs = refs[len(operands) : len(operands) + count]
            views = [
                ref.at[micro] if shared else ref
                for ref, (shared, *_) in zip(outs, kept_shapes)
            ]
            body(*refs[: len(inputs)], *views, *refs[len(operands) + count :])

    return pl.pallas_call(
        kernel,
        out_shape=shapes,
        in_specs=[SMEM] * small + [ANY] * (len(operands) - small),
        out_specs=[ANY] * len(shapes),
        input_output_aliases=aliases,
        scratch_shapes=list(scratch),
        compiler_params=pltpu.CompilerParams(vmem_limit_bytes=VMEM_LIMIT),
        cost_estimate=pl.CostEstimate(
            flops=flops, bytes_accessed=flops // 200, transcendentals=flops // 4000
        ),
        name=name,
    )(*operands)


def forward_call(owner, micro, direct, ids, lengths, given, wide, down, norms, before):
    scratch = (
        ATTENTION_WEIGHTS
        + HIDDEN_WEIGHTS
        + (
            pltpu.VMEM((SEQ, D), BF),
            pltpu.VMEM((SEQ, 3 * D), BF),
            pltpu.VMEM((HEADS, SEQ, SEQ), BF),
            pltpu.VMEM((SEQ, D), BF),
            pltpu.VMEM((SEQ, D), F32),
            pltpu.VMEM((SEQ, D), BF),
            pltpu.VMEM((SEQ, D), F32),
            pltpu.VMEM((SEQ, 128), F32),
            pltpu.VMEM((SEQ, D), BF),
            pltpu.VMEM((8, D), F32),
            pltpu.VMEM((3 * D, SEQ), BF),
            DMA((4 + 6 * CHUNKS,)),
            DMA((12,)),
            DMA((2,)),
        )
    )
    return call_window(
        functools.partial(forward_window, micro=micro, direct=direct),
        "layer_forward",
        owner,
        micro,
        (ids, lengths, given, wide, down, norms),
        FORWARD_KEPT,
        BF,
        before,
        scratch,
        5_000_000_000,
        2,
    )


def backward_call(owner, micro, direct, ids, given, wide, down, norms, stash, before, gates):
    return call_window(
        functools.partial(backward_window, micro=micro, direct=direct),
        "layer_backward",
        owner,
        micro,
        (ids, given, wide, down, norms) + tuple(stash),
        HIDDEN_KEPT + ATTENTION_KEPT,
        BF,
        before,
        HIDDEN_SCRATCH
        + ATTENTION_SCRATCH
        + (DMA((4 + 6 * CHUNKS,)), DMA((HIDDEN_STORES + 5,)), DMA((8,))),
        8_000_000_000,
        1,
        gates,
    )


def first_half_call(
    owner, micro, direct, ids, given, wide, down, norms, stash, before, gates
):
    return call_window(
        functools.partial(backward_first_half, micro=micro, direct=direct),
        "backward_hidden",
        owner,
        micro,
        (ids, given, wide, down, norms) + tuple(stash),
        HIDDEN_KEPT,
        F32,
        before,
        HIDDEN_SCRATCH
        + (
            pltpu.VMEM((SEQ, D), F32),
            DMA((6 * CHUNKS,)),
            DMA((HIDDEN_STORES + 1,)),
            DMA((6,)),
        ),
        60_000_000_000,
        1,
        gates,
    )


def second_half_call(owner, micro, ids, given, wide, stash, before, gates):
    return call_window(
        functools.partial(backward_second_half, micro=micro),
        "backward_attention",
        owner,
        micro,
        (ids, given, wide) + tuple(stash),
        ATTENTION_KEPT,
        BF,
        before,
        (pltpu.VMEM((SEQ, D), F32),) + ATTENTION_SCRATCH + (DMA((4,)), DMA((5,)), DMA((3,))),
        1000,
        1,
        gates,
    )


def pack(w_qkv, w_out, w_gate_up, w_down, norm_gain, norm_bias):
    rows = w_qkv.shape[0]
    split_down = w_down.reshape(4, rows, D).transpose(1, 0, 2).reshape(rows, FF)
    norms = jnp.concatenate([norm_gain, norm_bias], axis=0).T
    norms = jnp.pad(norms, ((0, 0), (0, 128 - 4)))
    return jnp.concatenate([w_qkv, w_out, w_gate_up, split_down, norms], axis=1)


BIT_CORE, BIT_X, BIT_NEAR, BIT_FAR = 1, 2, 4, 8


def weight_grad_kernel(ids, terms, norm_ins, sent, kept, scratch, *, rows, order, turned):
    buffers, result, i_sem, o_sem = scratch[:4]
    columns, pieces, count = 0, [], 0

    def fetch(source, target):
        nonlocal count
        count += 1
        return begin(source, target, i_sem.at[count - 1])

    owned = []
    for place in range(8):
        relative = sum(bit for k, bit in enumerate(order) if not (place >> (2 - k)) & 1)
        owned.append(ids[1] ^ relative)
    for term, (lefts, rights) in enumerate(terms):
        left_buffer, right_buffer = buffers[term]
        whole = []
        for k, left in enumerate(lefts):
            for place in range(8):
                source = left.at[pl.ds(pl.multiple_of(owned[place] * rows, 16), rows)]
                target = left_buffer.at[place, :, pl.ds(SEQ * k, SEQ)]
                whole.append(fetch(source, target))
        for start in range(0, D if turned else right_buffer.shape[1], D):
            cols = pl.ds(start, D)
            parts = []
            for k, right in enumerate(rights):
                tokens = pl.ds(SEQ * k, SEQ)
                if turned:
                    parts.append(fetch(right, right_buffer.at[:, tokens]))
                else:
                    parts.append(fetch(right.at[:, cols], right_buffer.at[tokens, cols]))
            pieces.append((term, start, whole, parts, columns))
            columns += D
            whole = []
    if norm_ins:
        norm_buffer, norm_turned, norm_sem = scratch[4:]
        norm_loads = [
            begin(source.at[pl.ds(16 * k, 16)], norm_buffer.at[n, :, pl.ds(SEQ * k, SEQ)], norm_sem.at[n, k])
            for n, source in enumerate(norm_ins)
            for k in range(3)
        ]
    stores = []

    def store(first, count, cols):
        target = sent if first < 4 else kept
        source = result.at[pl.ds(first, count), :, cols]
        place = target.at[pl.ds(first % 4, count), :, cols]
        stores.append(begin(source, place, o_sem.at[len(stores)]))

    group = 192 // rows
    for term, start, whole, parts, column in pieces:
        left_buffer, right_buffer = buffers[term]
        for load in whole + parts:
            load.wait()
        values = right_buffer[...] if turned else right_buffer[:, pl.ds(start, D)]
        cols = pl.ds(column, D)
        for first in range(0, 8, 2 * group):
            taken = left_buffer[pl.ds(first, 2 * group)].reshape(2 * group * rows, TOKENS)
            value = matmul(taken, values, NT if turned else NN).astype(BF)
            result[pl.ds(first, 2 * group), :, cols] = value.reshape(2 * group, rows, D)
            for half in range(2):
                store(first + group * half, group, cols)
    if norm_ins:
        for load in norm_loads:
            load.wait()
        total = sum(norm_buffer[n].astype(F32) for n in range(4))
        total = jnp.concatenate([total, jnp.zeros((112, D), F32)], axis=0).T.astype(BF)
        norm_turned[...] = total.reshape(16, rows, 128)
        cols = pl.ds(columns, 128)
        for place in range(8):
            result[place, :, cols] = norm_turned[owned[place]]
        store(0, 4, cols)
        store(4, 4, cols)
    for copy in stores:
        copy.wait()


def weight_grad(ids, pairs, rows, order, gates, norms=None, turned=False):
    width = 0
    arrays, scratch = [], []

    def position(array):
        for k, known in enumerate(arrays):
            if known is array:
                return k
        arrays.append(array)
        return len(arrays) - 1

    def placed(side):
        return [(position(array), micro) for array, micro in side[0]], side[1]

    terms = [(placed(left), placed(right)) for left, right in pairs]
    norm_places = placed(norms) if norms else None
    loads, stores = 0, 0
    for _, (_, taken) in terms:
        size = taken.stop - taken.start
        shape = (size, TOKENS) if turned else (TOKENS, size)
        scratch += [pltpu.VMEM((8, rows, TOKENS), BF), pltpu.VMEM(shape, BF)]
        loads += 32 + 4 * (size // D)
        stores += 8 * (size // D)
        width += size
    total = width + 128 * bool(norms)
    shape = jax.ShapeDtypeStruct((4, rows, total), BF)
    count = 1 + len(arrays) + len(gates)

    def view(refs, place, taken, along_rows):
        index, micro = place
        ref = refs[1 + index] if micro is None else refs[1 + index].at[micro]
        span = pl.ds(taken.start, taken.stop - taken.start)
        return ref.at[span] if along_rows else ref.at[:, span]

    def body(*refs):
        sources = [
            (
                [view(refs, place, left[1], True) for place in left[0]],
                [view(refs, place, right[1], turned) for place in right[0]],
            )
            for left, right in terms
        ]
        norm_views = []
        if norms:
            norm_views = [view(refs, place, norm_places[1], True) for place in norm_places[0]]
        rest = refs[count + 2 :]
        buffers = [(rest[2 * k], rest[2 * k + 1]) for k in range(len(terms))]
        weight_grad_kernel(
            refs[0],
            sources,
            norm_views,
            refs[count],
            refs[count + 1],
            (buffers,) + tuple(rest[2 * len(terms) :]),
            rows=rows,
            order=order,
            turned=turned,
        )

    scratch += [pltpu.VMEM((8, rows, total), BF), DMA((loads,)), DMA((stores + 2,))]
    if norms:
        scratch += [pltpu.VMEM((4, 16, D), BF), pltpu.VMEM((16, rows, 128), BF), DMA((4, 3))]
    return pl.pallas_call(
        body,
        out_shape=[shape, shape],
        in_specs=[SMEM] + [ANY] * (count - 1),
        out_specs=[ANY] * 2,
        scratch_shapes=scratch,
        compiler_params=pltpu.CompilerParams(vmem_limit_bytes=VMEM_LIMIT),
        cost_estimate=pl.CostEstimate(flops=1000, bytes_accessed=1000, transcendentals=0),
        name="weight_grad",
    )(ids, *arrays, *gates)


def exchange(values, bit):
    count = lax.axis_size("dp")
    return lax.ppermute(values, "dp", [(i, i ^ bit) for i in range(count)])


def halve(parts, gates):
    half = len(parts[0]) // 2
    arrays = []
    for part in parts:
        for array, _ in part[:half]:
            if not any(array is known for known in arrays):
                arrays.append(array)
    where = [
        [next((k, at) for k, known in enumerate(arrays) if known is array) for array, at in part[:half]]
        for part in parts
    ]
    block = arrays[0].shape[1:]
    count = len(parts)

    def body(*refs):
        outgoing, held, result, i_sem, o_sem = refs[len(arrays) + len(gates) :]
        loads = [
            [
                begin(refs[where[p][i][0]].at[where[p][i][1]], held.at[p, i], i_sem.at[p, i])
                for p in range(count)
            ]
            for i in range(half)
        ]
        stores = []
        for i in range(half):
            total = None
            for p in range(count):
                loads[i][p].wait()
                value = held[p, i].astype(F32)
                total = value if total is None else total + value
            result[i] = total.astype(BF)
            stores.append(begin(result.at[i], outgoing.at[i], o_sem.at[i]))
        for copy in stores:
            copy.wait()

    return pl.pallas_call(
        body,
        out_shape=jax.ShapeDtypeStruct((half,) + block, BF),
        in_specs=[ANY] * (len(arrays) + len(gates)),
        out_specs=ANY,
        scratch_shapes=[
            pltpu.VMEM((count, half) + block, BF),
            pltpu.VMEM((half,) + block, BF),
            DMA((count, half)),
            DMA((half,)),
        ],
        compiler_params=pltpu.CompilerParams(vmem_limit_bytes=VMEM_LIMIT),
        cost_estimate=pl.CostEstimate(flops=1000, bytes_accessed=1000, transcendentals=0),
        name="halve",
    )(*arrays, *gates)


def blocks_of(array):
    return [(array, at) for at in range(array.shape[0])]


def own_sum(parts):
    return sum(array[at].astype(F32) for ((array, at),) in parts)


LINKS = {
    "down": (BIT_X, BIT_NEAR, BIT_FAR),
    "gate": (BIT_NEAR, BIT_X, BIT_FAR),
    "rise": (BIT_X, BIT_NEAR, BIT_FAR),
    "attn": (BIT_X, BIT_NEAR, BIT_FAR),
}
PLAN = (
    ("local", "down"),
    ("local", "gate"),
    ("local", "rise"),
    ("attention", "attn"),
    ("local", "attn"),
    ("step", "down"),
    ("step", "gate"),
    ("step", "rise"),
    ("step", "down"),
    ("step", "rise"),
    ("step", "attn"),
    ("step", "gate"),
    ("step", "attn"),
)


def reduce_shares(ids, lefts, hidden, gates_ups, attention_first, second_half):
    parts, last = {}, []
    order = {}

    def local(name, pairs, rows, bits, norms=None, turned=False):
        order[name] = list(bits)
        sent, kept = weight_grad(ids, pairs, rows, bits, last, norms, turned)
        parts[name] = [blocks_of(kept), blocks_of(exchange(sent, order[name].pop(0)))]
        last[:] = [sent]

    def step(name):
        sent = halve(parts[name], last)
        parts[name] = [part[sent.shape[0] :] for part in parts[name]]
        parts[name].append(blocks_of(exchange(sent, order[name].pop(0))))
        last[:] = [sent]

    inputs, context, h1 = ((lefts, slice(D * k, D * (k + 1))) for k in range(3))
    hidden_pairs = {
        "down": [((hidden, slice(0, FF)), (hidden, slice(FF, FF + D)))],
        "gate": [(h1, (gates_ups[0], slice(0, FF)))],
        "rise": [(h1, (gates_ups[1], slice(0, FF)))],
    }
    for action, name in PLAN:
        if action == "step":
            step(name)
        elif action == "attention":
            attention_second, input_grads, _ = second_half(
                last + [other[0] for _, other in attention_first]
            )
            last[:] = [attention_second[0]]
            q_grads, v_grads = (
                [own, (array, None), other, (exchange(array, BIT_CORE), None)]
                for (own, other), array in zip(attention_first, attention_second)
            )
        elif name == "attn":
            pairs = [
                (inputs, (q_grads, slice(0, 2 * D))),
                (inputs, (v_grads, slice(0, D))),
                (context, (v_grads, slice(D, 2 * D))),
            ]
            local(name, pairs, ROWS, LINKS[name], (hidden, slice(FF + D, FF + D + 48)))
        else:
            rows = 4 * ROWS if name == "down" else ROWS
            local(name, hidden_pairs[name], rows, LINKS[name], turned=name == "down")
    down, gate, rise, attn = (own_sum(parts[name]) for name in ("down", "gate", "rise", "attn"))
    norm = attn[:, 4 * D : 4 * D + 4].T
    shares = (
        attn[:, : 3 * D],
        attn[:, 3 * D : 4 * D],
        jnp.concatenate([gate, rise], axis=1),
        down,
        norm[:2],
        norm[2:],
    )
    return shares, input_grads


def packed_shares(rows, left, hidden, gates, ups, attention):
    def product(lefts, rights, dims=NN):
        lefts = jnp.concatenate(lefts, axis=1)
        rights = jnp.concatenate(rights, axis=1 if dims == NT else 0)
        return matmul(lefts, rights, dims).astype(BF)

    def cut(arrays, start, stop):
        return [array[start:stop] for array in arrays]

    left = list(left)
    down = product(cut(hidden, 0, FF), cut(hidden, FF, FF + D), NT).reshape(D // rows, 4, rows, D)
    norm_sum = sum(array[FF + D :].astype(F32) for array in hidden)
    norm_sum = norm_sum.reshape(3, 16, SEQ)[:, :4].transpose(1, 0, 2).reshape(4, D).T.astype(BF)
    attention = [jnp.concatenate(pair, axis=1) for pair in attention]
    summed = [
        product(cut(left, 0, D), [array[:, : 3 * D] for array in attention]),
        product(cut(left, D, 2 * D), [array[:, 3 * D :] for array in attention]),
        product(cut(left, 2 * D, 3 * D), gates),
        product(cut(left, 2 * D, 3 * D), ups),
        down.transpose(0, 2, 1, 3).reshape(D, FF),
        jnp.pad(norm_sum, ((0, 0), (0, 128 - 4))),
    ]
    summed = jnp.concatenate(summed, axis=1)
    share = lax.psum_scatter(summed, "dp", scatter_dimension=0, tiled=True).astype(F32)
    down = share[:, COL_DOWN:COL_NORM].reshape(rows, 4, D).transpose(1, 0, 2)
    norm = share[:, COL_NORM : COL_NORM + 4].T
    return (
        share[:, :COL_OUT],
        share[:, COL_OUT:COL_GU],
        share[:, COL_GU:COL_DOWN],
        down.reshape(4 * rows, D),
        norm[:2],
        norm[2:],
    )


def shards(tokens, lengths, w_qkv, w_out, w_gate_up, w_down, norm_gain, norm_bias, cotangent):
    rows = w_qkv.shape[1]
    direct = rows == ROWS
    section = lax.axis_index("section")
    ids = jnp.stack([section, lax.axis_index("dp")]).astype(jnp.int32)
    packed = pack(
        *(w[0].astype(BF) for w in (w_qkv, w_out, w_gate_up, w_down, norm_gain, norm_bias))
    )
    wide = lax.all_gather(packed, "dp", axis=0, tiled=True)
    if direct:
        down = wide.reshape(D // rows, rows, WIDE)
    else:
        down = wide[:, COL_DOWN:COL_NORM].reshape(D // rows, rows, 4, D)
        down = down.transpose(0, 2, 1, 3).reshape(FF // (4 * ROWS), 4, ROWS, D)
    norms = wide[:, COL_NORM : COL_NORM + 8].astype(F32).T

    def hop(rows_sent, pair):
        return lax.ppermute(rows_sent, "section", [pair])

    def forward(owner, micro, given, before):
        return forward_call(
            owner, micro, direct, ids, lengths, given, wide, down, norms, before
        )

    *kept, sent = forward(0, 0, tokens, [None] * len(FORWARD_KEPT))
    arrived_first = hop(sent, (0, 1))
    *kept, sent = forward(0, 1, tokens, kept)
    arrived_second = hop(sent, (0, 1))
    *kept, sent = forward(1, 0, arrived_first, kept)
    *kept, sent = forward(1, 1, arrived_second, kept)
    left, qkv, probs, n1, h1, n2, inv, layer_out = kept
    stash = (qkv, probs, n1, h1, n2, inv)

    def backward(owner, micro, given, before, gates=()):
        return backward_call(
            owner, micro, direct, ids, given, wide, down, norms, stash, before, gates
        )

    def both(array):
        return [(array, None), (exchange(array, BIT_CORE), None)]

    left_other = exchange(left, BIT_CORE) if direct else left
    *first, input_grads, sent = backward(1, 0, cotangent, [None] * 6)
    arrived_first = hop(sent, (1, 0))
    gates = (left_other,) if direct else ()
    *second, input_grads, sent = backward(
        1, 1, cotangent, [None] * 5 + [input_grads], gates
    )
    arrived_second = hop(sent, (1, 0))
    *first, input_grads, sent = backward(0, 0, arrived_first, first + [input_grads])
    if direct:
        first = [both(array) for array in first]
    *hidden, half = first_half_call(
        0, 1, direct, ids, arrived_second, wide, down, norms, (n1, h1, n2, inv), second[:3], ()
    )

    def second_half(gates):
        before = second[3:] + [input_grads]
        *made, input_sum, _ = second_half_call(
            0, 1, ids, half, wide, (qkv, probs), before, gates
        )
        return made, input_sum, None

    if direct:
        lefts = [(left, 0), (left, 1), (left_other, 0), (left_other, 1)]

        def paired(k):
            own, other = zip(first[k], both(hidden[k]))
            return list(own) + list(other)

        shares, input_grads = reduce_shares(
            ids,
            lefts,
            paired(0),
            [paired(1), paired(2)],
            [[first[3][0], first[3][1]], [first[4][0], first[4][1]]],
            second_half,
        )
    else:
        attention, input_grads, _ = second_half(())
        pairs = [first[3:5], attention]
        shares = packed_shares(
            rows, left, [first[0], hidden[0]], [first[1], hidden[1]], [first[2], hidden[2]], pairs
        )
    return (layer_out[None], input_grads[None]) + tuple(share[None] for share in shares)


def solution(mesh):
    return jax.shard_map(
        shards,
        mesh=mesh,
        in_specs=(
            P(None, "dp", None),
            P(),
            P("section", "dp", None),
            P("section", "dp", None),
            P("section", "dp", None),
            P("section", "dp", None),
            P("section", None, "dp"),
            P("section", None, "dp"),
            P(None, "dp", None),
        ),
        out_specs=(
            P("section", None, "dp", None),
            P("section", None, "dp", None),
            P("section", "dp", None),
            P("section", "dp", None),
            P("section", "dp", None),
            P("section", "dp", None),
            P("section", None, "dp"),
            P("section", None, "dp"),
        ),
        check_vma=False,
    )
```

```python
import functools

import jax
import jax.numpy as jnp
from jax import lax
from jax.experimental import pallas as pl
from jax.experimental.pallas import tpu as pltpu
from jax.sharding import PartitionSpec as P

D = 768
HEADS = 12
HEAD = 64
FF = 3072
SEQ = 256
MICRO = 2
TOKENS = 2 * MICRO * SEQ
EPSILON = 1e-05
FAR = 1e30
INV_SQRT_2PI = 0.3989422804014327
ROOT_HALF = 2.0 ** (-0.5)

COL_OUT = 3 * D
COL_GU = 4 * D
COL_DOWN = COL_GU + 2 * FF
COL_NORM = COL_DOWN + FF
WIDE = COL_NORM + 128

CHUNK = 768
CHUNKS = FF // CHUNK
ROWS = 48
BF = jnp.bfloat16
F32 = jnp.float32
NN = (((1,), (0,)), ((), ()))
NT = (((1,), (1,)), ((), ()))
TN = (((0,), (0,)), ((), ()))
SLOPES = [2.0 ** (-8.0 * (h + 1) / HEADS) for h in range(HEADS)]

VMEM_LIMIT = 64 << 20
ANY = pl.BlockSpec(memory_space=pl.ANY)
SMEM = pl.BlockSpec(memory_space=pltpu.SMEM)


def matmul(left, right, dims=NN):
    return lax.dot_general(left, right, dims, preferred_element_type=F32)


def begin(source, target, semaphore):
    copy = pltpu.make_async_copy(source, target, semaphore)
    copy.start()
    return copy


PACE = 9_200_000_000


def cost_of(microseconds):
    return pl.CostEstimate(
        flops=microseconds * PACE, bytes_accessed=microseconds * PACE // 200, transcendentals=0
    )


def own_window(given, micro):
    return given if len(given.shape) == 2 else given.at[micro]


def row_mean(values):
    return jnp.mean(values, axis=-1, keepdims=True)


def norm_forward(values, gain, bias):
    center = values - row_mean(values)
    inverse = lax.rsqrt(row_mean(center * center) + EPSILON)
    normed = center * inverse
    return normed * gain + bias, normed, inverse


def norm_backward(upstream, normed, inverse, gain):
    scaled = upstream * gain
    return inverse * (scaled - row_mean(scaled) - normed * row_mean(scaled * normed))


def forward_window(
    ids, lengths, given, wide, down, norms,
    left_out, qkv_out, probs_out, n1_out, h1_out, n2_out, inv_out, layer_out, hop_out,
    w_qkv, w_out, w_gu, w_down, x, qkv, probs, context, n1, h1, n2, inv, result, norm, left,
    w_sem, o_sem, i_sem, *, micro, direct,
):
    window = ids[1]
    copies = {}
    copies["x"] = begin(own_window(given, micro), x, i_sem.at[0])
    for k in range(3):
        cols = pl.ds(D * k, D)
        copies["qkv", k] = begin(wide.at[:, cols], w_qkv.at[:, cols], w_sem.at[k])
    copies["norm"] = begin(norms, norm, i_sem.at[1])

    def fetch_down(j, base):
        owners = down.at[pl.ds(4 * j, 4)]
        for q in range(4):
            source = owners.at[:, :, pl.ds(COL_DOWN + D * q, D)] if direct else owners.at[:, q]
            copies["down", j, q] = begin(
                source, w_down.at[j, :, q], w_sem.at[base + 4 * j + q]
            )

    def fetch_chunk(j):
        gate = wide.at[:, pl.ds(COL_GU + j * CHUNK, CHUNK)]
        rise = wide.at[:, pl.ds(COL_GU + FF + j * CHUNK, CHUNK)]
        copies["gate", j] = begin(gate, w_gu.at[j], w_sem.at[4 + j])
        copies["up", j] = begin(rise, w_gu.at[CHUNKS + j], w_sem.at[4 + CHUNKS + j])
        fetch_down(j, 4 + 2 * CHUNKS)

    flushed = []

    def flush(source, target):
        flushed.append(begin(source, target, o_sem.at[len(flushed)]))

    row_place = lax.broadcasted_iota(jnp.int32, (SEQ, SEQ), 0)
    key_place = lax.broadcasted_iota(jnp.int32, (SEQ, SEQ), 1)
    distance = jnp.abs(row_place - key_place).astype(F32)
    distance = jnp.where(key_place < lengths[micro, window], distance, FAR)
    lane = lax.broadcasted_iota(jnp.int32, (SEQ, 128), 1)
    first = lane < HEAD
    copies["x"].wait()
    rows_in = x[...]


    def flush_turned(part, values):
        rows = pl.ds(D * part, D)
        left[rows] = values.T
        flush(left.at[rows], left_out.at[rows])

    flush_turned(0, rows_in)
    for k in range(3):
        copies["qkv", k].wait()
        if k == 1:
            copies["out"] = begin(wide.at[:, pl.ds(COL_OUT, D)], w_out, w_sem.at[3])
            fetch_chunk(0)
        if k == 2:
            for j in range(1, CHUNKS):
                fetch_chunk(j)
        cols = pl.ds(D * k, D)
        qkv[:, cols] = matmul(rows_in, w_qkv[:, cols]).astype(BF)
    flush(qkv, qkv_out)
    for pair in range(HEADS // 2):
        query = qkv[:, pl.ds(128 * pair, 128)] * jnp.asarray(HEAD ** (-0.5), BF)
        key = qkv[:, pl.ds(D + 128 * pair, 128)]
        value = qkv[:, pl.ds(2 * D + 128 * pair, 128)]
        total = None
        for side in range(2):
            head = 2 * pair + side
            keep = first if side == 0 else ~first
            own_query = jnp.where(keep, query, jnp.zeros_like(query))
            own_value = jnp.where(keep, value, jnp.zeros_like(value))
            scores = matmul(own_query, key, NT) - distance * SLOPES[head]
            peak = jnp.max(scores, axis=-1, keepdims=True)
            grown = jnp.exp(scores - peak)
            share = 1.0 / jnp.sum(grown, axis=-1, keepdims=True)
            low_probs = (grown * share).astype(BF)
            probs[head] = low_probs
            mixed = matmul(low_probs, own_value)
            total = mixed if total is None else total + mixed
        context[:, pl.ds(128 * pair, 128)] = total.astype(BF)
    flush(probs, probs_out)
    flush_turned(1, context[...])
    copies["out"].wait()
    copies["norm"].wait()
    summed = rows_in.astype(F32) + matmul(context[...], w_out[...])
    hidden, normed, inverse_one = norm_forward(summed, norm[0:1, :], norm[2:3, :])
    n1[...] = normed
    flush(n1, n1_out)
    low_hidden = hidden.astype(BF)
    h1[...] = low_hidden
    flush(h1, h1_out)
    flush_turned(2, low_hidden)
    for j in range(CHUNKS):
        copies["gate", j].wait()
        copies["up", j].wait()
        gate = matmul(low_hidden, w_gu[j])
        rise = matmul(low_hidden, w_gu[CHUNKS + j])
        gated = (gate * (0.5 * (1.0 + lax.erf(gate * ROOT_HALF))) * rise).astype(BF)
        for q in range(4):
            copies["down", j, q].wait()
        hidden = hidden + matmul(gated, w_down[j].reshape(CHUNK, D))
    final, normed, inverse_two = norm_forward(hidden, norm[1:2, :], norm[3:4, :])
    result[...] = final.astype(BF)
    flush(result, hop_out)
    flush(result, layer_out)
    n2[...] = normed
    flush(n2, n2_out)
    inv[...] = jnp.where(first, inverse_one, inverse_two)
    flush(inv, inv_out)
    for copy in flushed:
        copy.wait()


def backward_hidden(
    ids, given, wide, down, norms, n1_in, h1_in, n2_in, inv_in, hidden_out, gate_out, up_out,
    w_gu, w_down, upstream, n1, h1, n2, inv, norm, gated, down_grad, gu_grad, norm_grad,
    low_norm, w_sem, o_sem, i_sem, *, micro, direct, ahead,
):
    arriving = begin(own_window(given, micro), upstream, i_sem.at[0])
    normed_two = begin(n2_in.at[micro], n2, i_sem.at[1])
    inverses = begin(inv_in.at[micro], inv, i_sem.at[2])
    gains = begin(norms, norm, i_sem.at[3])
    hidden = begin(h1_in.at[micro], h1, i_sem.at[4])
    copies = {}

    def fetch_down(j, base):
        owners = down.at[pl.ds(4 * j, 4)]
        for q in range(4):
            source = owners.at[:, :, pl.ds(COL_DOWN + D * q, D)] if direct else owners.at[:, q]
            copies["down", j, q] = begin(
                source, w_down.at[j, :, q], w_sem.at[base + 4 * j + q]
            )

    def fetch_chunk(j):
        gate = wide.at[:, pl.ds(COL_GU + j * CHUNK, CHUNK)]
        rise = wide.at[:, pl.ds(COL_GU + FF + j * CHUNK, CHUNK)]
        copies["gate", j] = begin(gate, w_gu.at[j], w_sem.at[j])
        copies["up", j] = begin(rise, w_gu.at[CHUNKS + j], w_sem.at[CHUNKS + j])
        fetch_down(j, 2 * CHUNKS)

    fetch_chunk(0)
    flushed = []

    def flush(source, target):
        flushed.append(begin(source, target, o_sem.at[len(flushed)]))

    arriving.wait()
    normed_two.wait()
    inverses.wait()
    gains.wait()
    up = upstream[...].astype(F32)
    normed = n2[...]
    grad_two = norm_backward(up, normed, inv[:, HEAD : HEAD + 1], norm[1:2, :])
    norm_grad[...] = jnp.zeros_like(norm_grad)
    norm_grad[1:2, :] = jnp.sum(up * normed, axis=0, keepdims=True)
    norm_grad[3:4, :] = jnp.sum(up, axis=0, keepdims=True)
    low_grad = grad_two.astype(BF)
    down_grad[...] = low_grad.T
    flush(down_grad, hidden_out.at[pl.ds(FF, D)])
    hidden.wait()
    low_hidden = h1[...]
    total = grad_two
    for j in range(CHUNKS):
        copies["gate", j].wait()
        copies["up", j].wait()
        if j + 1 < CHUNKS:
            fetch_chunk(j + 1)
        else:
            first_norm = begin(n1_in.at[micro], n1, i_sem.at[5])
            ahead()
        gate = matmul(low_hidden, w_gu[j])
        rise = matmul(low_hidden, w_gu[CHUNKS + j])
        for q in range(4):
            copies["down", j, q].wait()
        gated_grad = matmul(low_grad, w_down[j].reshape(CHUNK, D), NT)
        cdf = 0.5 * (1.0 + lax.erf(gate * ROOT_HALF))
        density = jnp.exp(-0.5 * gate * gate) * INV_SQRT_2PI
        bent = gate * cdf
        cols = pl.ds(j * CHUNK, CHUNK)
        late_cols = pl.ds(FF + j * CHUNK, CHUNK)
        gated[cols] = (bent * rise).astype(BF).T
        flush(gated.at[cols], hidden_out.at[cols])
        gate_grad = (gated_grad * rise * (cdf + gate * density)).astype(BF)
        rise_grad = (gated_grad * bent).astype(BF)
        gu_grad[:, cols] = gate_grad
        gu_grad[:, late_cols] = rise_grad
        flush(gu_grad.at[:, cols], gate_out.at[:, cols])
        flush(gu_grad.at[:, late_cols], up_out.at[:, cols])
        total = total + matmul(gate_grad, w_gu[j], NT) + matmul(rise_grad, w_gu[CHUNKS + j], NT)
    first_norm.wait()
    normed = n1[...]
    grad_one = norm_backward(total, normed, inv[:, 0:1], norm[0:1, :])
    norm_grad[0:1, :] = jnp.sum(total * normed, axis=0, keepdims=True)
    norm_grad[2:3, :] = jnp.sum(total, axis=0, keepdims=True)
    low_norm[...] = norm_grad[...].astype(BF)
    for k in range(3):
        source = low_norm.at[:, pl.ds(SEQ * k, SEQ)]
        flush(source, hidden_out.at[pl.ds(FF + D + 16 * k, 16)])
    return grad_one, flushed


def fetch_attention(wide, qkv_in, probs_in, w_qkv, w_out, qkv, probs, w_sem, i_sem, micro):
    copies = [
        begin(wide.at[:, pl.ds(COL_OUT, D)], w_out, w_sem.at[0]),
        begin(probs_in.at[micro], probs, i_sem.at[0]),
        begin(qkv_in.at[micro], qkv, i_sem.at[1]),
    ]
    for k in range(3):
        cols = pl.ds(D * k, D)
        copies.append(begin(wide.at[:, cols], w_qkv.at[:, cols], w_sem.at[1 + k]))
    return copies


def backward_attention(
    grad_one, copies, qk_out, vc_out, grad_out, hop_out,
    w_qkv, w_out, qkv, probs, attn_grad, context_grad, qkv_grad, grad, result,
    o_sem, *, micro,
):
    flushed = []

    def flush(source, target):
        flushed.append(begin(source, target, o_sem.at[len(flushed)]))

    low_attn = grad_one.astype(BF)
    attn_grad[...] = low_attn
    flush(attn_grad, vc_out.at[:, pl.ds(D, D)])
    copies[0].wait()
    context_grad[...] = matmul(low_attn, w_out[...], NT).astype(BF)
    copies[1].wait()
    copies[2].wait()
    first = lax.broadcasted_iota(jnp.int32, (SEQ, 128), 1) < HEAD
    root = jnp.asarray(HEAD ** (-0.5), BF)
    for pair in range(HEADS // 2):
        query = qkv[:, pl.ds(128 * pair, 128)] * root
        key = qkv[:, pl.ds(D + 128 * pair, 128)]
        value = qkv[:, pl.ds(2 * D + 128 * pair, 128)]
        upper = context_grad[:, pl.ds(128 * pair, 128)]
        query_across = query.T
        upper_across = upper.T
        query_sum, key_parts, value_parts = None, [], []
        for side in range(2):
            keep = first if side == 0 else ~first
            own_upper = jnp.where(keep, upper, jnp.zeros_like(upper))
            own_key = jnp.where(keep, key * root, jnp.zeros_like(key))
            low_probs = probs[2 * pair + side]
            wide_probs = low_probs.astype(F32)
            weighted = wide_probs * matmul(own_upper, value, NT)
            inner = jnp.sum(weighted, axis=-1, keepdims=True)
            score_grad = (weighted - wide_probs * inner).astype(BF)
            part = matmul(score_grad, own_key)
            query_sum = part if query_sum is None else query_sum + part
            rows = slice(HEAD * side, HEAD * (side + 1))
            key_parts.append(matmul(query_across[rows], score_grad))
            value_parts.append(matmul(upper_across[rows], low_probs))
        qkv_grad[:, pl.ds(128 * pair, 128)] = query_sum.astype(BF)
        key_grad = jnp.concatenate(key_parts, axis=0).T
        qkv_grad[:, pl.ds(D + 128 * pair, 128)] = key_grad.astype(BF)
        value_grad = jnp.concatenate(value_parts, axis=0).T
        qkv_grad[:, pl.ds(2 * D + 128 * pair, 128)] = value_grad.astype(BF)
    flush(qkv_grad.at[:, pl.ds(0, 2 * D)], qk_out)
    flush(qkv_grad.at[:, pl.ds(2 * D, D)], vc_out.at[:, pl.ds(0, D)])
    input_grad = grad_one
    for k in range(3):
        copies[3 + k].wait()
        cols = pl.ds(D * k, D)
        input_grad = input_grad + matmul(qkv_grad[:, cols], w_qkv[:, cols], NT)
    result[...] = input_grad.astype(BF)
    flush(result, hop_out)
    grad[...] = input_grad
    flush(grad, grad_out)
    return flushed


def backward_window(
    ids, given, wide, down, norms, qkv_in, probs_in, n1_in, h1_in, n2_in, inv_in,
    hidden_out, gate_out, up_out, qk_out, vc_out, grad_out, hop_out,
    w_gu, w_down, upstream, n1, h1, n2, inv, norm, gated, down_grad, gu_grad, norm_grad, low_norm,
    w_qkv, w_out, qkv, probs, attn_grad, context_grad, qkv_grad, grad, result,
    w_sem, o_sem, i_sem, *, micro, direct,
):
    copies = []

    def ahead():
        copies.extend(
            fetch_attention(
                wide, qkv_in, probs_in, w_qkv, w_out, qkv, probs,
                w_sem.at[pl.ds(6 * CHUNKS, 4)], i_sem.at[pl.ds(6, 2)], micro,
            )
        )

    grad_one, flushed = backward_hidden(
        ids, given, wide, down, norms, n1_in, h1_in, n2_in, inv_in, hidden_out, gate_out, up_out,
        w_gu, w_down, upstream, n1, h1, n2, inv, norm, gated, down_grad, gu_grad, norm_grad,
        low_norm, w_sem, o_sem, i_sem, micro=micro, direct=direct, ahead=ahead,
    )
    flushed += backward_attention(
        grad_one, copies, qk_out, vc_out, grad_out, hop_out,
        w_qkv, w_out, qkv, probs, attn_grad, context_grad, qkv_grad, grad, result,
        o_sem.at[pl.ds(HIDDEN_STORES, 5)], micro=micro,
    )
    for copy in flushed:
        copy.wait()


def backward_first_half(
    ids, given, wide, down, norms, n1_in, h1_in, n2_in, inv_in,
    hidden_out, gate_out, up_out, half_out,
    w_gu, w_down, upstream, n1, h1, n2, inv, norm, gated, down_grad, gu_grad, norm_grad, low_norm,
    half, w_sem, o_sem, i_sem, *, micro, direct,
):
    grad_one, flushed = backward_hidden(
        ids, given, wide, down, norms, n1_in, h1_in, n2_in, inv_in, hidden_out, gate_out, up_out,
        w_gu, w_down, upstream, n1, h1, n2, inv, norm, gated, down_grad, gu_grad, norm_grad,
        low_norm, w_sem, o_sem, i_sem, micro=micro, direct=direct, ahead=lambda: None,
    )
    half[...] = grad_one
    flushed.append(begin(half, half_out, o_sem.at[HIDDEN_STORES]))
    for copy in flushed:
        copy.wait()


def backward_second_half(
    ids, given, wide, qkv_in, probs_in,
    qk_out, vc_out, grad_out, hop_out,
    half, w_qkv, w_out, qkv, probs, attn_grad, context_grad, qkv_grad, grad, result,
    w_sem, o_sem, i_sem, *, micro,
):
    arriving = begin(given, half, i_sem.at[2])
    copies = fetch_attention(
        wide, qkv_in, probs_in, w_qkv, w_out, qkv, probs, w_sem, i_sem, micro
    )
    arriving.wait()
    flushed = backward_attention(
        half[...], copies, qk_out, vc_out, grad_out, hop_out,
        w_qkv, w_out, qkv, probs, attn_grad, context_grad, qkv_grad, grad, result,
        o_sem, micro=micro,
    )
    for copy in flushed:
        copy.wait()


FORWARD_KEPT = (
    (True, 3 * D, SEQ, BF),
    (True, SEQ, 3 * D, BF),
    (True, HEADS, SEQ, SEQ, BF),
    (True, SEQ, D, F32),
    (True, SEQ, D, BF),
    (True, SEQ, D, F32),
    (True, SEQ, 128, F32),
    (True, SEQ, D, BF),
)
HIDDEN_KEPT = ((False, FF + D + 48, SEQ, BF), (False, SEQ, FF, BF), (False, SEQ, FF, BF))
ATTENTION_KEPT = ((False, SEQ, 2 * D, BF), (False, SEQ, 2 * D, BF), (True, SEQ, D, F32))
HIDDEN_STORES = 3 * CHUNKS + 4
HIDDEN_WEIGHTS = (
    pltpu.VMEM((2 * CHUNKS, D, CHUNK), BF),
    pltpu.VMEM((CHUNKS, 4, 4, ROWS, D), BF),
)
ATTENTION_WEIGHTS = (pltpu.VMEM((D, 3 * D), BF), pltpu.VMEM((D, D), BF))
HIDDEN_SCRATCH = HIDDEN_WEIGHTS + (
    pltpu.VMEM((SEQ, D), BF),
    pltpu.VMEM((SEQ, D), F32),
    pltpu.VMEM((SEQ, D), BF),
    pltpu.VMEM((SEQ, D), F32),
    pltpu.VMEM((SEQ, 128), F32),
    pltpu.VMEM((8, D), F32),
    pltpu.VMEM((FF, SEQ), BF),
    pltpu.VMEM((D, SEQ), BF),
    pltpu.VMEM((SEQ, 2 * FF), BF),
    pltpu.VMEM((16, D), F32),
    pltpu.VMEM((16, D), BF),
)
ATTENTION_SCRATCH = ATTENTION_WEIGHTS + (
    pltpu.VMEM((SEQ, 3 * D), BF),
    pltpu.VMEM((HEADS, SEQ, SEQ), BF),
    pltpu.VMEM((SEQ, D), BF),
    pltpu.VMEM((SEQ, D), BF),
    pltpu.VMEM((SEQ, 3 * D), BF),
    pltpu.VMEM((SEQ, D), F32),
    pltpu.VMEM((SEQ, D), BF),
)
DMA = pltpu.SemaphoreType.DMA


def call_window(
    body, name, owner, micro, inputs, kept_shapes, sent, before, scratch, flops, small, gates=()
):
    count = len(kept_shapes)
    operands = tuple(inputs)
    aliases = {}
    for position, array in enumerate(before):
        if array is not None:
            aliases[len(operands)] = position
            operands += (array,)
    operands += tuple(gates)
    shapes = [
        jax.ShapeDtypeStruct((MICRO,) * shared + tuple(shape), dtype)
        for shared, *shape, dtype in kept_shapes
    ]
    shapes.append(jax.ShapeDtypeStruct((SEQ, D), sent))

    def kernel(*refs):
        @pl.when(refs[0][0] == owner)
        def _():
            outs = refs[len(operands) : len(operands) + count]
            views = [
                ref.at[micro] if shared else ref
                for ref, (shared, *_) in zip(outs, kept_shapes)
            ]
            body(*refs[: len(inputs)], *views, *refs[len(operands) + count :])

    return pl.pallas_call(
        kernel,
        out_shape=shapes,
        in_specs=[SMEM] * small + [ANY] * (len(operands) - small),
        out_specs=[ANY] * len(shapes),
        input_output_aliases=aliases,
        scratch_shapes=list(scratch),
        compiler_params=pltpu.CompilerParams(vmem_limit_bytes=VMEM_LIMIT),
        cost_estimate=pl.CostEstimate(
            flops=flops, bytes_accessed=flops // 200, transcendentals=flops // 4000
        ),
        name=name,
    )(*operands)


def forward_call(owner, micro, direct, ids, lengths, given, wide, down, norms, before):
    scratch = (
        ATTENTION_WEIGHTS
        + HIDDEN_WEIGHTS
        + (
            pltpu.VMEM((SEQ, D), BF),
            pltpu.VMEM((SEQ, 3 * D), BF),
            pltpu.VMEM((HEADS, SEQ, SEQ), BF),
            pltpu.VMEM((SEQ, D), BF),
            pltpu.VMEM((SEQ, D), F32),
            pltpu.VMEM((SEQ, D), BF),
            pltpu.VMEM((SEQ, D), F32),
            pltpu.VMEM((SEQ, 128), F32),
            pltpu.VMEM((SEQ, D), BF),
            pltpu.VMEM((8, D), F32),
            pltpu.VMEM((3 * D, SEQ), BF),
            DMA((4 + 6 * CHUNKS,)),
            DMA((12,)),
            DMA((2,)),
        )
    )
    return call_window(
        functools.partial(forward_window, micro=micro, direct=direct),
        "layer_forward",
        owner,
        micro,
        (ids, lengths, given, wide, down, norms),
        FORWARD_KEPT,
        BF,
        before,
        scratch,
        5_000_000_000,
        2,
    )


def backward_call(owner, micro, direct, ids, given, wide, down, norms, stash, before, gates):
    return call_window(
        functools.partial(backward_window, micro=micro, direct=direct),
        "layer_backward",
        owner,
        micro,
        (ids, given, wide, down, norms) + tuple(stash),
        HIDDEN_KEPT + ATTENTION_KEPT,
        BF,
        before,
        HIDDEN_SCRATCH
        + ATTENTION_SCRATCH
        + (DMA((4 + 6 * CHUNKS,)), DMA((HIDDEN_STORES + 5,)), DMA((8,))),
        8_000_000_000,
        1,
        gates,
    )


def first_half_call(
    owner, micro, direct, ids, given, wide, down, norms, stash, before, gates
):
    return call_window(
        functools.partial(backward_first_half, micro=micro, direct=direct),
        "backward_hidden",
        owner,
        micro,
        (ids, given, wide, down, norms) + tuple(stash),
        HIDDEN_KEPT,
        F32,
        before,
        HIDDEN_SCRATCH
        + (
            pltpu.VMEM((SEQ, D), F32),
            DMA((6 * CHUNKS,)),
            DMA((HIDDEN_STORES + 1,)),
            DMA((6,)),
        ),
        60_000_000_000,
        1,
        gates,
    )


def second_half_call(owner, micro, ids, given, wide, stash, before, gates):
    return call_window(
        functools.partial(backward_second_half, micro=micro),
        "backward_attention",
        owner,
        micro,
        (ids, given, wide) + tuple(stash),
        ATTENTION_KEPT,
        BF,
        before,
        (pltpu.VMEM((SEQ, D), F32),) + ATTENTION_SCRATCH + (DMA((4,)), DMA((5,)), DMA((3,))),
        10 * PACE,
        1,
        gates,
    )


def pack(w_qkv, w_out, w_gate_up, w_down, norm_gain, norm_bias):
    rows = w_qkv.shape[0]
    split_down = w_down.reshape(4, rows, D).transpose(1, 0, 2).reshape(rows, FF)
    norms = jnp.concatenate([norm_gain, norm_bias], axis=0).T
    norms = jnp.pad(norms, ((0, 0), (0, 128 - 4)))
    return jnp.concatenate([w_qkv, w_out, w_gate_up, split_down, norms], axis=1)


BIT_CORE, BIT_X, BIT_NEAR, BIT_FAR = 1, 2, 4, 8


def weight_grad_kernel(ids, terms, norm_ins, sent, kept, scratch, *, rows, order, turned):
    buffers, result, i_sem, o_sem = scratch[:4]
    columns, pieces, count = 0, [], 0

    def fetch(source, target):
        nonlocal count
        count += 1
        return begin(source, target, i_sem.at[count - 1])

    owned = []
    for place in range(8):
        relative = sum(bit for k, bit in enumerate(order) if not (place >> (2 - k)) & 1)
        owned.append(ids[1] ^ relative)
    for term, (lefts, rights) in enumerate(terms):
        left_buffer, right_buffer = buffers[term]
        whole = []
        for k, left in enumerate(lefts):
            for place in range(8):
                source = left.at[pl.ds(pl.multiple_of(owned[place] * rows, 16), rows)]
                target = left_buffer.at[place, :, pl.ds(SEQ * k, SEQ)]
                whole.append(fetch(source, target))
        for start in range(0, D if turned else right_buffer.shape[1], D):
            cols = pl.ds(start, D)
            parts = []
            for k, right in enumerate(rights):
                tokens = pl.ds(SEQ * k, SEQ)
                if turned:
                    parts.append(fetch(right, right_buffer.at[:, tokens]))
                else:
                    parts.append(fetch(right.at[:, cols], right_buffer.at[tokens, cols]))
            pieces.append((term, start, whole, parts, columns))
            columns += D
            whole = []
    if norm_ins:
        norm_buffer, norm_turned, norm_sem = scratch[4:]
        norm_loads = [
            begin(source.at[pl.ds(16 * k, 16)], norm_buffer.at[n, :, pl.ds(SEQ * k, SEQ)], norm_sem.at[n, k])
            for n, source in enumerate(norm_ins)
            for k in range(3)
        ]
    stores = []

    def store(first, count, cols):
        target = sent if first < 4 else kept
        source = result.at[pl.ds(first, count), :, cols]
        place = target.at[pl.ds(first % 4, count), :, cols]
        stores.append(begin(source, place, o_sem.at[len(stores)]))

    group = 192 // rows
    for term, start, whole, parts, column in pieces:
        left_buffer, right_buffer = buffers[term]
        for load in whole + parts:
            load.wait()
        values = right_buffer[...] if turned else right_buffer[:, pl.ds(start, D)]
        cols = pl.ds(column, D)
        for first in range(0, 8, 2 * group):
            taken = left_buffer[pl.ds(first, 2 * group)].reshape(2 * group * rows, TOKENS)
            value = matmul(taken, values, NT if turned else NN).astype(BF)
            result[pl.ds(first, 2 * group), :, cols] = value.reshape(2 * group, rows, D)
            for half in range(2):
                store(first + group * half, group, cols)
    if norm_ins:
        for load in norm_loads:
            load.wait()
        total = sum(norm_buffer[n].astype(F32) for n in range(4))
        total = jnp.concatenate([total, jnp.zeros((112, D), F32)], axis=0).T.astype(BF)
        norm_turned[...] = total.reshape(16, rows, 128)
        cols = pl.ds(columns, 128)
        for place in range(8):
            result[place, :, cols] = norm_turned[owned[place]]
        store(0, 4, cols)
        store(4, 4, cols)
    for copy in stores:
        copy.wait()


def weight_grad(ids, pairs, rows, order, gates, norms=None, turned=False):
    width = 0
    arrays, scratch = [], []

    def position(array):
        for k, known in enumerate(arrays):
            if known is array:
                return k
        arrays.append(array)
        return len(arrays) - 1

    def placed(side):
        return [(position(array), micro) for array, micro in side[0]], side[1]

    terms = [(placed(left), placed(right)) for left, right in pairs]
    norm_places = placed(norms) if norms else None
    loads, stores = 0, 0
    for _, (_, taken) in terms:
        size = taken.stop - taken.start
        shape = (size, TOKENS) if turned else (TOKENS, size)
        scratch += [pltpu.VMEM((8, rows, TOKENS), BF), pltpu.VMEM(shape, BF)]
        loads += 32 + 4 * (size // D)
        stores += 8 * (size // D)
        width += size
    total = width + 128 * bool(norms)
    shape = jax.ShapeDtypeStruct((4, rows, total), BF)
    count = 1 + len(arrays) + len(gates)

    def view(refs, place, taken, along_rows):
        index, micro = place
        ref = refs[1 + index] if micro is None else refs[1 + index].at[micro]
        span = pl.ds(taken.start, taken.stop - taken.start)
        return ref.at[span] if along_rows else ref.at[:, span]

    def body(*refs):
        sources = [
            (
                [view(refs, place, left[1], True) for place in left[0]],
                [view(refs, place, right[1], turned) for place in right[0]],
            )
            for left, right in terms
        ]
        norm_views = []
        if norms:
            norm_views = [view(refs, place, norm_places[1], True) for place in norm_places[0]]
        rest = refs[count + 2 :]
        buffers = [(rest[2 * k], rest[2 * k + 1]) for k in range(len(terms))]
        weight_grad_kernel(
            refs[0],
            sources,
            norm_views,
            refs[count],
            refs[count + 1],
            (buffers,) + tuple(rest[2 * len(terms) :]),
            rows=rows,
            order=order,
            turned=turned,
        )

    scratch += [pltpu.VMEM((8, rows, total), BF), DMA((loads,)), DMA((stores + 2,))]
    if norms:
        scratch += [pltpu.VMEM((4, 16, D), BF), pltpu.VMEM((16, rows, 128), BF), DMA((4, 3))]
    return pl.pallas_call(
        body,
        out_shape=[shape, shape],
        in_specs=[SMEM] + [ANY] * (count - 1),
        out_specs=[ANY] * 2,
        scratch_shapes=scratch,
        compiler_params=pltpu.CompilerParams(vmem_limit_bytes=VMEM_LIMIT),
        cost_estimate=cost_of(8),
        name="weight_grad",
    )(ids, *arrays, *gates)


def exchange(values, bit):
    count = lax.axis_size("dp")
    return lax.ppermute(values, "dp", [(i, i ^ bit) for i in range(count)])


def halve(parts, gates):
    half = len(parts[0]) // 2
    arrays = []
    for part in parts:
        for array, _ in part[:half]:
            if not any(array is known for known in arrays):
                arrays.append(array)
    where = [
        [next((k, at) for k, known in enumerate(arrays) if known is array) for array, at in part[:half]]
        for part in parts
    ]
    block = arrays[0].shape[1:]
    count = len(parts)

    def body(*refs):
        outgoing, held, result, i_sem, o_sem = refs[len(arrays) + len(gates) :]
        loads = [
            [
                begin(refs[where[p][i][0]].at[where[p][i][1]], held.at[p, i], i_sem.at[p, i])
                for p in range(count)
            ]
            for i in range(half)
        ]
        stores = []
        for i in range(half):
            total = None
            for p in range(count):
                loads[i][p].wait()
                value = held[p, i].astype(F32)
                total = value if total is None else total + value
            result[i] = total.astype(BF)
            stores.append(begin(result.at[i], outgoing.at[i], o_sem.at[i]))
        for copy in stores:
            copy.wait()

    return pl.pallas_call(
        body,
        out_shape=jax.ShapeDtypeStruct((half,) + block, BF),
        in_specs=[ANY] * (len(arrays) + len(gates)),
        out_specs=ANY,
        scratch_shapes=[
            pltpu.VMEM((count, half) + block, BF),
            pltpu.VMEM((half,) + block, BF),
            DMA((count, half)),
            DMA((half,)),
        ],
        compiler_params=pltpu.CompilerParams(vmem_limit_bytes=VMEM_LIMIT),
        cost_estimate=cost_of(2),
        name="halve",
    )(*arrays, *gates)


def blocks_of(array):
    return [(array, at) for at in range(array.shape[0])]


def finish(parts, gates, pieces, carried=None):
    arrays, places = [], []
    for ((array, at),) in parts:
        if not any(array is known for known in arrays):
            arrays.append(array)
        places.append((next(k for k, known in enumerate(arrays) if known is array), at))
    rows, width = arrays[0].shape[1:]
    operands = tuple(arrays) + tuple(gates) + (() if carried is None else (carried,))

    def body(*refs):
        outs = refs[len(operands) :][: len(pieces)]
        held, made, i_sem, o_sem = refs[len(operands) + len(pieces) :]
        loads = [
            begin(refs[index].at[at], held.at[k], i_sem.at[k])
            for k, (index, at) in enumerate(places)
        ]
        total = None
        for k, load in enumerate(loads):
            load.wait()
            value = held[k].astype(F32)
            total = value if total is None else total + value
        if width > 4 * D:
            norms = jnp.concatenate(
                [total[:, 4 * D :], jnp.zeros((128 - rows, 128), F32)], axis=0
            ).T
            made[:, pl.ds(0, 4 * D)] = total[:, : 4 * D]
            made[pl.ds(0, 8), pl.ds(4 * D, 128)] = norms[:8]
        else:
            made[...] = total
        stores = []
        for k, (out, (shape, start, column)) in enumerate(zip(outs, pieces)):
            count, size = min(shape[0], rows), min(shape[1], width)
            source = made.at[pl.ds(0, count), pl.ds(start, size)]
            stores.append(begin(source, out.at[:, pl.ds(column, size)], o_sem.at[k]))
        for store in stores:
            store.wait()

    return pl.pallas_call(
        body,
        out_shape=[jax.ShapeDtypeStruct(shape, F32) for shape, _, _ in pieces],
        in_specs=[ANY] * len(operands),
        out_specs=[ANY] * len(pieces),
        input_output_aliases={} if carried is None else {len(operands) - 1: 0},
        scratch_shapes=[
            pltpu.VMEM((len(parts), rows, width), BF),
            pltpu.VMEM((rows, width), F32),
            DMA((len(parts),)),
            DMA((len(pieces),)),
        ],
        compiler_params=pltpu.CompilerParams(vmem_limit_bytes=VMEM_LIMIT),
        cost_estimate=cost_of(2),
        name="finish",
    )(*operands)


LINKS = {
    "down": (BIT_X, BIT_NEAR, BIT_FAR),
    "gate": (BIT_NEAR, BIT_X, BIT_FAR),
    "rise": (BIT_X, BIT_NEAR, BIT_FAR),
    "attn": (BIT_X, BIT_NEAR, BIT_FAR),
}
PLAN = (
    ("local", "down"),
    ("local", "gate"),
    ("local", "rise"),
    ("attention", "attn"),
    ("step", "down"),
    ("local", "attn"),
    ("step", "gate"),
    ("step", "rise"),
    ("step", "down"),
    ("step", "rise"),
    ("step", "attn"),
    ("finish", "down"),
    ("step", "gate"),
    ("finish", "rise"),
    ("step", "attn"),
    ("finish", "gate"),
    ("finish", "attn"),
)


def reduce_shares(ids, lefts, hidden, gates_ups, attention_first, second_half):
    parts, last, done = {}, [], {}
    order = {}

    def local(name, pairs, rows, bits, norms=None, turned=False):
        order[name] = list(bits)
        sent, kept = weight_grad(ids, pairs, rows, bits, last, norms, turned)
        parts[name] = [blocks_of(kept), blocks_of(exchange(sent, order[name].pop(0)))]
        last[:] = [sent]

    def step(name):
        sent = halve(parts[name], last)
        parts[name] = [part[sent.shape[0] :] for part in parts[name]]
        parts[name].append(blocks_of(exchange(sent, order[name].pop(0))))
        last[:] = [sent]

    inputs, context, h1 = ((lefts, slice(D * k, D * (k + 1))) for k in range(3))
    hidden_pairs = {
        "down": [((hidden, slice(0, FF)), (hidden, slice(FF, FF + D)))],
        "gate": [(h1, (gates_ups[0], slice(0, FF)))],
        "rise": [(h1, (gates_ups[1], slice(0, FF)))],
    }
    for action, name in PLAN:
        if action == "step":
            step(name)
        elif action == "finish":
            wide = (ROWS, 2 * FF)
            pieces = {
                "down": [((4 * ROWS, D), 0, 0)],
                "gate": [(wide, 0, 0)],
                "rise": [(wide, 0, FF)],
                "attn": [((ROWS, 3 * D), 0, 0), ((ROWS, D), 3 * D, 0), ((8, 128), 4 * D, 0)],
            }
            carried = done["gate"][0] if "gate" in done and name in ("gate", "rise") else None
            made = finish(parts[name], last, pieces[name], carried)
            done["gate" if name == "rise" else name] = made
            last[:] = [made[0]] if name not in ("gate", "rise") else []
        elif action == "attention":
            attention_second, input_grads, _ = second_half(
                last + [other[0] for _, other in attention_first]
            )
            last[:] = [attention_second[0]]
            q_grads, v_grads = (
                [own, (array, None), other, (exchange(array, BIT_CORE), None)]
                for (own, other), array in zip(attention_first, attention_second)
            )
        elif name == "attn":
            pairs = [
                (inputs, (q_grads, slice(0, 2 * D))),
                (inputs, (v_grads, slice(0, D))),
                (context, (v_grads, slice(D, 2 * D))),
            ]
            local(name, pairs, ROWS, LINKS[name], (hidden, slice(FF + D, FF + D + 48)))
        else:
            rows = 4 * ROWS if name == "down" else ROWS
            local(name, hidden_pairs[name], rows, LINKS[name], turned=name == "down")
    norm = done["attn"][2][:4, :ROWS]
    shares = (
        done["attn"][0],
        done["attn"][1],
        done["gate"][0],
        done["down"][0],
        norm[:2],
        norm[2:],
    )
    return shares, input_grads


def packed_shares(rows, left, hidden, gates, ups, attention):
    def product(lefts, rights, dims=NN):
        lefts = jnp.concatenate(lefts, axis=1)
        rights = jnp.concatenate(rights, axis=1 if dims == NT else 0)
        return matmul(lefts, rights, dims).astype(BF)

    def cut(arrays, start, stop):
        return [array[start:stop] for array in arrays]

    left = list(left)
    down = product(cut(hidden, 0, FF), cut(hidden, FF, FF + D), NT).reshape(D // rows, 4, rows, D)
    norm_sum = sum(array[FF + D :].astype(F32) for array in hidden)
    norm_sum = norm_sum.reshape(3, 16, SEQ)[:, :4].transpose(1, 0, 2).reshape(4, D).T.astype(BF)
    attention = [jnp.concatenate(pair, axis=1) for pair in attention]
    summed = [
        product(cut(left, 0, D), [array[:, : 3 * D] for array in attention]),
        product(cut(left, D, 2 * D), [array[:, 3 * D :] for array in attention]),
        product(cut(left, 2 * D, 3 * D), gates),
        product(cut(left, 2 * D, 3 * D), ups),
        down.transpose(0, 2, 1, 3).reshape(D, FF),
        jnp.pad(norm_sum, ((0, 0), (0, 128 - 4))),
    ]
    summed = jnp.concatenate(summed, axis=1)
    share = lax.psum_scatter(summed, "dp", scatter_dimension=0, tiled=True).astype(F32)
    down = share[:, COL_DOWN:COL_NORM].reshape(rows, 4, D).transpose(1, 0, 2)
    norm = share[:, COL_NORM : COL_NORM + 4].T
    return (
        share[:, :COL_OUT],
        share[:, COL_OUT:COL_GU],
        share[:, COL_GU:COL_DOWN],
        down.reshape(4 * rows, D),
        norm[:2],
        norm[2:],
    )


def shards(tokens, lengths, w_qkv, w_out, w_gate_up, w_down, norm_gain, norm_bias, cotangent):
    rows = w_qkv.shape[1]
    direct = rows == ROWS
    section = lax.axis_index("section")
    ids = jnp.stack([section, lax.axis_index("dp")]).astype(jnp.int32)
    packed = pack(
        *(w[0].astype(BF) for w in (w_qkv, w_out, w_gate_up, w_down, norm_gain, norm_bias))
    )
    wide = lax.all_gather(packed, "dp", axis=0, tiled=True)
    if direct:
        down = wide.reshape(D // rows, rows, WIDE)
    else:
        down = wide[:, COL_DOWN:COL_NORM].reshape(D // rows, rows, 4, D)
        down = down.transpose(0, 2, 1, 3).reshape(FF // (4 * ROWS), 4, ROWS, D)
    norms = wide[:, COL_NORM : COL_NORM + 8].astype(F32).T

    def hop(rows_sent, pair):
        return lax.ppermute(rows_sent, "section", [pair])

    def forward(owner, micro, given, before):
        return forward_call(
            owner, micro, direct, ids, lengths, given, wide, down, norms, before
        )

    *kept, sent = forward(0, 0, tokens, [None] * len(FORWARD_KEPT))
    arrived_first = hop(sent, (0, 1))
    *kept, sent = forward(0, 1, tokens, kept)
    arrived_second = hop(sent, (0, 1))
    *kept, sent = forward(1, 0, arrived_first, kept)
    *kept, sent = forward(1, 1, arrived_second, kept)
    left, qkv, probs, n1, h1, n2, inv, layer_out = kept
    stash = (qkv, probs, n1, h1, n2, inv)

    def backward(owner, micro, given, before, gates=()):
        return backward_call(
            owner, micro, direct, ids, given, wide, down, norms, stash, before, gates
        )

    def both(array):
        return [(array, None), (exchange(array, BIT_CORE), None)]

    left_other = exchange(left, BIT_CORE) if direct else left
    *first, input_grads, sent = backward(1, 0, cotangent, [None] * 6)
    arrived_first = hop(sent, (1, 0))
    gates = (left_other,) if direct else ()
    *second, input_grads, sent = backward(
        1, 1, cotangent, [None] * 5 + [input_grads], gates
    )
    arrived_second = hop(sent, (1, 0))
    *first, input_grads, sent = backward(0, 0, arrived_first, first + [input_grads])
    if direct:
        first = [both(array) for array in first]
    *hidden, half = first_half_call(
        0, 1, direct, ids, arrived_second, wide, down, norms, (n1, h1, n2, inv), second[:3], ()
    )

    def second_half(gates):
        before = second[3:] + [input_grads]
        *made, input_sum, _ = second_half_call(
            0, 1, ids, half, wide, (qkv, probs), before, gates
        )
        return made, input_sum, None

    if direct:
        lefts = [(left, 0), (left, 1), (left_other, 0), (left_other, 1)]

        def paired(k):
            own, other = zip(first[k], both(hidden[k]))
            return list(own) + list(other)

        shares, input_grads = reduce_shares(
            ids,
            lefts,
            paired(0),
            [paired(1), paired(2)],
            [[first[3][0], first[3][1]], [first[4][0], first[4][1]]],
            second_half,
        )
    else:
        attention, input_grads, _ = second_half(())
        pairs = [first[3:5], attention]
        shares = packed_shares(
            rows, left, [first[0], hidden[0]], [first[1], hidden[1]], [first[2], hidden[2]], pairs
        )
    return (layer_out[None], input_grads[None]) + tuple(share[None] for share in shares)


def solution(mesh):
    return jax.shard_map(
        shards,
        mesh=mesh,
        in_specs=(
            P(None, "dp", None),
            P(),
            P("section", "dp", None),
            P("section", "dp", None),
            P("section", "dp", None),
            P("section", "dp", None),
            P("section", None, "dp"),
            P("section", None, "dp"),
            P(None, "dp", None),
        ),
        out_specs=(
            P("section", None, "dp", None),
            P("section", None, "dp", None),
            P("section", "dp", None),
            P("section", "dp", None),
            P("section", "dp", None),
            P("section", "dp", None),
            P("section", None, "dp"),
            P("section", None, "dp"),
        ),
        check_vma=False,
    )
```

```python
import functools

import jax
import jax.numpy as jnp
from jax import lax
from jax.experimental import pallas as pl
from jax.experimental.pallas import tpu as pltpu
from jax.sharding import PartitionSpec as P

D = 768
HEADS = 12
HEAD = 64
FF = 3072
SEQ = 256
MICRO = 2
TOKENS = 2 * MICRO * SEQ
EPSILON = 1e-05
FAR = 1e30
INV_SQRT_2PI = 0.3989422804014327
ROOT_HALF = 2.0 ** (-0.5)

COL_OUT = 3 * D
COL_GU = 4 * D
COL_DOWN = COL_GU + 2 * FF
COL_NORM = COL_DOWN + FF
WIDE = COL_NORM + 128

CHUNK = 768
CHUNKS = FF // CHUNK
ROWS = 48
BF = jnp.bfloat16
F32 = jnp.float32
NN = (((1,), (0,)), ((), ()))
NT = (((1,), (1,)), ((), ()))
TN = (((0,), (0,)), ((), ()))
SLOPES = [2.0 ** (-8.0 * (h + 1) / HEADS) for h in range(HEADS)]

VMEM_LIMIT = 64 << 20
ANY = pl.BlockSpec(memory_space=pl.ANY)
SMEM = pl.BlockSpec(memory_space=pltpu.SMEM)


def matmul(left, right, dims=NN):
    return lax.dot_general(left, right, dims, preferred_element_type=F32)


def begin(source, target, semaphore):
    copy = pltpu.make_async_copy(source, target, semaphore)
    copy.start()
    return copy


PACE = 9_200_000_000


def cost_of(microseconds):
    return pl.CostEstimate(
        flops=microseconds * PACE, bytes_accessed=microseconds * PACE // 200, transcendentals=0
    )


def own_window(given, micro):
    return given if len(given.shape) == 2 else given.at[micro]


def row_mean(values):
    return jnp.mean(values, axis=-1, keepdims=True)


def norm_forward(values, gain, bias):
    center = values - row_mean(values)
    inverse = lax.rsqrt(row_mean(center * center) + EPSILON)
    normed = center * inverse
    return normed * gain + bias, normed, inverse


def norm_backward(upstream, normed, inverse, gain):
    scaled = upstream * gain
    return inverse * (scaled - row_mean(scaled) - normed * row_mean(scaled * normed))


def forward_window(
    ids, lengths, given, wide, down,
    left_out, qkv_out, probs_out, n1_out, h1_out, n2_out, inv_out, layer_out, hop_out,
    w_qkv, w_out, w_gu, w_down, x, qkv, probs, context, n1, h1, n2, inv, result, norm, left,
    w_sem, o_sem, i_sem, *, micro, direct, fused=False,
):
    window = ids[1]
    copies = {}
    copies["x"] = begin(own_window(given, micro), x, i_sem.at[0])
    for k in range(3):
        cols = pl.ds(D * k, D)
        copies["qkv", k] = begin(wide.at[:, cols], w_qkv.at[:, cols], w_sem.at[k])
    copies["norm"] = begin(wide.at[:, pl.ds(COL_NORM, 128)], norm, i_sem.at[1])

    def fetch_down(j, base):
        owners = down.at[pl.ds(4 * j, 4)]
        for q in range(4):
            source = owners.at[:, :, pl.ds(COL_DOWN + D * q, D)] if direct else owners.at[:, q]
            copies["down", j, q] = begin(
                source, w_down.at[j, :, q], w_sem.at[base + 4 * j + q]
            )

    def fetch_chunk(j):
        gate = wide.at[:, pl.ds(COL_GU + j * CHUNK, CHUNK)]
        rise = wide.at[:, pl.ds(COL_GU + FF + j * CHUNK, CHUNK)]
        copies["gate", j] = begin(gate, w_gu.at[j], w_sem.at[4 + j])
        copies["up", j] = begin(rise, w_gu.at[CHUNKS + j], w_sem.at[4 + CHUNKS + j])
        fetch_down(j, 4 + 2 * CHUNKS)

    flushed = []

    def flush(source, target):
        if target is None:
            return
        flushed.append(begin(source, target, o_sem.at[len(flushed)]))

    row_place = lax.broadcasted_iota(jnp.int32, (SEQ, SEQ), 0)
    key_place = lax.broadcasted_iota(jnp.int32, (SEQ, SEQ), 1)
    distance = jnp.abs(row_place - key_place).astype(F32)
    distance = jnp.where(key_place < lengths[micro, window], distance, FAR)
    lane = lax.broadcasted_iota(jnp.int32, (SEQ, 128), 1)
    first = lane < HEAD
    copies["x"].wait()
    rows_in = x[...]


    def flush_turned(part, values):
        rows = pl.ds(D * part, D)
        left[rows] = values.T
        flush(left.at[rows], left_out.at[rows])

    flush_turned(0, rows_in)
    for k in range(3):
        copies["qkv", k].wait()
        if k == 1:
            copies["out"] = begin(wide.at[:, pl.ds(COL_OUT, D)], w_out, w_sem.at[3])
            fetch_chunk(0)
        if k == 2:
            for j in range(1, CHUNKS):
                fetch_chunk(j)
        cols = pl.ds(D * k, D)
        qkv[:, cols] = matmul(rows_in, w_qkv[:, cols]).astype(BF)
    flush(qkv, qkv_out)
    for pair in range(HEADS // 2):
        query = qkv[:, pl.ds(128 * pair, 128)] * jnp.asarray(HEAD ** (-0.5), BF)
        key = qkv[:, pl.ds(D + 128 * pair, 128)]
        value = qkv[:, pl.ds(2 * D + 128 * pair, 128)]
        total = None
        for side in range(2):
            head = 2 * pair + side
            keep = first if side == 0 else ~first
            own_query = jnp.where(keep, query, jnp.zeros_like(query))
            own_value = jnp.where(keep, value, jnp.zeros_like(value))
            scores = matmul(own_query, key, NT) - distance * SLOPES[head]
            peak = jnp.max(scores, axis=-1, keepdims=True)
            grown = jnp.exp(scores - peak)
            share = 1.0 / jnp.sum(grown, axis=-1, keepdims=True)
            low_probs = (grown * share).astype(BF)
            probs[head] = low_probs
            mixed = matmul(low_probs, own_value)
            total = mixed if total is None else total + mixed
        context[:, pl.ds(128 * pair, 128)] = total.astype(BF)
    flush(probs, probs_out)
    flush_turned(1, context[...])
    copies["out"].wait()
    copies["norm"].wait()
    params = norm[...].astype(F32).T
    summed = rows_in.astype(F32) + matmul(context[...], w_out[...])
    hidden, normed, inverse_one = norm_forward(summed, params[0:1], params[2:3])
    n1[...] = normed
    flush(n1, n1_out)
    low_hidden = hidden.astype(BF)
    h1[...] = low_hidden
    flush(h1, h1_out)
    flush_turned(2, low_hidden)
    for j in range(CHUNKS):
        copies["gate", j].wait()
        copies["up", j].wait()
        gate = matmul(low_hidden, w_gu[j])
        rise = matmul(low_hidden, w_gu[CHUNKS + j])
        gated = (gate * (0.5 * (1.0 + lax.erf(gate * ROOT_HALF))) * rise).astype(BF)
        for q in range(4):
            copies["down", j, q].wait()
        hidden = hidden + matmul(gated, w_down[j].reshape(CHUNK, D))
    final, normed, inverse_two = norm_forward(hidden, params[1:2], params[3:4])
    result[...] = final.astype(BF)
    flush(result, hop_out)
    flush(result, layer_out)
    n2[...] = normed
    flush(n2, n2_out)
    inv[...] = jnp.where(first, inverse_one, inverse_two)
    flush(inv, inv_out)
    if fused:
        return flushed
    for copy in flushed:
        copy.wait()


class InPlace:
    def wait(self):
        return None


def backward_hidden(
    ids, given, wide, down, n1_in, h1_in, n2_in, inv_in, hidden_out, gate_out, up_out,
    w_gu, w_down, upstream, n1, h1, n2, inv, norm, gated, down_grad, gu_grad, norm_grad,
    low_norm, w_sem, o_sem, i_sem, *, micro, direct, ahead, arriving=None,
):
    resident = arriving is not None

    def load(source, target, semaphore):
        return InPlace() if resident else begin(source, target, semaphore)

    if not resident:
        arriving = begin(own_window(given, micro), upstream, i_sem.at[0])
        normed_two = begin(n2_in.at[micro], n2, i_sem.at[1])
        inverses = begin(inv_in.at[micro], inv, i_sem.at[2])
        gains = begin(wide.at[:, pl.ds(COL_NORM, 128)], norm, i_sem.at[3])
        hidden = begin(h1_in.at[micro], h1, i_sem.at[4])
    else:
        normed_two = inverses = gains = hidden = InPlace()
    copies = {}

    def fetch_down(j, base):
        owners = down.at[pl.ds(4 * j, 4)]
        for q in range(4):
            source = owners.at[:, :, pl.ds(COL_DOWN + D * q, D)] if direct else owners.at[:, q]
            copies["down", j, q] = load(
                source, w_down.at[j, :, q], w_sem.at[base + 4 * j + q]
            )

    def fetch_chunk(j):
        gate = wide.at[:, pl.ds(COL_GU + j * CHUNK, CHUNK)]
        rise = wide.at[:, pl.ds(COL_GU + FF + j * CHUNK, CHUNK)]
        copies["gate", j] = load(gate, w_gu.at[j], w_sem.at[j])
        copies["up", j] = load(rise, w_gu.at[CHUNKS + j], w_sem.at[CHUNKS + j])
        fetch_down(j, 2 * CHUNKS)

    fetch_chunk(0)
    flushed = []

    def flush(source, target):
        flushed.append(begin(source, target, o_sem.at[len(flushed)]))

    arriving.wait()
    normed_two.wait()
    inverses.wait()
    gains.wait()
    params = norm[...].astype(F32).T
    up = upstream[...].astype(F32)
    normed = n2[...]
    grad_two = norm_backward(up, normed, inv[:, HEAD : HEAD + 1], params[1:2])
    norm_grad[...] = jnp.zeros_like(norm_grad)
    norm_grad[1:2, :] = jnp.sum(up * normed, axis=0, keepdims=True)
    norm_grad[3:4, :] = jnp.sum(up, axis=0, keepdims=True)
    low_grad = grad_two.astype(BF)
    down_grad[...] = low_grad.T
    flush(down_grad, hidden_out.at[pl.ds(FF, D)])
    hidden.wait()
    low_hidden = h1[...]
    total = grad_two
    for j in range(CHUNKS):
        copies["gate", j].wait()
        copies["up", j].wait()
        if j + 1 < CHUNKS:
            fetch_chunk(j + 1)
        else:
            first_norm = InPlace()
            if not resident:
                first_norm = begin(n1_in.at[micro], n1, i_sem.at[5])
            ahead()
        gate = matmul(low_hidden, w_gu[j])
        rise = matmul(low_hidden, w_gu[CHUNKS + j])
        for q in range(4):
            copies["down", j, q].wait()
        gated_grad = matmul(low_grad, w_down[j].reshape(CHUNK, D), NT)
        cdf = 0.5 * (1.0 + lax.erf(gate * ROOT_HALF))
        density = jnp.exp(-0.5 * gate * gate) * INV_SQRT_2PI
        bent = gate * cdf
        cols = pl.ds(j * CHUNK, CHUNK)
        late_cols = pl.ds(FF + j * CHUNK, CHUNK)
        gated[cols] = (bent * rise).astype(BF).T
        flush(gated.at[cols], hidden_out.at[cols])
        gate_grad = (gated_grad * rise * (cdf + gate * density)).astype(BF)
        rise_grad = (gated_grad * bent).astype(BF)
        gu_grad[:, cols] = gate_grad
        gu_grad[:, late_cols] = rise_grad
        flush(gu_grad.at[:, cols], gate_out.at[:, cols])
        flush(gu_grad.at[:, late_cols], up_out.at[:, cols])
        total = total + matmul(gate_grad, w_gu[j], NT) + matmul(rise_grad, w_gu[CHUNKS + j], NT)
    first_norm.wait()
    normed = n1[...]
    grad_one = norm_backward(total, normed, inv[:, 0:1], params[0:1])
    norm_grad[0:1, :] = jnp.sum(total * normed, axis=0, keepdims=True)
    norm_grad[2:3, :] = jnp.sum(total, axis=0, keepdims=True)
    low_norm[...] = norm_grad[...].astype(BF)
    for k in range(3):
        source = low_norm.at[:, pl.ds(SEQ * k, SEQ)]
        flush(source, hidden_out.at[pl.ds(FF + D + 16 * k, 16)])
    return grad_one, flushed


def fetch_attention(wide, qkv_in, probs_in, w_qkv, w_out, qkv, probs, w_sem, i_sem, micro):
    copies = [
        begin(wide.at[:, pl.ds(COL_OUT, D)], w_out, w_sem.at[0]),
        begin(probs_in.at[micro], probs, i_sem.at[0]),
        begin(qkv_in.at[micro], qkv, i_sem.at[1]),
    ]
    for k in range(3):
        cols = pl.ds(D * k, D)
        copies.append(begin(wide.at[:, cols], w_qkv.at[:, cols], w_sem.at[1 + k]))
    return copies


def backward_attention(
    grad_one, copies, qk_out, vc_out, grad_out, hop_out,
    w_qkv, w_out, qkv, probs, attn_grad, context_grad, qkv_grad, grad, result,
    o_sem, *, micro,
):
    flushed = []

    def flush(source, target):
        flushed.append(begin(source, target, o_sem.at[len(flushed)]))

    low_attn = grad_one.astype(BF)
    attn_grad[...] = low_attn
    flush(attn_grad, vc_out.at[:, pl.ds(D, D)])
    copies[0].wait()
    context_grad[...] = matmul(low_attn, w_out[...], NT).astype(BF)
    copies[1].wait()
    copies[2].wait()
    first = lax.broadcasted_iota(jnp.int32, (SEQ, 128), 1) < HEAD
    root = jnp.asarray(HEAD ** (-0.5), BF)
    for pair in range(HEADS // 2):
        query = qkv[:, pl.ds(128 * pair, 128)] * root
        key = qkv[:, pl.ds(D + 128 * pair, 128)]
        value = qkv[:, pl.ds(2 * D + 128 * pair, 128)]
        upper = context_grad[:, pl.ds(128 * pair, 128)]
        query_across = query.T
        upper_across = upper.T
        query_sum, key_parts, value_parts = None, [], []
        for side in range(2):
            keep = first if side == 0 else ~first
            own_upper = jnp.where(keep, upper, jnp.zeros_like(upper))
            own_key = jnp.where(keep, key * root, jnp.zeros_like(key))
            low_probs = probs[2 * pair + side]
            wide_probs = low_probs.astype(F32)
            weighted = wide_probs * matmul(own_upper, value, NT)
            inner = jnp.sum(weighted, axis=-1, keepdims=True)
            score_grad = (weighted - wide_probs * inner).astype(BF)
            part = matmul(score_grad, own_key)
            query_sum = part if query_sum is None else query_sum + part
            rows = slice(HEAD * side, HEAD * (side + 1))
            key_parts.append(matmul(query_across[rows], score_grad))
            value_parts.append(matmul(upper_across[rows], low_probs))
        qkv_grad[:, pl.ds(128 * pair, 128)] = query_sum.astype(BF)
        key_grad = jnp.concatenate(key_parts, axis=0).T
        qkv_grad[:, pl.ds(D + 128 * pair, 128)] = key_grad.astype(BF)
        value_grad = jnp.concatenate(value_parts, axis=0).T
        qkv_grad[:, pl.ds(2 * D + 128 * pair, 128)] = value_grad.astype(BF)
    flush(qkv_grad.at[:, pl.ds(0, 2 * D)], qk_out)
    flush(qkv_grad.at[:, pl.ds(2 * D, D)], vc_out.at[:, pl.ds(0, D)])
    input_grad = grad_one
    for k in range(3):
        copies[3 + k].wait()
        cols = pl.ds(D * k, D)
        input_grad = input_grad + matmul(qkv_grad[:, cols], w_qkv[:, cols], NT)
    result[...] = input_grad.astype(BF)
    flush(result, hop_out)
    grad[...] = input_grad
    flush(grad, grad_out)
    return flushed


def backward_window(
    ids, given, wide, down, qkv_in, probs_in, n1_in, h1_in, n2_in, inv_in,
    hidden_out, gate_out, up_out, qk_out, vc_out, grad_out, hop_out,
    w_gu, w_down, upstream, n1, h1, n2, inv, norm, gated, down_grad, gu_grad, norm_grad, low_norm,
    w_qkv, w_out, qkv, probs, attn_grad, context_grad, qkv_grad, grad, result,
    w_sem, o_sem, i_sem, *, micro, direct,
):
    copies = []

    def ahead():
        copies.extend(
            fetch_attention(
                wide, qkv_in, probs_in, w_qkv, w_out, qkv, probs,
                w_sem.at[pl.ds(6 * CHUNKS, 4)], i_sem.at[pl.ds(6, 2)], micro,
            )
        )

    grad_one, flushed = backward_hidden(
        ids, given, wide, down, n1_in, h1_in, n2_in, inv_in, hidden_out, gate_out, up_out,
        w_gu, w_down, upstream, n1, h1, n2, inv, norm, gated, down_grad, gu_grad, norm_grad,
        low_norm, w_sem, o_sem, i_sem, micro=micro, direct=direct, ahead=ahead,
    )
    flushed += backward_attention(
        grad_one, copies, qk_out, vc_out, grad_out, hop_out,
        w_qkv, w_out, qkv, probs, attn_grad, context_grad, qkv_grad, grad, result,
        o_sem.at[pl.ds(HIDDEN_STORES, 5)], micro=micro,
    )
    for copy in flushed:
        copy.wait()


def both_ways(
    ids, lengths, given, cotangent, wide, down,
    left_out, layer_out, hidden_out, gate_out, up_out, qk_out, vc_out, grad_out, hop_out,
    w_gu, w_down, upstream, n1, h1, n2, inv, norm, gated, down_grad, gu_grad, norm_grad, low_norm,
    w_qkv, w_out, qkv, probs, attn_grad, context_grad, qkv_grad, grad, result,
    x, context, final, left, w_sem, o_sem, i_sem, f_sem, *, micro, direct,
):
    arriving = begin(own_window(cotangent, micro), upstream, i_sem.at[2])
    flushed = forward_window(
        ids, lengths, given, wide, down,
        left_out, None, None, None, None, None, None, layer_out, None,
        w_qkv, w_out, w_gu, w_down, x, qkv, probs, context, n1, h1, n2, inv, final, norm, left,
        w_sem, f_sem, i_sem, micro=micro, direct=direct, fused=True,
    )
    grad_one, stores = backward_hidden(
        ids, None, wide, down, None, None, None, None, hidden_out, gate_out, up_out,
        w_gu, w_down, upstream, n1, h1, n2, inv, norm, gated, down_grad, gu_grad, norm_grad,
        low_norm, w_sem, o_sem, i_sem, micro=micro, direct=direct, ahead=lambda: None,
        arriving=arriving,
    )
    flushed += stores
    flushed += backward_attention(
        grad_one, [InPlace()] * 6, qk_out, vc_out, grad_out, hop_out,
        w_qkv, w_out, qkv, probs, attn_grad, context_grad, qkv_grad, grad, result,
        o_sem.at[pl.ds(HIDDEN_STORES, 5)], micro=micro,
    )
    for copy in flushed:
        copy.wait()


def backward_first_half(
    ids, given, wide, down, n1_in, h1_in, n2_in, inv_in,
    hidden_out, gate_out, up_out, half_out,
    w_gu, w_down, upstream, n1, h1, n2, inv, norm, gated, down_grad, gu_grad, norm_grad, low_norm,
    half, w_sem, o_sem, i_sem, *, micro, direct,
):
    grad_one, flushed = backward_hidden(
        ids, given, wide, down, n1_in, h1_in, n2_in, inv_in, hidden_out, gate_out, up_out,
        w_gu, w_down, upstream, n1, h1, n2, inv, norm, gated, down_grad, gu_grad, norm_grad,
        low_norm, w_sem, o_sem, i_sem, micro=micro, direct=direct, ahead=lambda: None,
    )
    half[...] = grad_one
    flushed.append(begin(half, half_out, o_sem.at[HIDDEN_STORES]))
    for copy in flushed:
        copy.wait()


def backward_second_half(
    ids, given, wide, qkv_in, probs_in,
    qk_out, vc_out, grad_out, hop_out,
    half, w_qkv, w_out, qkv, probs, attn_grad, context_grad, qkv_grad, grad, result,
    w_sem, o_sem, i_sem, *, micro,
):
    arriving = begin(given, half, i_sem.at[2])
    copies = fetch_attention(
        wide, qkv_in, probs_in, w_qkv, w_out, qkv, probs, w_sem, i_sem, micro
    )
    arriving.wait()
    flushed = backward_attention(
        half[...], copies, qk_out, vc_out, grad_out, hop_out,
        w_qkv, w_out, qkv, probs, attn_grad, context_grad, qkv_grad, grad, result,
        o_sem, micro=micro,
    )
    for copy in flushed:
        copy.wait()


FORWARD_KEPT = (
    (True, 3 * D, SEQ, BF),
    (True, SEQ, 3 * D, BF),
    (True, HEADS, SEQ, SEQ, BF),
    (True, SEQ, D, F32),
    (True, SEQ, D, BF),
    (True, SEQ, D, F32),
    (True, SEQ, 128, F32),
    (True, SEQ, D, BF),
)
HIDDEN_KEPT = ((False, FF + D + 48, SEQ, BF), (False, SEQ, FF, BF), (False, SEQ, FF, BF))
ATTENTION_KEPT = ((False, SEQ, 2 * D, BF), (False, SEQ, 2 * D, BF), (True, SEQ, D, F32))
HIDDEN_STORES = 3 * CHUNKS + 4
HIDDEN_WEIGHTS = (
    pltpu.VMEM((2 * CHUNKS, D, CHUNK), BF),
    pltpu.VMEM((CHUNKS, 4, 4, ROWS, D), BF),
)
ATTENTION_WEIGHTS = (pltpu.VMEM((D, 3 * D), BF), pltpu.VMEM((D, D), BF))
HIDDEN_SCRATCH = HIDDEN_WEIGHTS + (
    pltpu.VMEM((SEQ, D), BF),
    pltpu.VMEM((SEQ, D), F32),
    pltpu.VMEM((SEQ, D), BF),
    pltpu.VMEM((SEQ, D), F32),
    pltpu.VMEM((SEQ, 128), F32),
    pltpu.VMEM((D, 128), BF),
    pltpu.VMEM((FF, SEQ), BF),
    pltpu.VMEM((D, SEQ), BF),
    pltpu.VMEM((SEQ, 2 * FF), BF),
    pltpu.VMEM((16, D), F32),
    pltpu.VMEM((16, D), BF),
)
ATTENTION_SCRATCH = ATTENTION_WEIGHTS + (
    pltpu.VMEM((SEQ, 3 * D), BF),
    pltpu.VMEM((HEADS, SEQ, SEQ), BF),
    pltpu.VMEM((SEQ, D), BF),
    pltpu.VMEM((SEQ, D), BF),
    pltpu.VMEM((SEQ, 3 * D), BF),
    pltpu.VMEM((SEQ, D), F32),
    pltpu.VMEM((SEQ, D), BF),
)
DMA = pltpu.SemaphoreType.DMA


def call_window(
    body, name, owner, micro, inputs, kept_shapes, sent, before, scratch, flops, small, gates=()
):
    count = len(kept_shapes)
    operands = tuple(inputs)
    aliases = {}
    for position, array in enumerate(before):
        if array is not None:
            aliases[len(operands)] = position
            operands += (array,)
    operands += tuple(gates)
    shapes = [
        jax.ShapeDtypeStruct((MICRO,) * shared + tuple(shape), dtype)
        for shared, *shape, dtype in kept_shapes
    ]
    shapes.append(jax.ShapeDtypeStruct((SEQ, D), sent))

    def kernel(*refs):
        @pl.when(refs[0][0] == owner)
        def _():
            outs = refs[len(operands) : len(operands) + count]
            views = [
                ref.at[micro] if shared else ref
                for ref, (shared, *_) in zip(outs, kept_shapes)
            ]
            body(*refs[: len(inputs)], *views, *refs[len(operands) + count :])

    return pl.pallas_call(
        kernel,
        out_shape=shapes,
        in_specs=[SMEM] * small + [ANY] * (len(operands) - small),
        out_specs=[ANY] * len(shapes),
        input_output_aliases=aliases,
        scratch_shapes=list(scratch),
        compiler_params=pltpu.CompilerParams(vmem_limit_bytes=VMEM_LIMIT),
        cost_estimate=pl.CostEstimate(
            flops=flops, bytes_accessed=flops // 200, transcendentals=flops // 4000
        ),
        name=name,
    )(*operands)


def forward_call(owner, micro, direct, ids, lengths, given, wide, down, before):
    scratch = (
        ATTENTION_WEIGHTS
        + HIDDEN_WEIGHTS
        + (
            pltpu.VMEM((SEQ, D), BF),
            pltpu.VMEM((SEQ, 3 * D), BF),
            pltpu.VMEM((HEADS, SEQ, SEQ), BF),
            pltpu.VMEM((SEQ, D), BF),
            pltpu.VMEM((SEQ, D), F32),
            pltpu.VMEM((SEQ, D), BF),
            pltpu.VMEM((SEQ, D), F32),
            pltpu.VMEM((SEQ, 128), F32),
            pltpu.VMEM((SEQ, D), BF),
            pltpu.VMEM((D, 128), BF),
            pltpu.VMEM((3 * D, SEQ), BF),
            DMA((4 + 6 * CHUNKS,)),
            DMA((12,)),
            DMA((2,)),
        )
    )
    return call_window(
        functools.partial(forward_window, micro=micro, direct=direct),
        "layer_forward",
        owner,
        micro,
        (ids, lengths, given, wide, down),
        FORWARD_KEPT,
        BF,
        before,
        scratch,
        5_000_000_000,
        2,
    )


def both_ways_call(owner, micro, direct, ids, lengths, given, cotangent, wide, down, before):
    return call_window(
        functools.partial(both_ways, micro=micro, direct=direct),
        "layer_both_ways",
        owner,
        micro,
        (ids, lengths, given, cotangent, wide, down),
        (FORWARD_KEPT[0], FORWARD_KEPT[-1]) + HIDDEN_KEPT + ATTENTION_KEPT,
        BF,
        before,
        HIDDEN_SCRATCH
        + ATTENTION_SCRATCH
        + (
            pltpu.VMEM((SEQ, D), BF),
            pltpu.VMEM((SEQ, D), BF),
            pltpu.VMEM((SEQ, D), BF),
            pltpu.VMEM((3 * D, SEQ), BF),
            DMA((4 + 6 * CHUNKS,)),
            DMA((HIDDEN_STORES + 5,)),
            DMA((3,)),
            DMA((12,)),
        ),
        130_000_000_000,
        2,
    )


def backward_call(owner, micro, direct, ids, given, wide, down, stash, before, gates):
    return call_window(
        functools.partial(backward_window, micro=micro, direct=direct),
        "layer_backward",
        owner,
        micro,
        (ids, given, wide, down) + tuple(stash),
        HIDDEN_KEPT + ATTENTION_KEPT,
        BF,
        before,
        HIDDEN_SCRATCH
        + ATTENTION_SCRATCH
        + (DMA((4 + 6 * CHUNKS,)), DMA((HIDDEN_STORES + 5,)), DMA((8,))),
        80_000_000_000,
        1,
        gates,
    )


def first_half_call(
    owner, micro, direct, ids, given, wide, down, stash, before, gates
):
    return call_window(
        functools.partial(backward_first_half, micro=micro, direct=direct),
        "backward_hidden",
        owner,
        micro,
        (ids, given, wide, down) + tuple(stash),
        HIDDEN_KEPT,
        F32,
        before,
        HIDDEN_SCRATCH
        + (
            pltpu.VMEM((SEQ, D), F32),
            DMA((6 * CHUNKS,)),
            DMA((HIDDEN_STORES + 1,)),
            DMA((6,)),
        ),
        60_000_000_000,
        1,
        gates,
    )


def second_half_call(owner, micro, ids, given, wide, stash, before, gates):
    return call_window(
        functools.partial(backward_second_half, micro=micro),
        "backward_attention",
        owner,
        micro,
        (ids, given, wide) + tuple(stash),
        ATTENTION_KEPT,
        BF,
        before,
        (pltpu.VMEM((SEQ, D), F32),) + ATTENTION_SCRATCH + (DMA((4,)), DMA((5,)), DMA((3,))),
        10 * PACE,
        1,
        gates,
    )


def pack_direct(w_qkv, w_out, w_gate_up, w_down, norm_gain, norm_bias):
    columns = [(0, 3 * D), (COL_OUT, D), (COL_GU, FF), (COL_GU + FF, FF)]
    columns += [(COL_DOWN + D * q, D) for q in range(4)]

    def body(qkv, out, gate_up, down, gain, bias, packed, held, low, square, i_sem, o_sem):
        sources = [qkv, out, gate_up.at[:, pl.ds(0, FF)], gate_up.at[:, pl.ds(FF, FF)]]
        sources += [down.at[pl.ds(ROWS * q, ROWS)] for q in range(4)]
        loads = [
            begin(source, held.at[:, pl.ds(start, size)], i_sem.at[k])
            for k, (source, (start, size)) in enumerate(zip(sources, columns))
        ]
        square[...] = jnp.zeros_like(square)
        square[pl.ds(0, 2), pl.ds(0, ROWS)] = gain[...]
        square[pl.ds(2, 2), pl.ds(0, ROWS)] = bias[...]
        low[:, pl.ds(COL_NORM, 128)] = square[...].T[:ROWS].astype(BF)
        stores = []
        for k, (load, (start, size)) in enumerate(zip(loads, columns)):
            cols = pl.ds(start, size)
            load.wait()
            low[:, cols] = held[:, cols].astype(BF)
            if k + 1 < len(loads):
                stores.append(begin(low.at[:, cols], packed.at[:, cols], o_sem.at[k]))
        cols = pl.ds(columns[-1][0], D + 128)
        stores.append(begin(low.at[:, cols], packed.at[:, cols], o_sem.at[len(loads) - 1]))
        for store in stores:
            store.wait()

    small = pl.BlockSpec(memory_space=pltpu.VMEM)
    return pl.pallas_call(
        body,
        out_shape=jax.ShapeDtypeStruct((ROWS, WIDE), BF),
        in_specs=[ANY] * 4 + [small] * 2,
        out_specs=ANY,
        scratch_shapes=[
            pltpu.VMEM((ROWS, COL_NORM), F32),
            pltpu.VMEM((ROWS, WIDE), BF),
            pltpu.VMEM((128, 128), F32),
            DMA((8,)),
            DMA((8,)),
        ],
        compiler_params=pltpu.CompilerParams(vmem_limit_bytes=VMEM_LIMIT),
        cost_estimate=cost_of(2),
        name="pack",
    )(w_qkv, w_out, w_gate_up, w_down, norm_gain, norm_bias)


def pack(w_qkv, w_out, w_gate_up, w_down, norm_gain, norm_bias):
    rows = w_qkv.shape[0]
    split_down = w_down.reshape(4, rows, D).transpose(1, 0, 2).reshape(rows, FF)
    norms = jnp.concatenate([norm_gain, norm_bias], axis=0).T
    norms = jnp.pad(norms, ((0, 0), (0, 128 - 4)))
    return jnp.concatenate([w_qkv, w_out, w_gate_up, split_down, norms], axis=1)


BIT_CORE, BIT_X, BIT_NEAR, BIT_FAR = 1, 2, 4, 8


def weight_grad_kernel(ids, terms, norm_ins, sent, kept, scratch, *, rows, order, turned):
    buffers, result, i_sem, o_sem = scratch[:4]
    columns, pieces, count = 0, [], 0

    def fetch(source, target):
        nonlocal count
        count += 1
        return begin(source, target, i_sem.at[count - 1])

    owned = []
    for place in range(8):
        relative = sum(bit for k, bit in enumerate(order) if not (place >> (2 - k)) & 1)
        owned.append(ids[1] ^ relative)
    for term, (lefts, rights) in enumerate(terms):
        left_buffer, right_buffer = buffers[term]
        whole = []
        for k, left in enumerate(lefts):
            for place in range(8):
                source = left.at[pl.ds(pl.multiple_of(owned[place] * rows, 16), rows)]
                target = left_buffer.at[place, :, pl.ds(SEQ * k, SEQ)]
                whole.append(fetch(source, target))
        for start in range(0, D if turned else right_buffer.shape[1], D):
            cols = pl.ds(start, D)
            parts = []
            for k, right in enumerate(rights):
                tokens = pl.ds(SEQ * k, SEQ)
                if turned:
                    parts.append(fetch(right, right_buffer.at[:, tokens]))
                else:
                    parts.append(fetch(right.at[:, cols], right_buffer.at[tokens, cols]))
            pieces.append((term, start, whole, parts, columns))
            columns += D
            whole = []
    if norm_ins:
        norm_buffer, norm_turned, norm_sem = scratch[4:]
        norm_loads = [
            begin(source.at[pl.ds(16 * k, 16)], norm_buffer.at[n, :, pl.ds(SEQ * k, SEQ)], norm_sem.at[n, k])
            for n, source in enumerate(norm_ins)
            for k in range(3)
        ]
    stores = []

    def store(first, count, cols):
        target = sent if first < 4 else kept
        source = result.at[pl.ds(first, count), :, cols]
        place = target.at[pl.ds(first % 4, count), :, cols]
        stores.append(begin(source, place, o_sem.at[len(stores)]))

    group = 192 // rows
    for term, start, whole, parts, column in pieces:
        left_buffer, right_buffer = buffers[term]
        for load in whole + parts:
            load.wait()
        values = right_buffer[...] if turned else right_buffer[:, pl.ds(start, D)]
        cols = pl.ds(column, D)
        for first in range(0, 8, 2 * group):
            taken = left_buffer[pl.ds(first, 2 * group)].reshape(2 * group * rows, TOKENS)
            value = matmul(taken, values, NT if turned else NN).astype(BF)
            result[pl.ds(first, 2 * group), :, cols] = value.reshape(2 * group, rows, D)
            for half in range(2):
                store(first + group * half, group, cols)
    if norm_ins:
        for load in norm_loads:
            load.wait()
        total = sum(norm_buffer[n].astype(F32) for n in range(4))
        total = jnp.concatenate([total, jnp.zeros((112, D), F32)], axis=0).T.astype(BF)
        norm_turned[...] = total.reshape(16, rows, 128)
        cols = pl.ds(columns, 128)
        for place in range(8):
            result[place, :, cols] = norm_turned[owned[place]]
        store(0, 4, cols)
        store(4, 4, cols)
    for copy in stores:
        copy.wait()


def weight_grad(ids, pairs, rows, order, gates, norms=None, turned=False):
    width = 0
    arrays, scratch = [], []

    def position(array):
        for k, known in enumerate(arrays):
            if known is array:
                return k
        arrays.append(array)
        return len(arrays) - 1

    def placed(side):
        return [(position(array), micro) for array, micro in side[0]], side[1]

    terms = [(placed(left), placed(right)) for left, right in pairs]
    norm_places = placed(norms) if norms else None
    loads, stores = 0, 0
    for _, (_, taken) in terms:
        size = taken.stop - taken.start
        shape = (size, TOKENS) if turned else (TOKENS, size)
        scratch += [pltpu.VMEM((8, rows, TOKENS), BF), pltpu.VMEM(shape, BF)]
        loads += 32 + 4 * (size // D)
        stores += 8 * (size // D)
        width += size
    total = width + 128 * bool(norms)
    shape = jax.ShapeDtypeStruct((4, rows, total), BF)
    count = 1 + len(arrays) + len(gates)

    def view(refs, place, taken, along_rows):
        index, micro = place
        ref = refs[1 + index] if micro is None else refs[1 + index].at[micro]
        span = pl.ds(taken.start, taken.stop - taken.start)
        return ref.at[span] if along_rows else ref.at[:, span]

    def body(*refs):
        sources = [
            (
                [view(refs, place, left[1], True) for place in left[0]],
                [view(refs, place, right[1], turned) for place in right[0]],
            )
            for left, right in terms
        ]
        norm_views = []
        if norms:
            norm_views = [view(refs, place, norm_places[1], True) for place in norm_places[0]]
        rest = refs[count + 2 :]
        buffers = [(rest[2 * k], rest[2 * k + 1]) for k in range(len(terms))]
        weight_grad_kernel(
            refs[0],
            sources,
            norm_views,
            refs[count],
            refs[count + 1],
            (buffers,) + tuple(rest[2 * len(terms) :]),
            rows=rows,
            order=order,
            turned=turned,
        )

    scratch += [pltpu.VMEM((8, rows, total), BF), DMA((loads,)), DMA((stores + 2,))]
    if norms:
        scratch += [pltpu.VMEM((4, 16, D), BF), pltpu.VMEM((16, rows, 128), BF), DMA((4, 3))]
    return pl.pallas_call(
        body,
        out_shape=[shape, shape],
        in_specs=[SMEM] + [ANY] * (count - 1),
        out_specs=[ANY] * 2,
        scratch_shapes=scratch,
        compiler_params=pltpu.CompilerParams(vmem_limit_bytes=VMEM_LIMIT),
        cost_estimate=cost_of(8),
        name="weight_grad",
    )(ids, *arrays, *gates)


def exchange(values, bit):
    count = lax.axis_size("dp")
    return lax.ppermute(values, "dp", [(i, i ^ bit) for i in range(count)])


def halve(parts, gates):
    half = len(parts[0]) // 2
    arrays = []
    for part in parts:
        for array, _ in part[:half]:
            if not any(array is known for known in arrays):
                arrays.append(array)
    where = [
        [next((k, at) for k, known in enumerate(arrays) if known is array) for array, at in part[:half]]
        for part in parts
    ]
    block = arrays[0].shape[1:]
    count = len(parts)

    def body(*refs):
        outgoing, held, result, i_sem, o_sem = refs[len(arrays) + len(gates) :]
        loads = [
            [
                begin(refs[where[p][i][0]].at[where[p][i][1]], held.at[p, i], i_sem.at[p, i])
                for p in range(count)
            ]
            for i in range(half)
        ]
        stores = []
        for i in range(half):
            total = None
            for p in range(count):
                loads[i][p].wait()
                value = held[p, i].astype(F32)
                total = value if total is None else total + value
            result[i] = total.astype(BF)
            stores.append(begin(result.at[i], outgoing.at[i], o_sem.at[i]))
        for copy in stores:
            copy.wait()

    return pl.pallas_call(
        body,
        out_shape=jax.ShapeDtypeStruct((half,) + block, BF),
        in_specs=[ANY] * (len(arrays) + len(gates)),
        out_specs=ANY,
        scratch_shapes=[
            pltpu.VMEM((count, half) + block, BF),
            pltpu.VMEM((half,) + block, BF),
            DMA((count, half)),
            DMA((half,)),
        ],
        compiler_params=pltpu.CompilerParams(vmem_limit_bytes=VMEM_LIMIT),
        cost_estimate=cost_of(2),
        name="halve",
    )(*arrays, *gates)


def blocks_of(array):
    return [(array, at) for at in range(array.shape[0])]


def finish(parts, gates, pieces, carried=None):
    arrays, places = [], []
    for ((array, at),) in parts:
        if not any(array is known for known in arrays):
            arrays.append(array)
        places.append((next(k for k, known in enumerate(arrays) if known is array), at))
    rows, width = arrays[0].shape[1:]
    operands = tuple(arrays) + tuple(gates) + (() if carried is None else (carried,))

    def body(*refs):
        outs = refs[len(operands) :][: len(pieces)]
        held, made, i_sem, o_sem = refs[len(operands) + len(pieces) :]
        loads = [
            begin(refs[index].at[at], held.at[k], i_sem.at[k])
            for k, (index, at) in enumerate(places)
        ]
        total = None
        for k, load in enumerate(loads):
            load.wait()
            value = held[k].astype(F32)
            total = value if total is None else total + value
        if width > 4 * D:
            norms = jnp.concatenate(
                [total[:, 4 * D :], jnp.zeros((128 - rows, 128), F32)], axis=0
            ).T
            made[:, pl.ds(0, 4 * D)] = total[:, : 4 * D]
            outs[2][...] = norms[0:2, :rows]
            outs[3][...] = norms[2:4, :rows]
        else:
            made[...] = total
        stores = []
        for k, (out, (shape, start, column)) in enumerate(zip(outs, pieces[:2])):
            count, size = min(shape[0], rows), min(shape[1], width)
            source = made.at[pl.ds(0, count), pl.ds(start, size)]
            stores.append(begin(source, out.at[:, pl.ds(column, size)], o_sem.at[k]))
        for store in stores:
            store.wait()

    return pl.pallas_call(
        body,
        out_shape=[jax.ShapeDtypeStruct(shape, F32) for shape, _, _ in pieces],
        in_specs=[ANY] * len(operands),
        out_specs=([ANY] * 2 + [pl.BlockSpec(memory_space=pltpu.VMEM)] * 2)[: len(pieces)]
        if len(pieces) > 1
        else [ANY],
        input_output_aliases={} if carried is None else {len(operands) - 1: 0},
        scratch_shapes=[
            pltpu.VMEM((len(parts), rows, width), BF),
            pltpu.VMEM((rows, width), F32),
            DMA((len(parts),)),
            DMA((len(pieces),)),
        ],
        compiler_params=pltpu.CompilerParams(vmem_limit_bytes=VMEM_LIMIT),
        cost_estimate=cost_of(2),
        name="finish",
    )(*operands)


LINKS = {
    "down": (BIT_X, BIT_NEAR, BIT_FAR),
    "gate": (BIT_NEAR, BIT_X, BIT_FAR),
    "rise": (BIT_X, BIT_NEAR, BIT_FAR),
    "attn": (BIT_X, BIT_NEAR, BIT_FAR),
}
PLAN = (
    ("local", "down"),
    ("local", "gate"),
    ("local", "rise"),
    ("attention", "attn"),
    ("step", "down"),
    ("local", "attn"),
    ("step", "gate"),
    ("step", "rise"),
    ("step", "down"),
    ("step", "rise"),
    ("step", "attn"),
    ("finish", "down"),
    ("step", "gate"),
    ("finish", "rise"),
    ("step", "attn"),
    ("finish", "gate"),
    ("finish", "attn"),
)


def reduce_shares(ids, lefts, hidden, gates_ups, attention_first, second_half):
    parts, last, done = {}, [], {}
    order = {}

    def local(name, pairs, rows, bits, norms=None, turned=False):
        order[name] = list(bits)
        sent, kept = weight_grad(ids, pairs, rows, bits, last, norms, turned)
        parts[name] = [blocks_of(kept), blocks_of(exchange(sent, order[name].pop(0)))]
        last[:] = [sent]

    def step(name):
        sent = halve(parts[name], last)
        parts[name] = [part[sent.shape[0] :] for part in parts[name]]
        parts[name].append(blocks_of(exchange(sent, order[name].pop(0))))
        last[:] = [sent]

    inputs, context, h1 = ((lefts, slice(D * k, D * (k + 1))) for k in range(3))
    hidden_pairs = {
        "down": [((hidden, slice(0, FF)), (hidden, slice(FF, FF + D)))],
        "gate": [(h1, (gates_ups[0], slice(0, FF)))],
        "rise": [(h1, (gates_ups[1], slice(0, FF)))],
    }
    for action, name in PLAN:
        if action == "step":
            step(name)
        elif action == "finish":
            wide = (ROWS, 2 * FF)
            pieces = {
                "down": [((4 * ROWS, D), 0, 0)],
                "gate": [(wide, 0, 0)],
                "rise": [(wide, 0, FF)],
                "attn": [((ROWS, 3 * D), 0, 0), ((ROWS, D), 3 * D, 0)] + [((2, ROWS), 0, 0)] * 2,
            }
            carried = done["gate"][0] if "gate" in done and name in ("gate", "rise") else None
            made = finish(parts[name], last, pieces[name], carried)
            done["gate" if name == "rise" else name] = made
            last[:] = [made[0]] if name not in ("gate", "rise") else []
        elif action == "attention":
            attention_second, input_grads, _ = second_half(
                last + [other[0] for _, other in attention_first]
            )
            last[:] = [attention_second[0]]
            q_grads, v_grads = (
                [own, (array, None), other, (exchange(array, BIT_CORE), None)]
                for (own, other), array in zip(attention_first, attention_second)
            )
        elif name == "attn":
            pairs = [
                (inputs, (q_grads, slice(0, 2 * D))),
                (inputs, (v_grads, slice(0, D))),
                (context, (v_grads, slice(D, 2 * D))),
            ]
            local(name, pairs, ROWS, LINKS[name], (hidden, slice(FF + D, FF + D + 48)))
        else:
            rows = 4 * ROWS if name == "down" else ROWS
            local(name, hidden_pairs[name], rows, LINKS[name], turned=name == "down")
    shares = (
        done["attn"][0],
        done["attn"][1],
        done["gate"][0],
        done["down"][0],
        done["attn"][2],
        done["attn"][3],
    )
    return shares, input_grads


def packed_shares(rows, left, hidden, gates, ups, attention):
    def product(lefts, rights, dims=NN):
        lefts = jnp.concatenate(lefts, axis=1)
        rights = jnp.concatenate(rights, axis=1 if dims == NT else 0)
        return matmul(lefts, rights, dims).astype(BF)

    def cut(arrays, start, stop):
        return [array[start:stop] for array in arrays]

    left = list(left)
    down = product(cut(hidden, 0, FF), cut(hidden, FF, FF + D), NT).reshape(D // rows, 4, rows, D)
    norm_sum = sum(array[FF + D :].astype(F32) for array in hidden)
    norm_sum = norm_sum.reshape(3, 16, SEQ)[:, :4].transpose(1, 0, 2).reshape(4, D).T.astype(BF)
    attention = [jnp.concatenate(pair, axis=1) for pair in attention]
    summed = [
        product(cut(left, 0, D), [array[:, : 3 * D] for array in attention]),
        product(cut(left, D, 2 * D), [array[:, 3 * D :] for array in attention]),
        product(cut(left, 2 * D, 3 * D), gates),
        product(cut(left, 2 * D, 3 * D), ups),
        down.transpose(0, 2, 1, 3).reshape(D, FF),
        jnp.pad(norm_sum, ((0, 0), (0, 128 - 4))),
    ]
    summed = jnp.concatenate(summed, axis=1)
    share = lax.psum_scatter(summed, "dp", scatter_dimension=0, tiled=True).astype(F32)
    down = share[:, COL_DOWN:COL_NORM].reshape(rows, 4, D).transpose(1, 0, 2)
    norm = share[:, COL_NORM : COL_NORM + 4].T
    return (
        share[:, :COL_OUT],
        share[:, COL_OUT:COL_GU],
        share[:, COL_GU:COL_DOWN],
        down.reshape(4 * rows, D),
        norm[:2],
        norm[2:],
    )


def shards(tokens, lengths, w_qkv, w_out, w_gate_up, w_down, norm_gain, norm_bias, cotangent):
    rows = w_qkv.shape[1]
    direct = rows == ROWS
    section = lax.axis_index("section")
    ids = jnp.stack([section, lax.axis_index("dp")]).astype(jnp.int32)
    sharded = [w[0] for w in (w_qkv, w_out, w_gate_up, w_down, norm_gain, norm_bias)]
    packed = pack_direct(*sharded) if direct else pack(*(w.astype(BF) for w in sharded))
    wide = lax.all_gather(packed, "dp", axis=0, tiled=True)
    if direct:
        down = wide.reshape(D // rows, rows, WIDE)
    else:
        down = wide[:, COL_DOWN:COL_NORM].reshape(D // rows, rows, 4, D)
        down = down.transpose(0, 2, 1, 3).reshape(FF // (4 * ROWS), 4, ROWS, D)

    def hop(rows_sent, pair):
        return lax.ppermute(rows_sent, "section", [pair])

    def forward(owner, micro, given, before):
        return forward_call(
            owner, micro, direct, ids, lengths, given, wide, down, before
        )

    *kept, sent = forward(0, 0, tokens, [None] * len(FORWARD_KEPT))
    arrived_first = hop(sent, (0, 1))
    *kept, sent = forward(0, 1, tokens, kept)
    arrived_second = hop(sent, (0, 1))
    left, qkv, probs, n1, h1, n2, inv, layer_out = kept
    stash = (qkv, probs, n1, h1, n2, inv)

    def both_passes(micro, given, before):
        return both_ways_call(
            1, micro, direct, ids, lengths, given, cotangent, wide, down, before
        )

    def both(array):
        return [(array, None), (exchange(array, BIT_CORE), None)]

    left, layer_out, *first, input_grads, sent = both_passes(
        0, arrived_first, [left, layer_out] + [None] * 6
    )
    arrived_first = hop(sent, (1, 0))
    left, layer_out, *second, input_grads, sent = both_passes(
        1, arrived_second, [left, layer_out] + [None] * 5 + [input_grads]
    )
    arrived_second = hop(sent, (1, 0))
    left_other = exchange(left, BIT_CORE) if direct else left
    *first, input_grads, sent = backward_call(
        0, 0, direct, ids, arrived_first, wide, down, stash, first + [input_grads], ()
    )
    if direct:
        first = [both(array) for array in first]
    gates = (left_other,) if direct else ()
    *hidden, half = first_half_call(
        0, 1, direct, ids, arrived_second, wide, down, (n1, h1, n2, inv), second[:3], gates
    )

    def second_half(gates):
        before = second[3:] + [input_grads]
        *made, input_sum, _ = second_half_call(
            0, 1, ids, half, wide, (qkv, probs), before, gates
        )
        return made, input_sum, None

    if direct:
        lefts = [(left, 0), (left, 1), (left_other, 0), (left_other, 1)]

        def paired(k):
            own, other = zip(first[k], both(hidden[k]))
            return list(own) + list(other)

        shares, input_grads = reduce_shares(
            ids,
            lefts,
            paired(0),
            [paired(1), paired(2)],
            [[first[3][0], first[3][1]], [first[4][0], first[4][1]]],
            second_half,
        )
    else:
        attention, input_grads, _ = second_half(())
        pairs = [first[3:5], attention]
        shares = packed_shares(
            rows, left, [first[0], hidden[0]], [first[1], hidden[1]], [first[2], hidden[2]], pairs
        )
    return (layer_out[None], input_grads[None]) + tuple(share[None] for share in shares)


def solution(mesh):
    return jax.shard_map(
        shards,
        mesh=mesh,
        in_specs=(
            P(None, "dp", None),
            P(),
            P("section", "dp", None),
            P("section", "dp", None),
            P("section", "dp", None),
            P("section", "dp", None),
            P("section", None, "dp"),
            P("section", None, "dp"),
            P(None, "dp", None),
        ),
        out_specs=(
            P("section", None, "dp", None),
            P("section", None, "dp", None),
            P("section", "dp", None),
            P("section", "dp", None),
            P("section", "dp", None),
            P("section", "dp", None),
            P("section", None, "dp"),
            P("section", None, "dp"),
        ),
        check_vma=False,
    )
```

```python
import functools

import jax
import jax.numpy as jnp
from jax import lax
from jax.experimental import pallas as pl
from jax.experimental.pallas import tpu as pltpu
from jax.sharding import PartitionSpec as P

D = 768
HEADS = 12
HEAD = 64
FF = 3072
SEQ = 256
MICRO = 2
TOKENS = 2 * MICRO * SEQ
EPSILON = 1e-05
FAR = 1e30
INV_SQRT_2PI = 0.3989422804014327
ROOT_HALF = 2.0 ** (-0.5)

COL_OUT = 3 * D
COL_GU = 4 * D
COL_DOWN = COL_GU + 2 * FF
COL_NORM = COL_DOWN + FF
WIDE = COL_NORM + 128

CHUNK = 768
CHUNKS = FF // CHUNK
ROWS = 48
BF = jnp.bfloat16
F32 = jnp.float32
NN = (((1,), (0,)), ((), ()))
NT = (((1,), (1,)), ((), ()))
TN = (((0,), (0,)), ((), ()))
SLOPES = [2.0 ** (-8.0 * (h + 1) / HEADS) for h in range(HEADS)]

VMEM_LIMIT = 64 << 20
ANY = pl.BlockSpec(memory_space=pl.ANY)
SMEM = pl.BlockSpec(memory_space=pltpu.SMEM)


def matmul(left, right, dims=NN):
    return lax.dot_general(left, right, dims, preferred_element_type=F32)


def begin(source, target, semaphore):
    copy = pltpu.make_async_copy(source, target, semaphore)
    copy.start()
    return copy


PACE = 9_200_000_000


def cost_of(microseconds):
    return pl.CostEstimate(
        flops=microseconds * PACE, bytes_accessed=microseconds * PACE // 200, transcendentals=0
    )


def own_window(given, micro):
    return given if len(given.shape) == 2 else given.at[micro]


def row_mean(values):
    return jnp.mean(values, axis=-1, keepdims=True)


def norm_forward(values, gain, bias):
    center = values - row_mean(values)
    inverse = lax.rsqrt(row_mean(center * center) + EPSILON)
    normed = center * inverse
    return normed * gain + bias, normed, inverse


def norm_backward(upstream, normed, inverse, gain):
    scaled = upstream * gain
    return inverse * (scaled - row_mean(scaled) - normed * row_mean(scaled * normed))


def forward_window(
    ids, lengths, given, wide, down,
    left_out, qkv_out, probs_out, n1_out, h1_out, n2_out, inv_out, layer_out, hop_out,
    w_qkv, w_out, w_gu, w_down, x, qkv, probs, context, n1, h1, n2, inv, result, norm, left,
    w_sem, o_sem, i_sem, *, micro, direct, fused=False, ready=None,
):
    window = ids[1]
    copies = {}
    copies["x"] = begin(own_window(given, micro), x, i_sem.at[0])
    for k in range(3):
        cols = pl.ds(D * k, D)
        copies["qkv", k] = begin(wide.at[:, cols], w_qkv.at[:, cols], w_sem.at[k])
    copies["norm"] = begin(wide.at[:, pl.ds(COL_NORM, 128)], norm, i_sem.at[1])

    def fetch_down(j, base):
        owners = down.at[pl.ds(4 * j, 4)]
        for q in range(4):
            source = owners.at[:, :, pl.ds(COL_DOWN + D * q, D)] if direct else owners.at[:, q]
            copies["down", j, q] = begin(
                source, w_down.at[j, :, q], w_sem.at[base + 4 * j + q]
            )

    def fetch_chunk(j):
        gate = wide.at[:, pl.ds(COL_GU + j * CHUNK, CHUNK)]
        rise = wide.at[:, pl.ds(COL_GU + FF + j * CHUNK, CHUNK)]
        copies["gate", j] = begin(gate, w_gu.at[j], w_sem.at[4 + j])
        copies["up", j] = begin(rise, w_gu.at[CHUNKS + j], w_sem.at[4 + CHUNKS + j])
        fetch_down(j, 4 + 2 * CHUNKS)

    flushed = []

    def flush(source, target):
        if target is None:
            return
        flushed.append(begin(source, target, o_sem.at[len(flushed)]))

    row_place = lax.broadcasted_iota(jnp.int32, (SEQ, SEQ), 0)
    key_place = lax.broadcasted_iota(jnp.int32, (SEQ, SEQ), 1)
    distance = jnp.abs(row_place - key_place).astype(F32)
    distance = jnp.where(key_place < lengths[micro, window], distance, FAR)
    lane = lax.broadcasted_iota(jnp.int32, (SEQ, 128), 1)
    first = lane < HEAD
    copies["x"].wait()
    rows_in = x[...]


    def flush_turned(part, values):
        rows = pl.ds(D * part, D)
        left[rows] = values.T
        flush(left.at[rows], left_out.at[rows])

    flush_turned(0, rows_in)
    for k in range(3):
        copies["qkv", k].wait()
        if k == 1:
            copies["out"] = begin(wide.at[:, pl.ds(COL_OUT, D)], w_out, w_sem.at[3])
            fetch_chunk(0)
        if k == 2:
            for j in range(1, CHUNKS):
                fetch_chunk(j)
        cols = pl.ds(D * k, D)
        qkv[:, cols] = matmul(rows_in, w_qkv[:, cols]).astype(BF)
    flush(qkv, qkv_out)
    for pair in range(HEADS // 2):
        query = qkv[:, pl.ds(128 * pair, 128)] * jnp.asarray(HEAD ** (-0.5), BF)
        key = qkv[:, pl.ds(D + 128 * pair, 128)]
        value = qkv[:, pl.ds(2 * D + 128 * pair, 128)]
        total = None
        for side in range(2):
            head = 2 * pair + side
            keep = first if side == 0 else ~first
            own_query = jnp.where(keep, query, jnp.zeros_like(query))
            own_value = jnp.where(keep, value, jnp.zeros_like(value))
            scores = matmul(own_query, key, NT) - distance * SLOPES[head]
            peak = jnp.max(scores, axis=-1, keepdims=True)
            grown = jnp.exp(scores - peak)
            share = 1.0 / jnp.sum(grown, axis=-1, keepdims=True)
            low_probs = (grown * share).astype(BF)
            probs[head] = low_probs
            mixed = matmul(low_probs, own_value)
            total = mixed if total is None else total + mixed
        context[:, pl.ds(128 * pair, 128)] = total.astype(BF)
    flush(probs, probs_out)
    flush_turned(1, context[...])
    copies["out"].wait()
    copies["norm"].wait()
    params = norm[...].astype(F32).T
    summed = rows_in.astype(F32) + matmul(context[...], w_out[...])
    hidden, normed, inverse_one = norm_forward(summed, params[0:1], params[2:3])
    n1[...] = normed
    flush(n1, n1_out)
    low_hidden = hidden.astype(BF)
    h1[...] = low_hidden
    flush(h1, h1_out)
    flush_turned(2, low_hidden)
    for j in range(CHUNKS):
        copies["gate", j].wait()
        copies["up", j].wait()
        gate = matmul(low_hidden, w_gu[j])
        rise = matmul(low_hidden, w_gu[CHUNKS + j])
        cdf = 0.5 * (1.0 + lax.erf(gate * ROOT_HALF))
        bent = gate * cdf
        gated = (bent * rise).astype(BF)
        if ready is not None:
            ready(j, gate, rise, cdf, bent, gated)
        for q in range(4):
            copies["down", j, q].wait()
        hidden = hidden + matmul(gated, w_down[j].reshape(CHUNK, D))
    final, normed, inverse_two = norm_forward(hidden, params[1:2], params[3:4])
    result[...] = final.astype(BF)
    flush(result, hop_out)
    flush(result, layer_out)
    n2[...] = normed
    flush(n2, n2_out)
    inv[...] = jnp.where(first, inverse_one, inverse_two)
    flush(inv, inv_out)
    if fused:
        return flushed
    for copy in flushed:
        copy.wait()


def forward_ready(
    ids, lengths, given, wide, down,
    left_out, qkv_out, probs_out, n1_out, h1_out, n2_out, inv_out, layer_out,
    hidden_out, slope_out, bent_out, hop_out, *scratch, micro, direct,
):
    gated_turned, slopes, bents, r_sem = scratch[-4:]
    stores = []

    def ready(j, gate, rise, cdf, bent, gated):
        cols = pl.ds(j * CHUNK, CHUNK)
        density = jnp.exp(-0.5 * gate * gate) * INV_SQRT_2PI
        slopes[:, cols] = rise * (cdf + gate * density)
        bents[:, cols] = bent
        gated_turned[cols] = gated.T
        made = (
            (gated_turned.at[cols], hidden_out.at[cols]),
            (slopes.at[:, cols], slope_out.at[:, cols]),
            (bents.at[:, cols], bent_out.at[:, cols]),
        )
        for source, target in made:
            stores.append(begin(source, target, r_sem.at[len(stores)]))

    forward_window(
        ids, lengths, given, wide, down,
        left_out, qkv_out, probs_out, n1_out, h1_out, n2_out, inv_out, layer_out, hop_out,
        *scratch[:-4], micro=micro, direct=direct, ready=ready,
    )
    for store in stores:
        store.wait()


class InPlace:
    def wait(self):
        return None


def backward_hidden(
    ids, given, wide, down, n1_in, h1_in, n2_in, inv_in, hidden_out, gate_out, up_out,
    w_gu, w_down, upstream, n1, h1, n2, inv, norm, gated, down_grad, gu_grad, norm_grad,
    low_norm, w_sem, o_sem, i_sem, *, micro, direct, ahead, arriving=None,
):
    resident = arriving is not None

    def load(source, target, semaphore):
        return InPlace() if resident else begin(source, target, semaphore)

    if not resident:
        arriving = begin(own_window(given, micro), upstream, i_sem.at[0])
        normed_two = begin(n2_in.at[micro], n2, i_sem.at[1])
        inverses = begin(inv_in.at[micro], inv, i_sem.at[2])
        gains = begin(wide.at[:, pl.ds(COL_NORM, 128)], norm, i_sem.at[3])
        hidden = begin(h1_in.at[micro], h1, i_sem.at[4])
    else:
        normed_two = inverses = gains = hidden = InPlace()
    copies = {}

    def fetch_down(j, base):
        owners = down.at[pl.ds(4 * j, 4)]
        for q in range(4):
            source = owners.at[:, :, pl.ds(COL_DOWN + D * q, D)] if direct else owners.at[:, q]
            copies["down", j, q] = load(
                source, w_down.at[j, :, q], w_sem.at[base + 4 * j + q]
            )

    def fetch_chunk(j):
        gate = wide.at[:, pl.ds(COL_GU + j * CHUNK, CHUNK)]
        rise = wide.at[:, pl.ds(COL_GU + FF + j * CHUNK, CHUNK)]
        copies["gate", j] = load(gate, w_gu.at[j], w_sem.at[j])
        copies["up", j] = load(rise, w_gu.at[CHUNKS + j], w_sem.at[CHUNKS + j])
        fetch_down(j, 2 * CHUNKS)

    fetch_chunk(0)
    flushed = []

    def flush(source, target):
        flushed.append(begin(source, target, o_sem.at[len(flushed)]))

    arriving.wait()
    normed_two.wait()
    inverses.wait()
    gains.wait()
    params = norm[...].astype(F32).T
    up = upstream[...].astype(F32)
    normed = n2[...]
    grad_two = norm_backward(up, normed, inv[:, HEAD : HEAD + 1], params[1:2])
    norm_grad[...] = jnp.zeros_like(norm_grad)
    norm_grad[1:2, :] = jnp.sum(up * normed, axis=0, keepdims=True)
    norm_grad[3:4, :] = jnp.sum(up, axis=0, keepdims=True)
    low_grad = grad_two.astype(BF)
    down_grad[...] = low_grad.T
    flush(down_grad, hidden_out.at[pl.ds(FF, D)])
    hidden.wait()
    low_hidden = h1[...]
    total = grad_two
    for j in range(CHUNKS):
        copies["gate", j].wait()
        copies["up", j].wait()
        if j + 1 < CHUNKS:
            fetch_chunk(j + 1)
        else:
            first_norm = InPlace()
            if not resident:
                first_norm = begin(n1_in.at[micro], n1, i_sem.at[5])
            ahead()
        gate = matmul(low_hidden, w_gu[j])
        rise = matmul(low_hidden, w_gu[CHUNKS + j])
        for q in range(4):
            copies["down", j, q].wait()
        gated_grad = matmul(low_grad, w_down[j].reshape(CHUNK, D), NT)
        cdf = 0.5 * (1.0 + lax.erf(gate * ROOT_HALF))
        density = jnp.exp(-0.5 * gate * gate) * INV_SQRT_2PI
        bent = gate * cdf
        cols = pl.ds(j * CHUNK, CHUNK)
        late_cols = pl.ds(FF + j * CHUNK, CHUNK)
        gated[cols] = (bent * rise).astype(BF).T
        flush(gated.at[cols], hidden_out.at[cols])
        gate_grad = (gated_grad * rise * (cdf + gate * density)).astype(BF)
        rise_grad = (gated_grad * bent).astype(BF)
        gu_grad[:, cols] = gate_grad
        gu_grad[:, late_cols] = rise_grad
        flush(gu_grad.at[:, cols], gate_out.at[:, cols])
        flush(gu_grad.at[:, late_cols], up_out.at[:, cols])
        total = total + matmul(gate_grad, w_gu[j], NT) + matmul(rise_grad, w_gu[CHUNKS + j], NT)
    first_norm.wait()
    normed = n1[...]
    grad_one = norm_backward(total, normed, inv[:, 0:1], params[0:1])
    norm_grad[0:1, :] = jnp.sum(total * normed, axis=0, keepdims=True)
    norm_grad[2:3, :] = jnp.sum(total, axis=0, keepdims=True)
    low_norm[...] = norm_grad[...].astype(BF)
    for k in range(3):
        source = low_norm.at[:, pl.ds(SEQ * k, SEQ)]
        flush(source, hidden_out.at[pl.ds(FF + D + 16 * k, 16)])
    return grad_one, flushed


def fetch_attention(wide, qkv_in, probs_in, w_qkv, w_out, qkv, probs, w_sem, i_sem, micro):
    copies = [
        begin(wide.at[:, pl.ds(COL_OUT, D)], w_out, w_sem.at[0]),
        begin(probs_in.at[micro], probs, i_sem.at[0]),
        begin(qkv_in.at[micro], qkv, i_sem.at[1]),
    ]
    for k in range(3):
        cols = pl.ds(D * k, D)
        copies.append(begin(wide.at[:, cols], w_qkv.at[:, cols], w_sem.at[1 + k]))
    return copies


def backward_attention(
    grad_one, copies, qk_out, vc_out, grad_out, hop_out,
    w_qkv, w_out, qkv, probs, attn_grad, context_grad, qkv_grad, grad, result,
    o_sem, *, micro,
):
    flushed = []

    def flush(source, target):
        flushed.append(begin(source, target, o_sem.at[len(flushed)]))

    low_attn = grad_one.astype(BF)
    attn_grad[...] = low_attn
    flush(attn_grad, vc_out.at[:, pl.ds(D, D)])
    copies[0].wait()
    context_grad[...] = matmul(low_attn, w_out[...], NT).astype(BF)
    copies[1].wait()
    copies[2].wait()
    first = lax.broadcasted_iota(jnp.int32, (SEQ, 128), 1) < HEAD
    root = jnp.asarray(HEAD ** (-0.5), BF)
    for pair in range(HEADS // 2):
        query = qkv[:, pl.ds(128 * pair, 128)] * root
        key = qkv[:, pl.ds(D + 128 * pair, 128)]
        value = qkv[:, pl.ds(2 * D + 128 * pair, 128)]
        upper = context_grad[:, pl.ds(128 * pair, 128)]
        query_across = query.T
        upper_across = upper.T
        query_sum, key_parts, value_parts = None, [], []
        for side in range(2):
            keep = first if side == 0 else ~first
            own_upper = jnp.where(keep, upper, jnp.zeros_like(upper))
            own_key = jnp.where(keep, key * root, jnp.zeros_like(key))
            low_probs = probs[2 * pair + side]
            wide_probs = low_probs.astype(F32)
            weighted = wide_probs * matmul(own_upper, value, NT)
            inner = jnp.sum(weighted, axis=-1, keepdims=True)
            score_grad = (weighted - wide_probs * inner).astype(BF)
            part = matmul(score_grad, own_key)
            query_sum = part if query_sum is None else query_sum + part
            rows = slice(HEAD * side, HEAD * (side + 1))
            key_parts.append(matmul(query_across[rows], score_grad))
            value_parts.append(matmul(upper_across[rows], low_probs))
        qkv_grad[:, pl.ds(128 * pair, 128)] = query_sum.astype(BF)
        key_grad = jnp.concatenate(key_parts, axis=0).T
        qkv_grad[:, pl.ds(D + 128 * pair, 128)] = key_grad.astype(BF)
        value_grad = jnp.concatenate(value_parts, axis=0).T
        qkv_grad[:, pl.ds(2 * D + 128 * pair, 128)] = value_grad.astype(BF)
    flush(qkv_grad.at[:, pl.ds(0, 2 * D)], qk_out)
    flush(qkv_grad.at[:, pl.ds(2 * D, D)], vc_out.at[:, pl.ds(0, D)])
    input_grad = grad_one
    for k in range(3):
        copies[3 + k].wait()
        cols = pl.ds(D * k, D)
        input_grad = input_grad + matmul(qkv_grad[:, cols], w_qkv[:, cols], NT)
    result[...] = input_grad.astype(BF)
    flush(result, hop_out)
    grad[...] = input_grad
    flush(grad, grad_out)
    return flushed


def backward_window(
    ids, given, wide, down, qkv_in, probs_in, n1_in, h1_in, n2_in, inv_in,
    hidden_out, gate_out, up_out, qk_out, vc_out, grad_out, hop_out,
    w_gu, w_down, upstream, n1, h1, n2, inv, norm, gated, down_grad, gu_grad, norm_grad, low_norm,
    w_qkv, w_out, qkv, probs, attn_grad, context_grad, qkv_grad, grad, result,
    w_sem, o_sem, i_sem, *, micro, direct,
):
    copies = []

    def ahead():
        copies.extend(
            fetch_attention(
                wide, qkv_in, probs_in, w_qkv, w_out, qkv, probs,
                w_sem.at[pl.ds(6 * CHUNKS, 4)], i_sem.at[pl.ds(6, 2)], micro,
            )
        )

    grad_one, flushed = backward_hidden(
        ids, given, wide, down, n1_in, h1_in, n2_in, inv_in, hidden_out, gate_out, up_out,
        w_gu, w_down, upstream, n1, h1, n2, inv, norm, gated, down_grad, gu_grad, norm_grad,
        low_norm, w_sem, o_sem, i_sem, micro=micro, direct=direct, ahead=ahead,
    )
    flushed += backward_attention(
        grad_one, copies, qk_out, vc_out, grad_out, hop_out,
        w_qkv, w_out, qkv, probs, attn_grad, context_grad, qkv_grad, grad, result,
        o_sem.at[pl.ds(HIDDEN_STORES, 5)], micro=micro,
    )
    for copy in flushed:
        copy.wait()


def both_ways(
    ids, lengths, given, cotangent, wide, down,
    left_out, layer_out, hidden_out, gate_out, up_out, qk_out, vc_out, grad_out, hop_out,
    w_gu, w_down, upstream, n1, h1, n2, inv, norm, gated, down_grad, gu_grad, norm_grad, low_norm,
    w_qkv, w_out, qkv, probs, attn_grad, context_grad, qkv_grad, grad, result,
    x, context, final, left, w_sem, o_sem, i_sem, f_sem, *, micro, direct,
):
    arriving = begin(own_window(cotangent, micro), upstream, i_sem.at[2])
    flushed = forward_window(
        ids, lengths, given, wide, down,
        left_out, None, None, None, None, None, None, layer_out, None,
        w_qkv, w_out, w_gu, w_down, x, qkv, probs, context, n1, h1, n2, inv, final, norm, left,
        w_sem, f_sem, i_sem, micro=micro, direct=direct, fused=True,
    )
    grad_one, stores = backward_hidden(
        ids, None, wide, down, None, None, None, None, hidden_out, gate_out, up_out,
        w_gu, w_down, upstream, n1, h1, n2, inv, norm, gated, down_grad, gu_grad, norm_grad,
        low_norm, w_sem, o_sem, i_sem, micro=micro, direct=direct, ahead=lambda: None,
        arriving=arriving,
    )
    flushed += stores
    flushed += backward_attention(
        grad_one, [InPlace()] * 6, qk_out, vc_out, grad_out, hop_out,
        w_qkv, w_out, qkv, probs, attn_grad, context_grad, qkv_grad, grad, result,
        o_sem.at[pl.ds(HIDDEN_STORES, 5)], micro=micro,
    )
    for copy in flushed:
        copy.wait()


def backward_first_half(
    ids, given, wide, down, n1_in, n2_in, inv_in, slope_in, bent_in,
    hidden_out, gate_out, up_out, half_out,
    w_gu, w_down, upstream, n1, n2, inv, norm, slopes, bents, down_grad, gu_grad, norm_grad,
    low_norm, half, w_sem, o_sem, i_sem, *, micro, direct,
):
    arriving = begin(own_window(given, micro), upstream, i_sem.at[0])
    small = [
        begin(n2_in.at[micro], n2, i_sem.at[1]),
        begin(inv_in.at[micro], inv, i_sem.at[2]),
        begin(wide.at[:, pl.ds(COL_NORM, 128)], norm, i_sem.at[3]),
    ]
    copies = {}

    def fetch_chunk(j):
        owners = down.at[pl.ds(4 * j, 4)]
        parts = []
        for q in range(4):
            source = owners.at[:, :, pl.ds(COL_DOWN + D * q, D)] if direct else owners.at[:, q]
            parts.append(begin(source, w_down.at[j, :, q], w_sem.at[2 * CHUNKS + 4 * j + q]))
        cols = pl.ds(j * CHUNK, CHUNK)
        parts.append(begin(slope_in.at[:, cols], slopes.at[:, cols], i_sem.at[5 + j]))
        parts.append(begin(bent_in.at[:, cols], bents.at[:, cols], i_sem.at[5 + CHUNKS + j]))
        copies["first", j] = parts
        gate = wide.at[:, pl.ds(COL_GU + j * CHUNK, CHUNK)]
        rise = wide.at[:, pl.ds(COL_GU + FF + j * CHUNK, CHUNK)]
        copies["second", j] = [
            begin(gate, w_gu.at[j], w_sem.at[j]),
            begin(rise, w_gu.at[CHUNKS + j], w_sem.at[CHUNKS + j]),
        ]

    fetch_chunk(0)
    fetch_chunk(1)
    flushed = []

    def flush(source, target):
        flushed.append(begin(source, target, o_sem.at[len(flushed)]))

    arriving.wait()
    for copy in small:
        copy.wait()
    params = norm[...].astype(F32).T
    up = upstream[...].astype(F32)
    normed = n2[...]
    grad_two = norm_backward(up, normed, inv[:, HEAD : HEAD + 1], params[1:2])
    norm_grad[...] = jnp.zeros_like(norm_grad)
    norm_grad[1:2, :] = jnp.sum(up * normed, axis=0, keepdims=True)
    norm_grad[3:4, :] = jnp.sum(up, axis=0, keepdims=True)
    low_grad = grad_two.astype(BF)
    down_grad[...] = low_grad.T
    flush(down_grad, hidden_out.at[pl.ds(FF, D)])
    total = grad_two
    for j in range(CHUNKS):
        for copy in copies["first", j]:
            copy.wait()
        if j + 2 < CHUNKS:
            fetch_chunk(j + 2)
        if j + 1 == CHUNKS:
            first_norm = begin(n1_in.at[micro], n1, i_sem.at[4])
        gated_grad = matmul(low_grad, w_down[j].reshape(CHUNK, D), NT)
        cols = pl.ds(j * CHUNK, CHUNK)
        late_cols = pl.ds(FF + j * CHUNK, CHUNK)
        gate_grad = (gated_grad * slopes[:, cols]).astype(BF)
        rise_grad = (gated_grad * bents[:, cols]).astype(BF)
        gu_grad[:, cols] = gate_grad
        gu_grad[:, late_cols] = rise_grad
        flush(gu_grad.at[:, cols], gate_out.at[:, cols])
        flush(gu_grad.at[:, late_cols], up_out.at[:, cols])
        for copy in copies["second", j]:
            copy.wait()
        total = total + matmul(gate_grad, w_gu[j], NT) + matmul(rise_grad, w_gu[CHUNKS + j], NT)
    first_norm.wait()
    normed = n1[...]
    grad_one = norm_backward(total, normed, inv[:, 0:1], params[0:1])
    norm_grad[0:1, :] = jnp.sum(total * normed, axis=0, keepdims=True)
    norm_grad[2:3, :] = jnp.sum(total, axis=0, keepdims=True)
    low_norm[...] = norm_grad[...].astype(BF)
    for k in range(3):
        source = low_norm.at[:, pl.ds(SEQ * k, SEQ)]
        flush(source, hidden_out.at[pl.ds(FF + D + 16 * k, 16)])
    half[...] = grad_one
    flush(half, half_out)
    for copy in flushed:
        copy.wait()


def backward_second_half(
    ids, given, wide, qkv_in, probs_in,
    qk_out, vc_out, grad_out, hop_out,
    half, w_qkv, w_out, qkv, probs, attn_grad, context_grad, qkv_grad, grad, result,
    w_sem, o_sem, i_sem, *, micro,
):
    arriving = begin(given, half, i_sem.at[2])
    copies = fetch_attention(
        wide, qkv_in, probs_in, w_qkv, w_out, qkv, probs, w_sem, i_sem, micro
    )
    arriving.wait()
    flushed = backward_attention(
        half[...], copies, qk_out, vc_out, grad_out, hop_out,
        w_qkv, w_out, qkv, probs, attn_grad, context_grad, qkv_grad, grad, result,
        o_sem, micro=micro,
    )
    for copy in flushed:
        copy.wait()


FORWARD_KEPT = (
    (True, 3 * D, SEQ, BF),
    (True, SEQ, 3 * D, BF),
    (True, HEADS, SEQ, SEQ, BF),
    (True, SEQ, D, F32),
    (True, SEQ, D, BF),
    (True, SEQ, D, F32),
    (True, SEQ, 128, F32),
    (True, SEQ, D, BF),
)
HIDDEN_KEPT = ((False, FF + D + 48, SEQ, BF), (False, SEQ, FF, BF), (False, SEQ, FF, BF))
READY_KEPT = (HIDDEN_KEPT[0], (False, SEQ, FF, F32), (False, SEQ, FF, F32))
ATTENTION_KEPT = ((False, SEQ, 2 * D, BF), (False, SEQ, 2 * D, BF), (True, SEQ, D, F32))
HIDDEN_STORES = 3 * CHUNKS + 4
HIDDEN_WEIGHTS = (
    pltpu.VMEM((2 * CHUNKS, D, CHUNK), BF),
    pltpu.VMEM((CHUNKS, 4, 4, ROWS, D), BF),
)
ATTENTION_WEIGHTS = (pltpu.VMEM((D, 3 * D), BF), pltpu.VMEM((D, D), BF))
HIDDEN_SCRATCH = HIDDEN_WEIGHTS + (
    pltpu.VMEM((SEQ, D), BF),
    pltpu.VMEM((SEQ, D), F32),
    pltpu.VMEM((SEQ, D), BF),
    pltpu.VMEM((SEQ, D), F32),
    pltpu.VMEM((SEQ, 128), F32),
    pltpu.VMEM((D, 128), BF),
    pltpu.VMEM((FF, SEQ), BF),
    pltpu.VMEM((D, SEQ), BF),
    pltpu.VMEM((SEQ, 2 * FF), BF),
    pltpu.VMEM((16, D), F32),
    pltpu.VMEM((16, D), BF),
)
ATTENTION_SCRATCH = ATTENTION_WEIGHTS + (
    pltpu.VMEM((SEQ, 3 * D), BF),
    pltpu.VMEM((HEADS, SEQ, SEQ), BF),
    pltpu.VMEM((SEQ, D), BF),
    pltpu.VMEM((SEQ, D), BF),
    pltpu.VMEM((SEQ, 3 * D), BF),
    pltpu.VMEM((SEQ, D), F32),
    pltpu.VMEM((SEQ, D), BF),
)
DMA = pltpu.SemaphoreType.DMA


def call_window(
    body, name, owner, micro, inputs, kept_shapes, sent, before, scratch, flops, small, gates=()
):
    count = len(kept_shapes)
    operands = tuple(inputs)
    aliases = {}
    for position, array in enumerate(before):
        if array is not None:
            aliases[len(operands)] = position
            operands += (array,)
    operands += tuple(gates)
    shapes = [
        jax.ShapeDtypeStruct((MICRO,) * shared + tuple(shape), dtype)
        for shared, *shape, dtype in kept_shapes
    ]
    shapes.append(jax.ShapeDtypeStruct((SEQ, D), sent))

    def kernel(*refs):
        @pl.when(refs[0][0] == owner)
        def _():
            outs = refs[len(operands) : len(operands) + count]
            views = [
                ref.at[micro] if shared else ref
                for ref, (shared, *_) in zip(outs, kept_shapes)
            ]
            body(*refs[: len(inputs)], *views, *refs[len(operands) + count :])

    return pl.pallas_call(
        kernel,
        out_shape=shapes,
        in_specs=[SMEM] * small + [ANY] * (len(operands) - small),
        out_specs=[ANY] * len(shapes),
        input_output_aliases=aliases,
        scratch_shapes=list(scratch),
        compiler_params=pltpu.CompilerParams(vmem_limit_bytes=VMEM_LIMIT),
        cost_estimate=pl.CostEstimate(
            flops=flops, bytes_accessed=flops // 200, transcendentals=flops // 4000
        ),
        name=name,
    )(*operands)


def forward_call(owner, micro, direct, ids, lengths, given, wide, down, before, ready=False):
    scratch = (
        ATTENTION_WEIGHTS
        + HIDDEN_WEIGHTS
        + (
            pltpu.VMEM((SEQ, D), BF),
            pltpu.VMEM((SEQ, 3 * D), BF),
            pltpu.VMEM((HEADS, SEQ, SEQ), BF),
            pltpu.VMEM((SEQ, D), BF),
            pltpu.VMEM((SEQ, D), F32),
            pltpu.VMEM((SEQ, D), BF),
            pltpu.VMEM((SEQ, D), F32),
            pltpu.VMEM((SEQ, 128), F32),
            pltpu.VMEM((SEQ, D), BF),
            pltpu.VMEM((D, 128), BF),
            pltpu.VMEM((3 * D, SEQ), BF),
            DMA((4 + 6 * CHUNKS,)),
            DMA((12,)),
            DMA((2,)),
        )
    )
    body, kept = forward_window, FORWARD_KEPT
    if ready:
        body, kept = forward_ready, FORWARD_KEPT + READY_KEPT
        scratch += (
            pltpu.VMEM((FF, SEQ), BF),
            pltpu.VMEM((SEQ, FF), F32),
            pltpu.VMEM((SEQ, FF), F32),
            DMA((3 * CHUNKS,)),
        )
    return call_window(
        functools.partial(body, micro=micro, direct=direct),
        "layer_forward",
        owner,
        micro,
        (ids, lengths, given, wide, down),
        kept,
        BF,
        before,
        scratch,
        5_000_000_000,
        2,
    )


def both_ways_call(owner, micro, direct, ids, lengths, given, cotangent, wide, down, before):
    return call_window(
        functools.partial(both_ways, micro=micro, direct=direct),
        "layer_both_ways",
        owner,
        micro,
        (ids, lengths, given, cotangent, wide, down),
        (FORWARD_KEPT[0], FORWARD_KEPT[-1]) + HIDDEN_KEPT + ATTENTION_KEPT,
        BF,
        before,
        HIDDEN_SCRATCH
        + ATTENTION_SCRATCH
        + (
            pltpu.VMEM((SEQ, D), BF),
            pltpu.VMEM((SEQ, D), BF),
            pltpu.VMEM((SEQ, D), BF),
            pltpu.VMEM((3 * D, SEQ), BF),
            DMA((4 + 6 * CHUNKS,)),
            DMA((HIDDEN_STORES + 5,)),
            DMA((3,)),
            DMA((12,)),
        ),
        130_000_000_000,
        2,
    )


def backward_call(owner, micro, direct, ids, given, wide, down, stash, before, gates):
    return call_window(
        functools.partial(backward_window, micro=micro, direct=direct),
        "layer_backward",
        owner,
        micro,
        (ids, given, wide, down) + tuple(stash),
        HIDDEN_KEPT + ATTENTION_KEPT,
        BF,
        before,
        HIDDEN_SCRATCH
        + ATTENTION_SCRATCH
        + (DMA((4 + 6 * CHUNKS,)), DMA((HIDDEN_STORES + 5,)), DMA((8,))),
        80_000_000_000,
        1,
        gates,
    )


def first_half_call(
    owner, micro, direct, ids, given, wide, down, stash, before, gates
):
    return call_window(
        functools.partial(backward_first_half, micro=micro, direct=direct),
        "backward_hidden",
        owner,
        micro,
        (ids, given, wide, down) + tuple(stash),
        HIDDEN_KEPT,
        F32,
        before,
        HIDDEN_WEIGHTS
        + (
            pltpu.VMEM((SEQ, D), BF),
            pltpu.VMEM((SEQ, D), F32),
            pltpu.VMEM((SEQ, D), F32),
            pltpu.VMEM((SEQ, 128), F32),
            pltpu.VMEM((D, 128), BF),
            pltpu.VMEM((SEQ, FF), F32),
            pltpu.VMEM((SEQ, FF), F32),
            pltpu.VMEM((D, SEQ), BF),
            pltpu.VMEM((SEQ, 2 * FF), BF),
            pltpu.VMEM((16, D), F32),
            pltpu.VMEM((16, D), BF),
            pltpu.VMEM((SEQ, D), F32),
            DMA((6 * CHUNKS,)),
            DMA((2 * CHUNKS + 5,)),
            DMA((5 + 2 * CHUNKS,)),
        ),
        60_000_000_000,
        1,
        gates,
    )


def second_half_call(owner, micro, ids, given, wide, stash, before, gates):
    return call_window(
        functools.partial(backward_second_half, micro=micro),
        "backward_attention",
        owner,
        micro,
        (ids, given, wide) + tuple(stash),
        ATTENTION_KEPT,
        BF,
        before,
        (pltpu.VMEM((SEQ, D), F32),) + ATTENTION_SCRATCH + (DMA((4,)), DMA((5,)), DMA((3,))),
        10 * PACE,
        1,
        gates,
    )


def pack_direct(w_qkv, w_out, w_gate_up, w_down, norm_gain, norm_bias):
    columns = [(0, 3 * D), (COL_OUT, D), (COL_GU, FF), (COL_GU + FF, FF)]
    columns += [(COL_DOWN + D * q, D) for q in range(4)]

    def body(qkv, out, gate_up, down, gain, bias, packed, held, low, square, i_sem, o_sem):
        sources = [qkv, out, gate_up.at[:, pl.ds(0, FF)], gate_up.at[:, pl.ds(FF, FF)]]
        sources += [down.at[pl.ds(ROWS * q, ROWS)] for q in range(4)]
        loads = [
            begin(source, held.at[:, pl.ds(start, size)], i_sem.at[k])
            for k, (source, (start, size)) in enumerate(zip(sources, columns))
        ]
        square[...] = jnp.zeros_like(square)
        square[pl.ds(0, 2), pl.ds(0, ROWS)] = gain[...]
        square[pl.ds(2, 2), pl.ds(0, ROWS)] = bias[...]
        low[:, pl.ds(COL_NORM, 128)] = square[...].T[:ROWS].astype(BF)
        stores = []
        for k, (load, (start, size)) in enumerate(zip(loads, columns)):
            cols = pl.ds(start, size)
            load.wait()
            low[:, cols] = held[:, cols].astype(BF)
            if k + 1 < len(loads):
                stores.append(begin(low.at[:, cols], packed.at[:, cols], o_sem.at[k]))
        cols = pl.ds(columns[-1][0], D + 128)
        stores.append(begin(low.at[:, cols], packed.at[:, cols], o_sem.at[len(loads) - 1]))
        for store in stores:
            store.wait()

    small = pl.BlockSpec(memory_space=pltpu.VMEM)
    return pl.pallas_call(
        body,
        out_shape=jax.ShapeDtypeStruct((ROWS, WIDE), BF),
        in_specs=[ANY] * 4 + [small] * 2,
        out_specs=ANY,
        scratch_shapes=[
            pltpu.VMEM((ROWS, COL_NORM), F32),
            pltpu.VMEM((ROWS, WIDE), BF),
            pltpu.VMEM((128, 128), F32),
            DMA((8,)),
            DMA((8,)),
        ],
        compiler_params=pltpu.CompilerParams(vmem_limit_bytes=VMEM_LIMIT),
        cost_estimate=cost_of(2),
        name="pack",
    )(w_qkv, w_out, w_gate_up, w_down, norm_gain, norm_bias)


def pack(w_qkv, w_out, w_gate_up, w_down, norm_gain, norm_bias):
    rows = w_qkv.shape[0]
    split_down = w_down.reshape(4, rows, D).transpose(1, 0, 2).reshape(rows, FF)
    norms = jnp.concatenate([norm_gain, norm_bias], axis=0).T
    norms = jnp.pad(norms, ((0, 0), (0, 128 - 4)))
    return jnp.concatenate([w_qkv, w_out, w_gate_up, split_down, norms], axis=1)


BIT_CORE, BIT_X, BIT_NEAR, BIT_FAR = 1, 2, 4, 8


def weight_grad_kernel(ids, terms, norm_ins, sent, kept, scratch, *, rows, order, turned):
    buffers, result, i_sem, o_sem = scratch[:4]
    columns, pieces, count = 0, [], 0

    def fetch(source, target):
        nonlocal count
        count += 1
        return begin(source, target, i_sem.at[count - 1])

    owned = []
    for place in range(8):
        relative = sum(bit for k, bit in enumerate(order) if not (place >> (2 - k)) & 1)
        owned.append(ids[1] ^ relative)
    for term, (lefts, rights) in enumerate(terms):
        left_buffer, right_buffer = buffers[term]
        whole = []
        for k, left in enumerate(lefts):
            for place in range(8):
                source = left.at[pl.ds(pl.multiple_of(owned[place] * rows, 16), rows)]
                target = left_buffer.at[place, :, pl.ds(SEQ * k, SEQ)]
                whole.append(fetch(source, target))
        for start in range(0, D if turned else right_buffer.shape[1], D):
            cols = pl.ds(start, D)
            parts = []
            for k, right in enumerate(rights):
                tokens = pl.ds(SEQ * k, SEQ)
                if turned:
                    parts.append(fetch(right, right_buffer.at[:, tokens]))
                else:
                    parts.append(fetch(right.at[:, cols], right_buffer.at[tokens, cols]))
            pieces.append((term, start, whole, parts, columns))
            columns += D
            whole = []
    if norm_ins:
        norm_buffer, norm_turned, norm_sem = scratch[4:]
        norm_loads = [
            begin(source.at[pl.ds(16 * k, 16)], norm_buffer.at[n, :, pl.ds(SEQ * k, SEQ)], norm_sem.at[n, k])
            for n, source in enumerate(norm_ins)
            for k in range(3)
        ]
    stores = []

    def store(first, count, cols):
        target = sent if first < 4 else kept
        source = result.at[pl.ds(first, count), :, cols]
        place = target.at[pl.ds(first % 4, count), :, cols]
        stores.append(begin(source, place, o_sem.at[len(stores)]))

    group = 192 // rows
    for term, start, whole, parts, column in pieces:
        left_buffer, right_buffer = buffers[term]
        for load in whole + parts:
            load.wait()
        values = right_buffer[...] if turned else right_buffer[:, pl.ds(start, D)]
        cols = pl.ds(column, D)
        for first in range(0, 8, 2 * group):
            taken = left_buffer[pl.ds(first, 2 * group)].reshape(2 * group * rows, TOKENS)
            value = matmul(taken, values, NT if turned else NN).astype(BF)
            result[pl.ds(first, 2 * group), :, cols] = value.reshape(2 * group, rows, D)
            for half in range(2):
                store(first + group * half, group, cols)
    if norm_ins:
        for load in norm_loads:
            load.wait()
        total = sum(norm_buffer[n].astype(F32) for n in range(4))
        total = jnp.concatenate([total, jnp.zeros((112, D), F32)], axis=0).T.astype(BF)
        norm_turned[...] = total.reshape(16, rows, 128)
        cols = pl.ds(columns, 128)
        for place in range(8):
            result[place, :, cols] = norm_turned[owned[place]]
        store(0, 4, cols)
        store(4, 4, cols)
    for copy in stores:
        copy.wait()


def weight_grad(ids, pairs, rows, order, gates, norms=None, turned=False):
    width = 0
    arrays, scratch = [], []

    def position(array):
        for k, known in enumerate(arrays):
            if known is array:
                return k
        arrays.append(array)
        return len(arrays) - 1

    def placed(side):
        return [(position(array), micro) for array, micro in side[0]], side[1]

    terms = [(placed(left), placed(right)) for left, right in pairs]
    norm_places = placed(norms) if norms else None
    loads, stores = 0, 0
    for _, (_, taken) in terms:
        size = taken.stop - taken.start
        shape = (size, TOKENS) if turned else (TOKENS, size)
        scratch += [pltpu.VMEM((8, rows, TOKENS), BF), pltpu.VMEM(shape, BF)]
        loads += 32 + 4 * (size // D)
        stores += 8 * (size // D)
        width += size
    total = width + 128 * bool(norms)
    shape = jax.ShapeDtypeStruct((4, rows, total), BF)
    count = 1 + len(arrays) + len(gates)

    def view(refs, place, taken, along_rows):
        index, micro = place
        ref = refs[1 + index] if micro is None else refs[1 + index].at[micro]
        span = pl.ds(taken.start, taken.stop - taken.start)
        return ref.at[span] if along_rows else ref.at[:, span]

    def body(*refs):
        sources = [
            (
                [view(refs, place, left[1], True) for place in left[0]],
                [view(refs, place, right[1], turned) for place in right[0]],
            )
            for left, right in terms
        ]
        norm_views = []
        if norms:
            norm_views = [view(refs, place, norm_places[1], True) for place in norm_places[0]]
        rest = refs[count + 2 :]
        buffers = [(rest[2 * k], rest[2 * k + 1]) for k in range(len(terms))]
        weight_grad_kernel(
            refs[0],
            sources,
            norm_views,
            refs[count],
            refs[count + 1],
            (buffers,) + tuple(rest[2 * len(terms) :]),
            rows=rows,
            order=order,
            turned=turned,
        )

    scratch += [pltpu.VMEM((8, rows, total), BF), DMA((loads,)), DMA((stores + 2,))]
    if norms:
        scratch += [pltpu.VMEM((4, 16, D), BF), pltpu.VMEM((16, rows, 128), BF), DMA((4, 3))]
    return pl.pallas_call(
        body,
        out_shape=[shape, shape],
        in_specs=[SMEM] + [ANY] * (count - 1),
        out_specs=[ANY] * 2,
        scratch_shapes=scratch,
        compiler_params=pltpu.CompilerParams(vmem_limit_bytes=VMEM_LIMIT),
        cost_estimate=cost_of(8),
        name="weight_grad",
    )(ids, *arrays, *gates)


def exchange(values, bit):
    count = lax.axis_size("dp")
    return lax.ppermute(values, "dp", [(i, i ^ bit) for i in range(count)])


def halve(parts, gates):
    half = len(parts[0]) // 2
    arrays = []
    for part in parts:
        for array, _ in part[:half]:
            if not any(array is known for known in arrays):
                arrays.append(array)
    where = [
        [next((k, at) for k, known in enumerate(arrays) if known is array) for array, at in part[:half]]
        for part in parts
    ]
    block = arrays[0].shape[1:]
    count = len(parts)

    def body(*refs):
        outgoing, held, result, i_sem, o_sem = refs[len(arrays) + len(gates) :]
        loads = [
            [
                begin(refs[where[p][i][0]].at[where[p][i][1]], held.at[p, i], i_sem.at[p, i])
                for p in range(count)
            ]
            for i in range(half)
        ]
        stores = []
        for i in range(half):
            total = None
            for p in range(count):
                loads[i][p].wait()
                value = held[p, i].astype(F32)
                total = value if total is None else total + value
            result[i] = total.astype(BF)
            stores.append(begin(result.at[i], outgoing.at[i], o_sem.at[i]))
        for copy in stores:
            copy.wait()

    return pl.pallas_call(
        body,
        out_shape=jax.ShapeDtypeStruct((half,) + block, BF),
        in_specs=[ANY] * (len(arrays) + len(gates)),
        out_specs=ANY,
        scratch_shapes=[
            pltpu.VMEM((count, half) + block, BF),
            pltpu.VMEM((half,) + block, BF),
            DMA((count, half)),
            DMA((half,)),
        ],
        compiler_params=pltpu.CompilerParams(vmem_limit_bytes=VMEM_LIMIT),
        cost_estimate=cost_of(2),
        name="halve",
    )(*arrays, *gates)


def blocks_of(array):
    return [(array, at) for at in range(array.shape[0])]


def finish(parts, gates, pieces, carried=None):
    arrays, places = [], []
    for ((array, at),) in parts:
        if not any(array is known for known in arrays):
            arrays.append(array)
        places.append((next(k for k, known in enumerate(arrays) if known is array), at))
    rows, width = arrays[0].shape[1:]
    operands = tuple(arrays) + tuple(gates) + (() if carried is None else (carried,))

    def body(*refs):
        outs = refs[len(operands) :][: len(pieces)]
        held, made, i_sem, o_sem = refs[len(operands) + len(pieces) :]
        loads = [
            begin(refs[index].at[at], held.at[k], i_sem.at[k])
            for k, (index, at) in enumerate(places)
        ]
        total = None
        for k, load in enumerate(loads):
            load.wait()
            value = held[k].astype(F32)
            total = value if total is None else total + value
        if width > 4 * D:
            norms = jnp.concatenate(
                [total[:, 4 * D :], jnp.zeros((128 - rows, 128), F32)], axis=0
            ).T
            made[:, pl.ds(0, 4 * D)] = total[:, : 4 * D]
            outs[2][...] = norms[0:2, :rows]
            outs[3][...] = norms[2:4, :rows]
        else:
            made[...] = total
        stores = []
        for k, (out, (shape, start, column)) in enumerate(zip(outs, pieces[:2])):
            count, size = min(shape[0], rows), min(shape[1], width)
            source = made.at[pl.ds(0, count), pl.ds(start, size)]
            stores.append(begin(source, out.at[:, pl.ds(column, size)], o_sem.at[k]))
        for store in stores:
            store.wait()

    return pl.pallas_call(
        body,
        out_shape=[jax.ShapeDtypeStruct(shape, F32) for shape, _, _ in pieces],
        in_specs=[ANY] * len(operands),
        out_specs=([ANY] * 2 + [pl.BlockSpec(memory_space=pltpu.VMEM)] * 2)[: len(pieces)]
        if len(pieces) > 1
        else [ANY],
        input_output_aliases={} if carried is None else {len(operands) - 1: 0},
        scratch_shapes=[
            pltpu.VMEM((len(parts), rows, width), BF),
            pltpu.VMEM((rows, width), F32),
            DMA((len(parts),)),
            DMA((len(pieces),)),
        ],
        compiler_params=pltpu.CompilerParams(vmem_limit_bytes=VMEM_LIMIT),
        cost_estimate=cost_of(2),
        name="finish",
    )(*operands)


LINKS = {
    "down": (BIT_X, BIT_NEAR, BIT_FAR),
    "gate": (BIT_NEAR, BIT_X, BIT_FAR),
    "rise": (BIT_X, BIT_NEAR, BIT_FAR),
    "attn": (BIT_X, BIT_NEAR, BIT_FAR),
}
PLAN = (
    ("local", "down"),
    ("local", "gate"),
    ("local", "rise"),
    ("attention", "attn"),
    ("step", "down"),
    ("local", "attn"),
    ("step", "gate"),
    ("step", "rise"),
    ("step", "down"),
    ("step", "rise"),
    ("step", "attn"),
    ("finish", "down"),
    ("step", "gate"),
    ("finish", "rise"),
    ("step", "attn"),
    ("finish", "gate"),
    ("finish", "attn"),
)


def reduce_shares(ids, lefts, hidden, gates_ups, attention_first, second_half):
    parts, last, done = {}, [], {}
    order = {}

    def local(name, pairs, rows, bits, norms=None, turned=False):
        order[name] = list(bits)
        sent, kept = weight_grad(ids, pairs, rows, bits, last, norms, turned)
        parts[name] = [blocks_of(kept), blocks_of(exchange(sent, order[name].pop(0)))]
        last[:] = [sent]

    def step(name):
        sent = halve(parts[name], last)
        parts[name] = [part[sent.shape[0] :] for part in parts[name]]
        parts[name].append(blocks_of(exchange(sent, order[name].pop(0))))
        last[:] = [sent]

    inputs, context, h1 = ((lefts, slice(D * k, D * (k + 1))) for k in range(3))
    hidden_pairs = {
        "down": [((hidden, slice(0, FF)), (hidden, slice(FF, FF + D)))],
        "gate": [(h1, (gates_ups[0], slice(0, FF)))],
        "rise": [(h1, (gates_ups[1], slice(0, FF)))],
    }
    for action, name in PLAN:
        if action == "step":
            step(name)
        elif action == "finish":
            wide = (ROWS, 2 * FF)
            pieces = {
                "down": [((4 * ROWS, D), 0, 0)],
                "gate": [(wide, 0, 0)],
                "rise": [(wide, 0, FF)],
                "attn": [((ROWS, 3 * D), 0, 0), ((ROWS, D), 3 * D, 0)] + [((2, ROWS), 0, 0)] * 2,
            }
            carried = done["gate"][0] if "gate" in done and name in ("gate", "rise") else None
            made = finish(parts[name], last, pieces[name], carried)
            done["gate" if name == "rise" else name] = made
            last[:] = [made[0]] if name not in ("gate", "rise") else []
        elif action == "attention":
            attention_second, input_grads, _ = second_half(
                last + [other[0] for _, other in attention_first]
            )
            last[:] = [attention_second[0]]
            q_grads, v_grads = (
                [own, (array, None), other, (exchange(array, BIT_CORE), None)]
                for (own, other), array in zip(attention_first, attention_second)
            )
        elif name == "attn":
            pairs = [
                (inputs, (q_grads, slice(0, 2 * D))),
                (inputs, (v_grads, slice(0, D))),
                (context, (v_grads, slice(D, 2 * D))),
            ]
            local(name, pairs, ROWS, LINKS[name], (hidden, slice(FF + D, FF + D + 48)))
        else:
            rows = 4 * ROWS if name == "down" else ROWS
            local(name, hidden_pairs[name], rows, LINKS[name], turned=name == "down")
    shares = (
        done["attn"][0],
        done["attn"][1],
        done["gate"][0],
        done["down"][0],
        done["attn"][2],
        done["attn"][3],
    )
    return shares, input_grads


def packed_shares(rows, left, hidden, gates, ups, attention):
    def product(lefts, rights, dims=NN):
        lefts = jnp.concatenate(lefts, axis=1)
        rights = jnp.concatenate(rights, axis=1 if dims == NT else 0)
        return matmul(lefts, rights, dims).astype(BF)

    def cut(arrays, start, stop):
        return [array[start:stop] for array in arrays]

    left = list(left)
    down = product(cut(hidden, 0, FF), cut(hidden, FF, FF + D), NT).reshape(D // rows, 4, rows, D)
    norm_sum = sum(array[FF + D :].astype(F32) for array in hidden)
    norm_sum = norm_sum.reshape(3, 16, SEQ)[:, :4].transpose(1, 0, 2).reshape(4, D).T.astype(BF)
    attention = [jnp.concatenate(pair, axis=1) for pair in attention]
    summed = [
        product(cut(left, 0, D), [array[:, : 3 * D] for array in attention]),
        product(cut(left, D, 2 * D), [array[:, 3 * D :] for array in attention]),
        product(cut(left, 2 * D, 3 * D), gates),
        product(cut(left, 2 * D, 3 * D), ups),
        down.transpose(0, 2, 1, 3).reshape(D, FF),
        jnp.pad(norm_sum, ((0, 0), (0, 128 - 4))),
    ]
    summed = jnp.concatenate(summed, axis=1)
    share = lax.psum_scatter(summed, "dp", scatter_dimension=0, tiled=True).astype(F32)
    down = share[:, COL_DOWN:COL_NORM].reshape(rows, 4, D).transpose(1, 0, 2)
    norm = share[:, COL_NORM : COL_NORM + 4].T
    return (
        share[:, :COL_OUT],
        share[:, COL_OUT:COL_GU],
        share[:, COL_GU:COL_DOWN],
        down.reshape(4 * rows, D),
        norm[:2],
        norm[2:],
    )


def shards(tokens, lengths, w_qkv, w_out, w_gate_up, w_down, norm_gain, norm_bias, cotangent):
    rows = w_qkv.shape[1]
    direct = rows == ROWS
    section = lax.axis_index("section")
    ids = jnp.stack([section, lax.axis_index("dp")]).astype(jnp.int32)
    sharded = [w[0] for w in (w_qkv, w_out, w_gate_up, w_down, norm_gain, norm_bias)]
    packed = pack_direct(*sharded) if direct else pack(*(w.astype(BF) for w in sharded))
    wide = lax.all_gather(packed, "dp", axis=0, tiled=True)
    if direct:
        down = wide.reshape(D // rows, rows, WIDE)
    else:
        down = wide[:, COL_DOWN:COL_NORM].reshape(D // rows, rows, 4, D)
        down = down.transpose(0, 2, 1, 3).reshape(FF // (4 * ROWS), 4, ROWS, D)

    def hop(rows_sent, pair):
        return lax.ppermute(rows_sent, "section", [pair])

    def forward(owner, micro, given, before, ready=False):
        return forward_call(
            owner, micro, direct, ids, lengths, given, wide, down, before, ready
        )

    *kept, sent = forward(0, 0, tokens, [None] * len(FORWARD_KEPT))
    arrived_first = hop(sent, (0, 1))
    *kept, hidden_second, slopes, bents, sent = forward(0, 1, tokens, kept + [None] * 3, True)
    arrived_second = hop(sent, (0, 1))
    left, qkv, probs, n1, h1, n2, inv, layer_out = kept
    stash = (qkv, probs, n1, h1, n2, inv)

    def both_passes(micro, given, before):
        return both_ways_call(
            1, micro, direct, ids, lengths, given, cotangent, wide, down, before
        )

    def both(array):
        return [(array, None), (exchange(array, BIT_CORE), None)]

    left, layer_out, *first, input_grads, sent = both_passes(
        0, arrived_first, [left, layer_out] + [None] * 6
    )
    arrived_first = hop(sent, (1, 0))
    left, layer_out, *second, input_grads, sent = both_passes(
        1, arrived_second, [left, layer_out, hidden_second] + [None] * 4 + [input_grads]
    )
    arrived_second = hop(sent, (1, 0))
    left_other = exchange(left, BIT_CORE) if direct else left
    *first, input_grads, sent = backward_call(
        0, 0, direct, ids, arrived_first, wide, down, stash, first + [input_grads], ()
    )
    if direct:
        first = [both(array) for array in first]
    gates = (left_other,) if direct else ()
    *hidden, half = first_half_call(
        0, 1, direct, ids, arrived_second, wide, down, (n1, n2, inv, slopes, bents), second[:3], gates
    )

    def second_half(gates):
        before = second[3:] + [input_grads]
        *made, input_sum, _ = second_half_call(
            0, 1, ids, half, wide, (qkv, probs), before, gates
        )
        return made, input_sum, None

    if direct:
        lefts = [(left, 0), (left, 1), (left_other, 0), (left_other, 1)]

        def paired(k):
            own, other = zip(first[k], both(hidden[k]))
            return list(own) + list(other)

        shares, input_grads = reduce_shares(
            ids,
            lefts,
            paired(0),
            [paired(1), paired(2)],
            [[first[3][0], first[3][1]], [first[4][0], first[4][1]]],
            second_half,
        )
    else:
        attention, input_grads, _ = second_half(())
        pairs = [first[3:5], attention]
        shares = packed_shares(
            rows, left, [first[0], hidden[0]], [first[1], hidden[1]], [first[2], hidden[2]], pairs
        )
    return (layer_out[None], input_grads[None]) + tuple(share[None] for share in shares)


def solution(mesh):
    return jax.shard_map(
        shards,
        mesh=mesh,
        in_specs=(
            P(None, "dp", None),
            P(),
            P("section", "dp", None),
            P("section", "dp", None),
            P("section", "dp", None),
            P("section", "dp", None),
            P("section", None, "dp"),
            P("section", None, "dp"),
            P(None, "dp", None),
        ),
        out_specs=(
            P("section", None, "dp", None),
            P("section", None, "dp", None),
            P("section", "dp", None),
            P("section", "dp", None),
            P("section", "dp", None),
            P("section", "dp", None),
            P("section", None, "dp"),
            P("section", None, "dp"),
        ),
        check_vma=False,
    )
```
